512 devices in a mesh: tm: 4 (over y_hi, core), space: 128 (over x, z, y_lo).
Axes of the slice: x: 4, y: 4 (y_hi: 2, y_lo: 2; y = y_hi * 2 + y_lo), z: 16, core: 2. Of those that a mesh axis runs over, the one named last changes fastest.
Arguments:
- sources: bfloat16 [4, 2, 4, 3, 12, 128, 128], P('tm', None, None, None, None, 'space'), may hold values from -6 to 6
- gauge_links: bfloat16 [4, 4, 2, 3, 3, 128, 128], P(None, 'tm', None, None, None, 'space'), may hold values from -2.5 to 2.5
- eigenvectors: bfloat16 [4, 128, 2, 3, 128, 128], P('tm', None, None, None, 'space'), may hold values from -0.078125 to 0.078125
- elementals: float32 [4, 2, 128, 128], P('tm', None, 'space'), may hold values from -0.375 to 0.375
Outputs:
- projected: float32 [4, 2, 4, 12, 128], P('tm', None, None, None, 'space')
- contracted: float32 [4, 2, 4, 12, 128], P('tm', None, None, None, 'space')
The draws below stay inside these ranges and needn't reach their ends.
All inputs are finite; a program needn't handle non-finite values.
Results may differ from the reference program's by a relative error of at most 0.0075.
Values may be sent and summed in bfloat16 or wider, within the bound.
No kernel may reach another device: no remote copies, remote signals or barrier semaphores. Data moves between devices by JAX's collectives and lax.ppermute only.
A program may use at most 64 MiB of HBM per device.

```python
import jax
import jax.numpy as jnp
from jax import lax

NSRC = 12
NMODE = 128
LX = 8
LY = 16
NT = 4
NZ = 128


def raised(values, stream_key, source, target, shards_of, factor):
    def block_of(axis_at):
        return (jnp.arange(values.shape[axis_at]) // (values.shape[axis_at] // shards_of)).reshape((-1,) + (1,) * (values.ndim - 1 - axis_at))

    one_side = jax.random.permutation(stream_key, shards_of)[block_of(target)]
    other_side = (block_of(target) + shards_of // 2) % shards_of
    return jnp.where((block_of(source) == one_side) | (block_of(source) == other_side), factor * values, values)


def levels(rng, extent, shards, low, largest):
    def one(dim, parts):
        draws = jax.random.uniform(jax.random.fold_in(jax.random.fold_in(rng, 6), dim), (parts,), jnp.float32, low / len(shards), largest / len(shards))
        return jnp.repeat(jnp.exp(draws), extent[dim] // parts).reshape((-1,) + (1,) * (len(extent) - dim - 1))

    factor_of = one(*shards[0])
    for cut in shards[1:]:
        factor_of = factor_of * one(*cut)
    return factor_of


def centred(stream_key, extent, width, bound, split=(), kind=jnp.bfloat16):
    result = width * jax.random.normal(stream_key, extent, jnp.float32)
    if split:
        result = result * levels(stream_key, extent, split, -0.22, 0.18)
    return jnp.clip(result, -bound, bound).astype(kind)


def bell_draw_with(stream_key, shape, spread, bound, pieces, heavy, kind=jnp.bfloat16):
    entries = spread * jax.random.normal(stream_key, shape, jnp.float32)
    if pieces:
        entries = entries * levels(stream_key, shape, pieces, -0.22, 0.18)
    return jnp.clip(raised(entries, jax.random.fold_in(stream_key, 3), *heavy), -bound, bound).astype(kind)


def setup_inputs(seed: int = 0) -> dict:
    streams_of = jax.random.split(jax.random.key(seed), 5)
    return {
        "sources": centred(streams_of[0], (NT, 2, 4, 3, NSRC, NZ, LX * LY), 1.0, 6.0, ((0, 4), (5, 128))),
        "gauge_links": centred(streams_of[1], (4, NT, 2, 3, 3, NZ, LX * LY), 0.41, 2.5, ((1, 4), (5, 128))),
        "eigenvectors": bell_draw_with(streams_of[2], (NT, NMODE, 2, 3, NZ, LX * LY), (6 * LX * LY * NZ) ** -0.5, 0.078125, ((0, 4), (4, 128)), (4, 1, 128, 5.5)),
        "elementals": centred(streams_of[3], (NT, 2, NMODE, NMODE), (2 * NMODE) ** -0.5, 0.375, ((0, 4), (2, 128)), jnp.float32),
    }


highest = lax.Precision.HIGHEST
hopping = 0.125


def times_unit(value, sign):
    return (-sign * value[1], sign * value[0])


def mult_block(direction, first, second):
    if direction == 0:
        return times_unit(second, -1.0), times_unit(first, -1.0)
    if direction == 1:
        return (-second[0], -second[1]), first
    if direction == 2:
        return times_unit(first, -1.0), times_unit(second, 1.0)
    return first, second


def half_spinor(direction, pair, sign):
    upper_a = (pair[0][:, 0], pair[1][:, 0])
    upper_b = (pair[0][:, 1], pair[1][:, 1])
    lower_a = (pair[0][:, 2], pair[1][:, 2])
    lower_b = (pair[0][:, 3], pair[1][:, 3])
    moved_a, moved_b = mult_block(direction, lower_a, lower_b)
    real_part = jnp.stack([upper_a[0] + sign * moved_a[0], upper_b[0] + sign * moved_b[0]], 1)
    imag_part = jnp.stack([upper_a[1] + sign * moved_a[1], upper_b[1] + sign * moved_b[1]], 1)
    return real_part, imag_part


def rebuild(direction, pair, sign):
    first = (pair[0][:, 0], pair[1][:, 0])
    second = (pair[0][:, 1], pair[1][:, 1])
    if direction == 3:
        lower_a = (sign * first[0], sign * first[1])
        lower_b = (sign * second[0], sign * second[1])
    else:
        moved_a, moved_b = mult_block(direction, first, second)
        lower_a = (-sign * moved_a[0], -sign * moved_a[1])
        lower_b = (-sign * moved_b[0], -sign * moved_b[1])
    real_part = jnp.stack([first[0], second[0], lower_a[0], lower_b[0]], 1)
    imag_part = jnp.stack([first[1], second[1], lower_a[1], lower_b[1]], 1)
    return real_part, imag_part


def color_apply(link_re, link_im, field_re, field_im, dagger):
    out_re = []
    out_im = []
    for row in range(3):
        acc_re = 0.0
        acc_im = 0.0
        for col in range(3):
            if dagger:
                entry_re = link_re[:, col, row][:, None, None]
                entry_im = -link_im[:, col, row][:, None, None]
            else:
                entry_re = link_re[:, row, col][:, None, None]
                entry_im = link_im[:, row, col][:, None, None]
            vec_re = field_re[:, :, col]
            vec_im = field_im[:, :, col]
            acc_re = acc_re + entry_re * vec_re - entry_im * vec_im
            acc_im = acc_im + entry_re * vec_im + entry_im * vec_re
        out_re.append(acc_re)
        out_im.append(acc_im)
    return jnp.stack(out_re, 2), jnp.stack(out_im, 2)


def plane_shift(values, direction, stride, row_len):
    if direction == 1:
        return jnp.roll(values, -stride * row_len, axis=-1)
    column = jnp.arange(values.shape[-1]) % row_len
    if stride == 1:
        return jnp.where(column == row_len - 1, jnp.roll(values, row_len - 1, -1), jnp.roll(values, -1, -1))
    return jnp.where(column == 0, jnp.roll(values, -(row_len - 1), -1), jnp.roll(values, 1, -1))


def split_parts(values):
    widened = values.astype(jnp.float32)
    return widened[:, 0], widened[:, 1]


def stored(pair):
    return jnp.stack([pair[0], pair[1]], 1).astype(jnp.bfloat16)


def minus_chi(direction, pair):
    return stored(half_spinor(direction, pair, -1.0))


def plus_chi(direction, pair, link_pair):
    half = half_spinor(direction, pair, 1.0)
    return stored(color_apply(link_pair[0], link_pair[1], half[0], half[1], True))


def direction_term(direction, ahead, behind, link_pair):
    ahead_pair = split_parts(ahead)
    behind_pair = split_parts(behind)
    moved = color_apply(link_pair[0], link_pair[1], ahead_pair[0], ahead_pair[1], False)
    forward = rebuild(direction, moved, -1.0)
    backward = rebuild(direction, behind_pair, 1.0)
    return forward[0] + backward[0], forward[1] + backward[1]


def contract(matrices, values):
    def product(left, right):
        return jnp.einsum('tkl,tasl->task', left, right, precision=highest)
    real_part = product(matrices[:, 0], values[:, 0]) - product(matrices[:, 1], values[:, 1])
    imag_part = product(matrices[:, 0], values[:, 1]) + product(matrices[:, 1], values[:, 0])
    return jnp.stack([real_part, imag_part], 1)


def reference(sources, gauge_links, eigenvectors, elementals):
    link_here = [split_parts(gauge_links[direction]) for direction in range(4)]

    def polynomial(source_one):
        current = source_one
        base = source_one.astype(jnp.float32)
        slices = source_one.shape[0]
        tpos = jnp.arange(slices).reshape(-1, 1, 1, 1, 1, 1, 1)
        ahead_sign = jnp.where(tpos == slices - 1, -1.0, 1.0)
        behind_sign = jnp.where(tpos == 0, -1.0, 1.0)
        for sweep in range(3):
            pair = split_parts(current)
            result_re = 0.0
            result_im = 0.0
            for direction in range(4):
                minus = minus_chi(direction, pair)
                plus = plus_chi(direction, pair, link_here[direction])
                if direction < 2:
                    ahead = plane_shift(minus, direction, 1, LX)
                    behind = plane_shift(plus, direction, -1, LX)
                elif direction == 2:
                    ahead = jnp.roll(minus, -1, 5)
                    behind = jnp.roll(plus, 1, 5)
                else:
                    ahead = ahead_sign * jnp.roll(minus, -1, 0).astype(jnp.float32)
                    behind = behind_sign * jnp.roll(plus, 1, 0).astype(jnp.float32)
                term_re, term_im = direction_term(direction, ahead, behind, link_here[direction])
                result_re = result_re + term_re
                result_im = result_im + term_im
            current = (base + hopping * jnp.stack([result_re, result_im], 1)).astype(jnp.bfloat16)
        return current[:, :, :, :, 0]

    per_source = jnp.moveaxis(sources, 4, 0)[:, :, :, :, :, None]
    finals = jnp.moveaxis(lax.map(polynomial, per_source), 0, 4)

    def project_slice(pair):
        vectors, values = pair
        widened = vectors.astype(jnp.float32)
        spinor = values.astype(jnp.float32)
        stacked = jnp.stack([spinor, jnp.stack([spinor[1], -spinor[0]])])
        return jnp.einsum('krczp,oracszp->oask', widened, stacked, precision=highest)

    projected = lax.map(project_slice, (eigenvectors, finals))
    contracted = contract(elementals, projected)
    return projected, contracted
```

```python
import jax
import jax.numpy as jnp
from jax import lax
from jax.sharding import Mesh
from jax.sharding import PartitionSpec as P

LX = 8
TM = ("y_hi", "core")
SPACE = ("x", "z", "y_lo")
PLANE = ("x", "y_lo")


highest = lax.Precision.HIGHEST
hopping = 0.125


def from_behind(value, axis, steps):
    count = lax.axis_size(axis)
    pairs = [(source, (source + steps) % count) for source in range(count)]
    return lax.ppermute(value, axis, pairs)


def with_halo(array, sides, width):
    for axis, dim in sides:
        peers, length = (lax.axis_size(axis), array.shape[dim])
        up = [(i, (i + 1) % peers) for i in range(peers)]
        down = [(j, i) for i, j in up]
        last = lax.slice_in_dim(array, length - width, length, axis=dim)
        leading = lax.slice_in_dim(array, 0, width, axis=dim)
        before = lax.ppermute(last, axis, up)
        after = lax.ppermute(leading, axis, down)
        array = jnp.concatenate([before, array, after], axis=dim)
    return array


def times_unit(value, sign):
    return (-sign * value[1], sign * value[0])


def mult_block(direction, first, second):
    if direction == 0:
        return (times_unit(second, -1.0), times_unit(first, -1.0))
    if direction == 1:
        return ((-second[0], -second[1]), first)
    if direction == 2:
        return (times_unit(first, -1.0), times_unit(second, 1.0))
    return (first, second)


def half_spinor(direction, pair, sign):
    upper_a = (pair[0][:, 0], pair[1][:, 0])
    upper_b = (pair[0][:, 1], pair[1][:, 1])
    lower_a = (pair[0][:, 2], pair[1][:, 2])
    lower_b = (pair[0][:, 3], pair[1][:, 3])
    moved_a, moved_b = mult_block(direction, lower_a, lower_b)
    real_part = jnp.stack([upper_a[0] + sign * moved_a[0], upper_b[0] + sign * moved_b[0]], 1)
    imag_part = jnp.stack([upper_a[1] + sign * moved_a[1], upper_b[1] + sign * moved_b[1]], 1)
    return (real_part, imag_part)


def rebuild(direction, pair, sign):
    first = (pair[0][:, 0], pair[1][:, 0])
    second = (pair[0][:, 1], pair[1][:, 1])
    if direction == 3:
        lower_a = (sign * first[0], sign * first[1])
        lower_b = (sign * second[0], sign * second[1])
    else:
        moved_a, moved_b = mult_block(direction, first, second)
        lower_a = (-sign * moved_a[0], -sign * moved_a[1])
        lower_b = (-sign * moved_b[0], -sign * moved_b[1])
    real_part = jnp.stack([first[0], second[0], lower_a[0], lower_b[0]], 1)
    imag_part = jnp.stack([first[1], second[1], lower_a[1], lower_b[1]], 1)
    return (real_part, imag_part)


def color_apply(link_re, link_im, field_re, field_im, dagger):
    out_re = []
    out_im = []
    for row in range(3):
        acc_re = 0.0
        acc_im = 0.0
        for col in range(3):
            if dagger:
                entry_re = link_re[:, col, row][:, None, None]
                entry_im = -link_im[:, col, row][:, None, None]
            else:
                entry_re = link_re[:, row, col][:, None, None]
                entry_im = link_im[:, row, col][:, None, None]
            vec_re = field_re[:, :, col]
            vec_im = field_im[:, :, col]
            acc_re = acc_re + entry_re * vec_re - entry_im * vec_im
            acc_im = acc_im + entry_re * vec_im + entry_im * vec_re
        out_re.append(acc_re)
        out_im.append(acc_im)
    return (jnp.stack(out_re, 2), jnp.stack(out_im, 2))


def plane_shift(values, direction, stride, row_len):
    if direction == 1:
        return jnp.roll(values, -stride * row_len, axis=-1)
    column = jnp.arange(values.shape[-1]) % row_len
    if stride == 1:
        return jnp.where(
            column == row_len - 1, jnp.roll(values, row_len - 1, -1), jnp.roll(values, -1, -1)
        )
    return jnp.where(column == 0, jnp.roll(values, -(row_len - 1), -1), jnp.roll(values, 1, -1))


def split_parts(values):
    widened = values.astype(jnp.float32)
    return (widened[:, 0], widened[:, 1])


def stored(pair):
    return jnp.stack([pair[0], pair[1]], 1).astype(jnp.bfloat16)


def minus_chi(direction, pair):
    return stored(half_spinor(direction, pair, -1.0))


def plus_chi(direction, pair, link_pair):
    half = half_spinor(direction, pair, 1.0)
    return stored(color_apply(link_pair[0], link_pair[1], half[0], half[1], True))


def direction_term(direction, ahead, behind, link_pair):
    ahead_pair = split_parts(ahead)
    behind_pair = split_parts(behind)
    moved = color_apply(link_pair[0], link_pair[1], ahead_pair[0], ahead_pair[1], False)
    forward = rebuild(direction, moved, -1.0)
    backward = rebuild(direction, behind_pair, 1.0)
    return (forward[0] + backward[0], forward[1] + backward[1])


def exchange(value, axes):
    return lax.all_to_all(value, axes, 0, 0, tiled=True)


def all_reduce(partial_value):
    plane = lax.axis_size(PLANE)
    depth = lax.axis_size("z")
    flat = partial_value.reshape(plane, -1, 128)
    mine = exchange(flat, PLANE).sum(0)
    copies = jnp.broadcast_to(mine, (depth, *mine.shape))
    mine = exchange(copies, "z").sum(0)
    copies = jnp.broadcast_to(mine, (plane, *mine.shape))
    return exchange(copies, PLANE).reshape(partial_value.shape)


def contract(matrices, values):

    def product(left, right):
        return jnp.einsum("tkl,tasl->task", left, right, precision=highest)

    real_part = product(matrices[:, 0], values[:, 0]) - product(matrices[:, 1], values[:, 1])
    imag_part = product(matrices[:, 0], values[:, 1]) + product(matrices[:, 1], values[:, 0])
    return jnp.stack([real_part, imag_part], 1)


def local(sources, gauge_links, eigenvectors, elementals):
    tm_last = lax.axis_size(TM) - 1
    tm_index = lax.axis_index(TM)
    local_t = sources.shape[0]
    link_here = [split_parts(gauge_links[direction]) for direction in range(4)]
    below_t = from_behind(gauge_links[3], TM, 1)
    below_z = from_behind(gauge_links[2], SPACE, 1)
    link_t_back = split_parts(jnp.concatenate([below_t, gauge_links[3][:-1]], 0))
    link_z_back = split_parts(jnp.concatenate([below_z, gauge_links[2][:, :, :, :, :-1, :]], 4))
    tpos = jnp.arange(local_t).reshape(-1, 1, 1, 1, 1, 1, 1)
    ahead_sign = jnp.where((tpos == local_t - 1) & (tm_index == tm_last), -1.0, 1.0)
    behind_sign = jnp.where((tpos == 0) & (tm_index == 0), -1.0, 1.0)
    current = sources
    for sweep in range(3):
        pair = split_parts(current)
        ahead = {}
        behind = {}
        for apply_direction in range(2):
            ahead[apply_direction] = plane_shift(
                minus_chi(apply_direction, pair), apply_direction, 1, LX
            )
            behind[apply_direction] = plane_shift(
                plus_chi(apply_direction, pair, link_here[apply_direction]), apply_direction, -1, LX
            )
        padded = with_halo(current, ((TM, 0), (SPACE, 5)), 1)
        along_t = padded[:, :, :, :, :, 1:-1, :].astype(jnp.float32)
        along_z = padded[1:-1]
        ahead[3] = minus_chi(3, split_parts(ahead_sign * along_t[2:]))
        behind[3] = plus_chi(3, split_parts(behind_sign * along_t[:-2]), link_t_back)
        ahead[2] = minus_chi(2, split_parts(along_z[:, :, :, :, :, 2:, :]))
        behind[2] = plus_chi(2, split_parts(along_z[:, :, :, :, :, :-2, :]), link_z_back)
        result_re = 0.0
        result_im = 0.0
        for apply_direction in range(4):
            term_re, term_im = direction_term(
                apply_direction,
                ahead[apply_direction],
                behind[apply_direction],
                link_here[apply_direction],
            )
            result_re = result_re + term_re
            result_im = result_im + term_im
        current = (
            sources.astype(jnp.float32) + hopping * jnp.stack([result_re, result_im], 1)
        ).astype(jnp.bfloat16)
    flipped = jnp.stack([current[:, 1], -current[:, 0]], 1)
    stacked = jnp.stack([current, flipped], 1)
    partial_value = jnp.einsum(
        "tkrczp,toracszp->toask", eigenvectors, stacked, preferred_element_type=jnp.float32
    )
    modes_dev = elementals.shape[2]
    totals = all_reduce(partial_value)
    projected = lax.dynamic_slice_in_dim(totals, lax.axis_index(SPACE) * modes_dev, modes_dev, 4)
    contracted = contract(elementals, totals)
    return (projected, contracted)


def solution(mesh):
    placed = (
        P(TM, None, None, None, None, SPACE, None),
        P(None, TM, None, None, None, SPACE, None),
        P(TM, None, None, None, SPACE, None),
        P(TM, None, SPACE, None),
    )
    fine = Mesh(mesh.devices.reshape(2, 2, 4, 16, 2), (*TM, *SPACE))
    return jax.shard_map(
        local,
        mesh=fine,
        in_specs=placed,
        out_specs=(P(TM, None, None, None, SPACE), P(TM, None, None, None, SPACE)),
        check_vma=False,
    )
```

```python
import functools

import jax
import jax.numpy as jnp
from jax import lax
from jax.experimental import pallas as pl
from jax.experimental.pallas import tpu as pltpu
from jax.sharding import Mesh
from jax.sharding import PartitionSpec as P

HOPPING = 0.125
TM = ("y_hi", "core")
SPACE = ("x", "z", "y_lo")
PLANE = ("x", "y_lo")
POSITION = ("x", "z")
BLOCK = ("y_lo", "y_hi", "core")
LX = 8
FIELD = 48
LINK = 72
ROWS = FIELD + LINK
SITES = 128
F32 = jnp.float32
BF16 = jnp.bfloat16


def exchange(value, axes):
    return lax.all_to_all(value, axes, 0, 0, tiled=True)


def from_behind(value, axes, steps):
    count = lax.axis_size(axes)
    return lax.ppermute(value, axes, [(i, (i + steps) % count) for i in range(count)])


def local_call(kernel, outs, scratch, flops):
    return pl.pallas_call(
        kernel,
        out_shape=outs,
        scratch_shapes=scratch,
        compiler_params=pltpu.CompilerParams(vmem_limit_bytes=16 << 20),
        cost_estimate=pl.CostEstimate(flops=flops, bytes_accessed=1 << 20, transcendentals=0),
    )


def pack_kernel(source_ref, link_ref, out_ref, rows, links):
    for entry in range(36):
        links[2 * entry : 2 * entry + 2] = link_ref[entry].astype(F32)
    shared = links[...]
    for target in range(8):
        for part in range(2):
            for color in range(3):
                for which in range(2):
                    at = part * 24 + color * 8 + which * 4
                    if target < 6:
                        piece = source_ref[part, color, 2 * target + which].astype(F32)
                    else:
                        piece = jnp.zeros((4, SITES), F32)
                    rows[target, at : at + 4] = piece
        rows[target, FIELD:] = shared
    out_ref[...] = rows[...].astype(BF16)


def signed_add(base, sign, value):
    if base is None:
        return value if sign > 0 else -value
    return base + value if sign > 0 else base - value


def block_terms(direction, first, second):
    if direction == 0:
        return (((1, second[1]), (-1, second[0])), ((1, first[1]), (-1, first[0])))
    if direction == 1:
        return (((-1, second[0]), (-1, second[1])), ((1, first[0]), (1, first[1])))
    if direction == 2:
        return (((1, first[1]), (-1, first[0])), ((-1, second[1]), (1, second[0])))
    return (((1, first[0]), (1, first[1])), ((1, second[0]), (1, second[1])))


def half_of(field, direction, sign):
    half = []
    for color in range(3):
        up = [(field(0, color, a), field(1, color, a)) for a in range(4)]
        terms = block_terms(direction, up[2], up[3])
        half.append(
            [
                tuple(
                    signed_add(up[a][part], sign * terms[a][part][0], terms[a][part][1])
                    for part in range(2)
                )
                for a in range(2)
            ]
        )
    return half


def color_apply(link, direction, half, dagger):
    out = []
    for row in range(3):
        acc = [[None, None], [None, None]]
        for col in range(3):
            i, j = (col, row) if dagger else (row, col)
            re, im = link(direction, i, j, 0), link(direction, i, j, 1)
            flip = -1 if dagger else 1
            for a in range(2):
                vec_re, vec_im = half[col][a]
                acc[a][0] = signed_add(acc[a][0], 1, re * vec_re)
                acc[a][0] = signed_add(acc[a][0], -flip, im * vec_im)
                acc[a][1] = signed_add(acc[a][1], 1, re * vec_im)
                acc[a][1] = signed_add(acc[a][1], flip, im * vec_re)
        out.append([tuple(acc[a]) for a in range(2)])
    return out


def shift(value, direction, ahead):
    if direction == 3:
        return pltpu.roll(value, 6 if ahead else 2, 0)
    if direction == 1:
        return pltpu.roll(value, SITES - LX if ahead else LX, 1)
    column = lax.broadcasted_iota(jnp.int32, value.shape, 1) % LX
    if ahead:
        return jnp.where(
            column == LX - 1, pltpu.roll(value, LX - 1, 1), pltpu.roll(value, SITES - 1, 1)
        )
    return jnp.where(column == 0, pltpu.roll(value, SITES - (LX - 1), 1), pltpu.roll(value, 1, 1))


def map_half(function, half):
    return [[tuple(function(v) for v in pair) for pair in spins] for spins in half]


def accumulate(total, direction, ahead, behind):
    for color in range(3):
        both = []
        for a in range(2):
            for part in range(2):
                key = (part, color, a)
                value = ahead[color][a][part] + behind[color][a][part]
                total[key] = value if key not in total else total[key] + value
            both.append(tuple(ahead[color][a][part] - behind[color][a][part] for part in range(2)))
        terms = block_terms(direction, both[0], both[1])
        outer = -1 if direction == 3 else 1
        for a in range(2):
            for part in range(2):
                key = (part, color, a + 2)
                sign, value = terms[a][part]
                total[key] = signed_add(total.get(key), outer * sign, value)


def hop(field, link, ahead_z, behind_z):
    total = {}
    for direction in (0, 1, 3):
        ahead = map_half(
            lambda v, d=direction: shift(v, d, True), half_of(field, direction, -1)
        )
        behind = color_apply(link, direction, half_of(field, direction, 1), True)
        behind = map_half(lambda v, d=direction: shift(v, d, False), behind)
        accumulate(total, direction, color_apply(link, direction, ahead, False), behind)
    accumulate(total, 2, color_apply(link, 2, ahead_z(), False), behind_z())
    return total


def comp(part, color, spin):
    return color * 8 + part * 4 + spin


def slot(direction, row, col, part):
    return direction * 18 + row * 6 + col * 2 + part


def field_at(ref, layer):
    return lambda part, color, spin: ref[layer, comp(part, color, spin)]


def link_at(ref, layer):
    return lambda direction, row, col, part: ref[layer, slot(direction, row, col, part)]


def put_half(ref, half):
    for color in range(3):
        for a in range(2):
            for part in range(2):
                ref[color * 4 + a * 2 + part] = half[color][a][part].astype(BF16)


def get_half(ref):
    return [
        [tuple(ref[color * 4 + a * 2 + part].astype(F32) for part in range(2)) for a in range(2)]
        for color in range(3)
    ]


def first_kernel(
    below_ref, own_ref, above_ref, base_ref, link_ref, out_ref, low_ref, high_ref, wide, src, phi, links
):
    for at, ref in enumerate((below_ref, own_ref, above_ref)):
        wide[at * 8 * ROWS : (at + 1) * 8 * ROWS] = ref[...].reshape(8 * ROWS, SITES).astype(F32)
    slices = lax.broadcasted_iota(jnp.int32, (4, SITES), 0)
    turn = jnp.where(slices == 3, -1.0, 1.0)

    def assemble(layer, carry):
        start = layer * 4 * ROWS
        for color in range(3):
            for part in range(2):
                for spin in range(4):
                    for which in range(2):
                        row = start + part * 24 + color * 8 + which * 4 + spin
                        src[layer, comp(part, color, spin), pl.ds(which, 4, stride=2)] = wide[
                            pl.ds(row, 4, stride=ROWS)
                        ]
        for entry in range(LINK):
            value = wide[pl.ds(start + FIELD + entry, 4, stride=ROWS)]
            if entry >= 54:
                value = value * turn
            for which in range(2):
                links[layer, entry, pl.ds(which, 4, stride=2)] = value
        return carry

    lax.fori_loop(0, 6, assemble, 0)

    def sweep(from_ref, to_ref, layer, target):
        def ahead_z():
            return half_of(field_at(from_ref, layer + 1), 2, -1)

        def behind_z():
            half = half_of(field_at(from_ref, layer - 1), 2, 1)
            return color_apply(link_at(links, layer - 1), 2, half, True)

        total = hop(field_at(from_ref, layer), link_at(links, layer), ahead_z, behind_z)
        for (part, color, spin), value in total.items():
            at = comp(part, color, spin)
            to_ref[target, at] = src[layer, at] + HOPPING * value

    def one(layer, carry):
        sweep(src, phi, layer, layer)
        return carry

    lax.fori_loop(1, 5, one, 0)

    def two(layer, carry):
        sweep(phi, out_ref, layer, layer - 2)
        return carry

    lax.fori_loop(2, 4, two, 0)
    base_ref[...] = src[2:4]
    link_ref[...] = links[2:4]
    put_half(low_ref, half_of(field_at(out_ref, 0), 2, -1))
    high = half_of(field_at(out_ref, 1), 2, 1)
    put_half(high_ref, color_apply(link_at(links, 3), 2, high, True))


def second_kernel(base_ref, link_ref, phi_ref, low_ref, high_ref, out_ref, done):
    for layer in range(2):
        if layer == 0:

            def ahead_z():
                return half_of(field_at(phi_ref, 1), 2, -1)

            def behind_z():
                return get_half(high_ref)
        else:

            def ahead_z():
                return get_half(low_ref)

            def behind_z():
                half = half_of(field_at(phi_ref, 0), 2, 1)
                return color_apply(link_at(link_ref, 0), 2, half, True)

        total = hop(field_at(phi_ref, layer), link_at(link_ref, layer), ahead_z, behind_z)
        for (part, color, spin), value in total.items():
            at = comp(part, color, spin)
            done[(layer * 24 + at) * 8 : (layer * 24 + at + 1) * 8] = (
                base_ref[layer, at] + HOPPING * value
            )
    for layer in range(2):
        for time in range(4):
            for color in range(3):
                start = (layer * 24 + color * 8) * 8 + 2 * time
                pair = [done[pl.ds(start + which, 8, stride=8)] for which in range(2)]
                out_ref[layer * 4 + time, color * 16 : color * 16 + 16] = jnp.concatenate(
                    pair, 0
                ).astype(BF16)


def project_kernel(phi_ref, vector_ref, out_ref):
    totals = [None, None]
    for color in range(3):
        rows = phi_ref[:, color * 16 : color * 16 + 16].reshape(8 * 16, SITES)
        for part in range(2):
            value = lax.dot_general(
                rows,
                vector_ref[color, part],
                (((1,), (1,)), ((), ())),
                preferred_element_type=F32,
            )
            totals[part] = value if totals[part] is None else totals[part] + value
    crossed = pltpu.roll(totals[1].reshape(16, 8, 128), 4, 1)
    upper = lax.broadcasted_iota(jnp.int32, crossed.shape, 1) < 4
    mixed = totals[0].reshape(16, 8, 128) + jnp.where(upper, crossed, -crossed)
    out_ref[...] = mixed.reshape(8, 16, 128)


def all_reduce(partial_value):
    plane = lax.axis_size(PLANE)
    depth = lax.axis_size("z")
    mine = exchange(partial_value, PLANE).sum(0)
    copies = jnp.broadcast_to(mine, (depth, *mine.shape))
    mine = exchange(copies, "z").sum(0)
    copies = jnp.broadcast_to(mine, (plane, *mine.shape))
    return exchange(copies, PLANE)


def spinors(sources, gauge_links):
    moved = sources[0, :, :, :, :, 0].transpose(0, 2, 3, 1, 4)
    entries = gauge_links[:, 0, :, :, :, 0].transpose(0, 2, 3, 1, 4).reshape(36, 2, SITES)
    packed = local_call(
        pack_kernel,
        jax.ShapeDtypeStruct((8, ROWS, SITES), BF16),
        [pltpu.VMEM((8, ROWS, SITES), F32), pltpu.VMEM((LINK, SITES), F32)],
        1 << 17,
    )(moved, entries)
    own = exchange(packed, BLOCK)
    below = from_behind(own, POSITION, 1)
    above = from_behind(own, POSITION, -1)
    vectors = (8, SITES)
    base, links, phi, low, high = local_call(
        first_kernel,
        (
            jax.ShapeDtypeStruct((2, 24, *vectors), F32),
            jax.ShapeDtypeStruct((2, LINK, *vectors), F32),
            jax.ShapeDtypeStruct((2, 24, *vectors), F32),
            jax.ShapeDtypeStruct((12, *vectors), BF16),
            jax.ShapeDtypeStruct((12, *vectors), BF16),
        ),
        [
            pltpu.VMEM((3 * 8 * ROWS, SITES), F32),
            pltpu.VMEM((6, 24, *vectors), F32),
            pltpu.VMEM((6, 24, *vectors), F32),
            pltpu.VMEM((6, LINK, *vectors), F32),
        ],
        1 << 24,
    )(below, own, above)
    high = from_behind(high, POSITION, 1)
    low = from_behind(low, POSITION, -1)
    done = local_call(
        second_kernel,
        jax.ShapeDtypeStruct((8, FIELD, SITES), BF16),
        [pltpu.VMEM((2 * 24 * 8, SITES), F32)],
        1 << 23,
    )(base, links, phi, low, high)
    return exchange(done, BLOCK)


def contract(matrices, values):
    product = functools.partial(jnp.einsum, "xl,sral->sra", precision=lax.Precision.HIGHEST)
    by_re, by_im = product(matrices[0], values), product(matrices[1], values)
    real_part = by_re[:, 0] - by_im[:, 1]
    imag_part = by_re[:, 1] + by_im[:, 0]
    return jnp.stack([real_part, imag_part], 1)


def placed_out(values):
    return values.transpose(1, 2, 0)[None, :, :, :, None]


def local(sources, gauge_links, eigenvectors, elementals):
    vectors = eigenvectors[0, :, :, :, 0].transpose(2, 1, 0, 3)
    finals = spinors(sources, gauge_links)
    partial_value = local_call(
        project_kernel, jax.ShapeDtypeStruct((8, 16, 128), F32), [], 1 << 25
    )(finals, vectors)
    totals = all_reduce(partial_value)[:6].reshape(12, 2, 4, 128)
    mine = lax.dynamic_slice_in_dim(totals, lax.axis_index(SPACE), 1, 3)[..., 0]
    return placed_out(mine), placed_out(contract(elementals[0], totals))


def solution(mesh):
    fine = Mesh(mesh.devices.reshape(2, 2, 4, 16, 2), (*TM, *SPACE))
    placed = (
        P(TM, None, None, None, None, SPACE, None),
        P(None, TM, None, None, None, SPACE, None),
        P(TM, None, None, None, SPACE, None),
        P(TM, None, SPACE, None),
    )
    result = P(TM, None, None, None, SPACE)
    return jax.shard_map(
        local, mesh=fine, in_specs=placed, out_specs=(result, result), check_vma=False
    )
```

```python
import jax
import jax.numpy as jnp
from jax import lax
from jax.experimental import pallas as pl
from jax.experimental.pallas import tpu as pltpu
from jax.sharding import Mesh
from jax.sharding import PartitionSpec as P

HOPPING = 0.125
TM = ("y_hi", "core")
SPACE = ("x", "z", "y_lo")
PLANE = ("x", "y_lo")
POSITION = ("x", "z")
BLOCK = ("y_lo", "y_hi", "core")
LX = 8
FIELD = 48
LINK = 72
ROWS = FIELD + LINK
SITES = 128
F32 = jnp.float32
BF16 = jnp.bfloat16


def exchange(value, axes):
    return lax.all_to_all(value, axes, 0, 0, tiled=True)


def from_behind(value, axes, steps):
    count = lax.axis_size(axes)
    return lax.ppermute(value, axes, [(i, (i + steps) % count) for i in range(count)])


def local_call(kernel, outs, scratch, flops, **options):
    return pl.pallas_call(
        kernel,
        **options,
        out_shape=outs,
        scratch_shapes=scratch,
        compiler_params=pltpu.CompilerParams(vmem_limit_bytes=16 << 20),
        cost_estimate=pl.CostEstimate(flops=flops, bytes_accessed=1 << 20, transcendentals=0),
    )


def pack_kernel(source_ref, link_ref, out_ref, rows, links):
    for entry in range(36):
        links[2 * entry : 2 * entry + 2] = link_ref[entry].astype(F32)
    shared = links[...]
    for target in range(8):
        rows[target, FIELD:] = shared
    for target in range(8):
        for part in range(2):
            for color in range(3):
                for which in range(2):
                    at = part * 24 + color * 8 + which * 4
                    if target < 6:
                        piece = source_ref[part, color, 2 * target + which].astype(F32)
                    else:
                        piece = jnp.zeros((4, SITES), F32)
                    rows[target, at : at + 4] = piece
    out_ref[...] = rows[...].astype(BF16)


def signed_add(base, sign, value):
    if base is None:
        return value if sign > 0 else -value
    return base + value if sign > 0 else base - value


def block_terms(direction, first, second):
    if direction == 0:
        return (((1, second[1]), (-1, second[0])), ((1, first[1]), (-1, first[0])))
    if direction == 1:
        return (((-1, second[0]), (-1, second[1])), ((1, first[0]), (1, first[1])))
    if direction == 2:
        return (((1, first[1]), (-1, first[0])), ((-1, second[1]), (1, second[0])))
    return (((1, first[0]), (1, first[1])), ((1, second[0]), (1, second[1])))


def half_of(field, direction, sign):
    half = []
    for color in range(3):
        up = [(field(0, color, a), field(1, color, a)) for a in range(4)]
        terms = block_terms(direction, up[2], up[3])
        half.append(
            [
                tuple(
                    signed_add(up[a][part], sign * terms[a][part][0], terms[a][part][1])
                    for part in range(2)
                )
                for a in range(2)
            ]
        )
    return half


def color_apply(link, direction, half, dagger):
    out = []
    for row in range(3):
        acc = [[None, None], [None, None]]
        for col in range(3):
            i, j = (col, row) if dagger else (row, col)
            re, im = link(direction, i, j, 0), link(direction, i, j, 1)
            flip = -1 if dagger else 1
            for a in range(2):
                vec_re, vec_im = half[col][a]
                acc[a][0] = signed_add(acc[a][0], 1, re * vec_re)
                acc[a][0] = signed_add(acc[a][0], -flip, im * vec_im)
                acc[a][1] = signed_add(acc[a][1], 1, re * vec_im)
                acc[a][1] = signed_add(acc[a][1], flip, im * vec_re)
        out.append([tuple(acc[a]) for a in range(2)])
    return out


def shift(value, direction, ahead):
    if direction == 3:
        return pltpu.roll(value, 6 if ahead else 2, 0)
    if direction == 1:
        return pltpu.roll(value, SITES - LX if ahead else LX, 1)
    column = lax.broadcasted_iota(jnp.int32, value.shape, 1) % LX
    if ahead:
        return jnp.where(
            column == LX - 1, pltpu.roll(value, LX - 1, 1), pltpu.roll(value, SITES - 1, 1)
        )
    return jnp.where(column == 0, pltpu.roll(value, SITES - (LX - 1), 1), pltpu.roll(value, 1, 1))


def map_half(function, half):
    return [[tuple(function(v) for v in pair) for pair in spins] for spins in half]


def accumulate(total, direction, ahead, behind):
    for color in range(3):
        both = []
        for a in range(2):
            for part in range(2):
                key = (part, color, a)
                value = ahead[color][a][part] + behind[color][a][part]
                total[key] = value if key not in total else total[key] + value
            both.append(tuple(ahead[color][a][part] - behind[color][a][part] for part in range(2)))
        terms = block_terms(direction, both[0], both[1])
        outer = -1 if direction == 3 else 1
        for a in range(2):
            for part in range(2):
                key = (part, color, a + 2)
                sign, value = terms[a][part]
                total[key] = signed_add(total.get(key), outer * sign, value)


def hop(field, link, ahead_z, behind_z):
    total = {}
    for direction in (0, 1, 3):
        ahead = map_half(
            lambda v, d=direction: shift(v, d, True), half_of(field, direction, -1)
        )
        behind = color_apply(link, direction, half_of(field, direction, 1), True)
        behind = map_half(lambda v, d=direction: shift(v, d, False), behind)
        accumulate(total, direction, color_apply(link, direction, ahead, False), behind)
    accumulate(total, 2, color_apply(link, 2, ahead_z, False), behind_z)
    return total


def comp(part, color, spin):
    return color * 8 + part * 4 + spin


def slot(direction, row, col, part):
    return direction * 18 + row * 6 + col * 2 + part


def field_at(ref, layer):
    return lambda part, color, spin: ref[layer, comp(part, color, spin)]


def link_at(ref, layer):
    return lambda direction, row, col, part: ref[layer, slot(direction, row, col, part)]


def half_slot(part, color, spin):
    return color * 4 + spin * 2 + part


def put_half(ref, half):
    for color in range(3):
        for a in range(2):
            for part in range(2):
                ref[half_slot(part, color, a)] = half[color][a][part].astype(ref.dtype)


def get_half(ref, layer):
    return [
        [tuple(ref[layer, half_slot(part, color, a)] for part in range(2)) for a in range(2)]
        for color in range(3)
    ]


def assemble(wide, start, src, links, layer):
    slices = lax.broadcasted_iota(jnp.int32, (4, SITES), 0)
    turn = jnp.where(slices == 3, -1.0, 1.0)
    for color in range(3):
        for part in range(2):
            for spin in range(4):
                for which in range(2):
                    row = start + part * 24 + color * 8 + which * 4 + spin
                    src[layer, comp(part, color, spin), pl.ds(which, 4, stride=2)] = wide[
                        pl.ds(row, 4, stride=ROWS)
                    ]
    for entry in range(LINK):
        value = wide[pl.ds(start + FIELD + entry, 4, stride=ROWS)]
        if entry >= 54:
            value = value * turn
        for which in range(2):
            links[layer, entry, pl.ds(which, 4, stride=2)] = value


def sent_down(field):
    return half_of(field, 2, -1)


def sent_up(field, link):
    return color_apply(link, 2, half_of(field, 2, 1), True)


def own_kernel(own_ref, matrix_ref, base_ref, link_ref, low_ref, high_ref, kept_ref, wide):
    kept_ref[...] = matrix_ref[...]
    wide[...] = own_ref[...].reshape(8 * ROWS, SITES).astype(F32)

    def one(layer, carry):
        assemble(wide, layer * 4 * ROWS, base_ref, link_ref, layer)
        return carry

    lax.fori_loop(0, 2, one, 0)
    put_half(low_ref, sent_down(field_at(base_ref, 0)))
    put_half(high_ref, sent_up(field_at(base_ref, 1), link_at(link_ref, 1)))


def sweep_kernel(
    below_ref, above_ref, base_ref, link_ref, low_ref, high_ref, out_ref,
    wide, src, one, two, links, ahead, behind, done,
):
    for at, ref in enumerate((below_ref, above_ref)):
        wide[at * 8 * ROWS : (at + 1) * 8 * ROWS] = ref[...].reshape(8 * ROWS, SITES).astype(F32)

    def gather(layer, carry):
        assemble(wide, layer * 4 * ROWS, src, links, layer + 2 * (layer // 2))
        return carry

    lax.fori_loop(0, 4, gather, 0)
    src[2:4] = base_ref[...]
    links[2:4] = link_ref[...]
    ahead[6] = low_ref[...].astype(F32)
    behind[0] = high_ref[...].astype(F32)

    def sweep(from_ref, halves, layers, put):
        def prepare(layer, carry):
            put_half(ahead.at[layer], sent_down(field_at(from_ref, layer)))
            put_half(behind.at[layer + 1], sent_up(field_at(from_ref, layer), link_at(links, layer)))
            return carry

        def step(layer, carry):
            total = hop(
                field_at(from_ref, layer),
                link_at(links, layer),
                get_half(ahead, layer + 1),
                get_half(behind, layer),
            )
            for key, value in total.items():
                put(layer, comp(*key), src[layer, comp(*key)] + HOPPING * value)
            return carry

        lax.fori_loop(*halves, prepare, 0)
        lax.fori_loop(*layers, step, 0)

    def put_one(layer, at, value):
        one[layer, at] = value

    def put_two(layer, at, value):
        two[layer, at] = value

    def put_done(layer, at, value):
        done[pl.ds(pl.multiple_of(((layer - 2) * 24 + at) * 8, 8), 8)] = value

    sweep(src, (0, 6), (0, 6), put_one)
    sweep(one, (0, 6), (1, 5), put_two)
    sweep(two, (1, 5), (2, 4), put_done)
    for layer in range(2):
        for time in range(4):
            for color in range(3):
                start = (layer * 24 + color * 8) * 8 + 2 * time
                pair = [done[pl.ds(start + which, 8, stride=8)] for which in range(2)]
                out_ref[layer * 4 + time, color * 16 : color * 16 + 16] = jnp.concatenate(
                    pair, 0
                ).astype(BF16)


def project_kernel(phi_ref, vector_ref, out_ref):
    totals = [None, None]
    for color in range(3):
        rows = phi_ref[:, color * 16 : color * 16 + 16].reshape(8 * 16, SITES)
        for part in range(2):
            value = lax.dot_general(
                rows,
                vector_ref[color, part],
                (((1,), (1,)), ((), ())),
                preferred_element_type=F32,
            )
            totals[part] = value if totals[part] is None else totals[part] + value
    crossed = pltpu.roll(totals[1].reshape(16, 8, 128), 4, 1)
    upper = lax.broadcasted_iota(jnp.int32, crossed.shape, 1) < 4
    mixed = totals[0].reshape(16, 8, 128) + jnp.where(upper, crossed, -crossed)
    out_ref[...] = mixed.reshape(8, 16, 128).astype(BF16)


def spread_kernel(value_ref, out_ref):
    total = value_ref[0].astype(F32)
    for member in range(1, value_ref.shape[0]):
        total = total + value_ref[member].astype(F32)
    total = total.astype(BF16)
    for member in range(out_ref.shape[0]):
        out_ref[member] = total


def summed(value, copies):
    shape = jax.ShapeDtypeStruct((copies, *value.shape[1:]), BF16)
    return local_call(spread_kernel, shape, [], 1 << 16)(value)


def all_reduce(partial_value):
    plane = lax.axis_size(PLANE)
    depth = lax.axis_size("z")
    copies = summed(exchange(partial_value, PLANE), depth)
    copies = summed(exchange(copies, "z"), plane)
    return exchange(copies, PLANE)


def spinors(sources, gauge_links, matrix):
    moved = sources[0, :, :, :, :, 0].transpose(0, 2, 3, 1, 4)
    entries = gauge_links[:, 0, :, :, :, 0].transpose(0, 2, 3, 1, 4).reshape(36, 2, SITES)
    packed = local_call(
        pack_kernel,
        jax.ShapeDtypeStruct((8, ROWS, SITES), BF16),
        [
            pltpu.VMEM((8, ROWS, SITES), F32),
            pltpu.VMEM((LINK, SITES), F32),
        ],
        1 << 17,
    )(moved, entries)
    own = exchange(packed, BLOCK)
    below = from_behind(own, POSITION, 1)
    above = from_behind(own, POSITION, -1)
    vectors = (8, SITES)
    base, links, low, high, kept = local_call(
        own_kernel,
        (
            jax.ShapeDtypeStruct((2, 24, *vectors), F32),
            jax.ShapeDtypeStruct((2, LINK, *vectors), F32),
            jax.ShapeDtypeStruct((12, *vectors), BF16),
            jax.ShapeDtypeStruct((12, *vectors), BF16),
            jax.ShapeDtypeStruct(matrix.shape, F32),
        ),
        [pltpu.VMEM((8 * ROWS, SITES), F32)],
        1 << 20,
    )(own, matrix)
    high = from_behind(high, POSITION, 2)
    low = from_behind(low, POSITION, -2)
    done = local_call(
        sweep_kernel,
        jax.ShapeDtypeStruct((8, FIELD, SITES), BF16),
        [
            pltpu.VMEM((2 * 8 * ROWS, SITES), F32),
            pltpu.VMEM((6, 24, *vectors), F32),
            pltpu.VMEM((6, 24, *vectors), F32),
            pltpu.VMEM((6, 24, *vectors), F32),
            pltpu.VMEM((6, LINK, *vectors), F32),
            pltpu.VMEM((7, 12, *vectors), F32),
            pltpu.VMEM((7, 12, *vectors), F32),
            pltpu.VMEM((2 * 24 * 8, SITES), F32),
        ],
        1 << 24,
    )(below, above, base, links, low, high)
    return exchange(done, BLOCK), kept


def finish_kernel(mine_ref, total_ref, matrix_ref, projected_ref, contracted_ref):
    lane = lax.broadcasted_iota(jnp.int32, (8, 128), 1)
    row_re = jnp.broadcast_to(matrix_ref[0:1], (8, 128))
    row_im = jnp.broadcast_to(matrix_ref[1:2], (8, 128))
    pick = lane == mine_ref[0]
    own, by_re, by_im = (jnp.zeros((8, 128), F32) for _ in range(3))
    for pair in range(6):
        both = total_ref[pair].astype(F32)
        for which in range(2):
            value = both[8 * which : 8 * which + 8]
            here = lane == 2 * pair + which
            own = jnp.where(here, jnp.sum(jnp.where(pick, value, 0.0), 1, keepdims=True), own)
            by_re = jnp.where(here, jnp.sum(value * row_re, 1, keepdims=True), by_re)
            by_im = jnp.where(here, jnp.sum(value * row_im, 1, keepdims=True), by_im)
    crossed = pltpu.roll(by_im, 4, 0)
    upper = lax.broadcasted_iota(jnp.int32, (8, 128), 0) < 4
    contracted = by_re + jnp.where(upper, -crossed, crossed)
    for row in range(8):
        projected_ref[row] = own[row : row + 1, :12]
        contracted_ref[row] = contracted[row : row + 1, :12]


def placed_out(values):
    return values.reshape(1, 2, 4, 1, 12).transpose(0, 1, 2, 4, 3)


def local(sources, gauge_links, eigenvectors, elementals):
    vectors = eigenvectors[0, :, :, :, 0].transpose(2, 1, 0, 3)
    finals, kept = spinors(sources, gauge_links, elementals[0, :, 0])
    partial_value = local_call(
        project_kernel, jax.ShapeDtypeStruct((8, 16, 128), BF16), [], 1 << 25
    )(finals, vectors)
    totals = all_reduce(partial_value)
    mine = lax.axis_index(SPACE).astype(jnp.int32).reshape(1)
    shape = jax.ShapeDtypeStruct((8, 1, 12), F32)
    projected, contracted = local_call(
        finish_kernel,
        (shape, shape),
        [],
        1 << 17,
        in_specs=[pl.BlockSpec(memory_space=pltpu.SMEM)] + [pl.BlockSpec()] * 2,
    )(mine, totals, kept)
    return placed_out(projected), placed_out(contracted)


def solution(mesh):
    fine = Mesh(mesh.devices.reshape(2, 2, 4, 16, 2), (*TM, *SPACE))
    placed = (
        P(TM, None, None, None, None, SPACE, None),
        P(None, TM, None, None, None, SPACE, None),
        P(TM, None, None, None, SPACE, None),
        P(TM, None, SPACE, None),
    )
    result = P(TM, None, None, None, SPACE)
    return jax.shard_map(
        local, mesh=fine, in_specs=placed, out_specs=(result, result), check_vma=False
    )
```

```python
import jax
import jax.numpy as jnp
from jax import lax
from jax.experimental import pallas as pl
from jax.experimental.pallas import tpu as pltpu
from jax.sharding import Mesh
from jax.sharding import PartitionSpec as P

HOPPING = 0.125
TM = ("y_hi", "core")
SPACE = ("x", "z_hi", "z_lo", "y_lo")
PLANE = ("x", "y_lo")
DEPTH = ("z_hi", "z_lo")
POSITION = ("x", *DEPTH)
BLOCK = ("y_lo", *TM)
GROUP = ("z_lo", *BLOCK)
LX = 8
FIELD = 48
LINK = 72
ROWS = FIELD + LINK
SITES = 128
F32 = jnp.float32
BF16 = jnp.bfloat16


def exchange(value, axes):
    return lax.all_to_all(value, axes, 0, 0, tiled=True)


def send(value, axes, steps):
    count = lax.axis_size(axes)
    pairs = [(i, (i + steps[1] if i % 2 else i - steps[0]) % count) for i in range(count)]
    return lax.ppermute(value, axes, pairs)


def local_call(kernel, outs, scratch, flops, **options):
    return pl.pallas_call(
        kernel,
        **options,
        out_shape=outs,
        scratch_shapes=scratch,
        compiler_params=pltpu.CompilerParams(vmem_limit_bytes=16 << 20),
        cost_estimate=pl.CostEstimate(flops=flops, bytes_accessed=1 << 20, transcendentals=0),
    )


def pack_kernel(place_ref, source_ref, link_ref, out_ref, side_ref, mine_ref, rows, links):
    side_ref[0] = place_ref[0]
    mine_ref[0] = place_ref[1]
    for entry in range(36):
        links[2 * entry : 2 * entry + 2] = link_ref[entry].astype(F32)
    shared = links[...]
    for target in range(8):
        rows[target, FIELD:] = shared
    for target in range(8):
        for part in range(2):
            for color in range(3):
                for which in range(2):
                    at = part * 24 + color * 8 + which * 4
                    if target < 6:
                        piece = source_ref[part, color, 2 * target + which].astype(F32)
                    else:
                        piece = jnp.zeros((4, SITES), F32)
                    rows[target, at : at + 4] = piece
    packed = rows[...].astype(BF16)
    out_ref[:8] = packed
    out_ref[8:] = packed


def signed_add(base, sign, value):
    if base is None:
        return value if sign > 0 else -value
    return base + value if sign > 0 else base - value


def block_terms(direction, first, second):
    if direction == 0:
        return (((1, second[1]), (-1, second[0])), ((1, first[1]), (-1, first[0])))
    if direction == 1:
        return (((-1, second[0]), (-1, second[1])), ((1, first[0]), (1, first[1])))
    if direction == 2:
        return (((1, first[1]), (-1, first[0])), ((-1, second[1]), (1, second[0])))
    return (((1, first[0]), (1, first[1])), ((1, second[0]), (1, second[1])))


def half_of(field, direction, sign):
    half = []
    for color in range(3):
        up = [(field(0, color, a), field(1, color, a)) for a in range(4)]
        terms = block_terms(direction, up[2], up[3])
        half.append(
            [
                tuple(
                    signed_add(up[a][part], sign * terms[a][part][0], terms[a][part][1])
                    for part in range(2)
                )
                for a in range(2)
            ]
        )
    return half


def color_apply(link, direction, half, dagger):
    out = []
    for row in range(3):
        acc = [[None, None], [None, None]]
        for col in range(3):
            i, j = (col, row) if dagger else (row, col)
            re, im = link(direction, i, j, 0), link(direction, i, j, 1)
            flip = -1 if dagger else 1
            for a in range(2):
                vec_re, vec_im = half[col][a]
                acc[a][0] = signed_add(acc[a][0], 1, re * vec_re)
                acc[a][0] = signed_add(acc[a][0], -flip, im * vec_im)
                acc[a][1] = signed_add(acc[a][1], 1, re * vec_im)
                acc[a][1] = signed_add(acc[a][1], flip, im * vec_re)
        out.append([tuple(acc[a]) for a in range(2)])
    return out


def shift(value, direction, ahead):
    if direction == 3:
        return pltpu.roll(value, 6 if ahead else 2, 0)
    if direction == 1:
        return pltpu.roll(value, SITES - LX if ahead else LX, 1)
    column = lax.broadcasted_iota(jnp.int32, value.shape, 1) % LX
    if ahead:
        return jnp.where(
            column == LX - 1, pltpu.roll(value, LX - 1, 1), pltpu.roll(value, SITES - 1, 1)
        )
    return jnp.where(column == 0, pltpu.roll(value, SITES - (LX - 1), 1), pltpu.roll(value, 1, 1))


def map_half(function, half):
    return [[tuple(function(v) for v in pair) for pair in spins] for spins in half]


def accumulate(total, direction, ahead, behind):
    for color in range(3):
        both = []
        for a in range(2):
            for part in range(2):
                key = (part, color, a)
                value = ahead[color][a][part] + behind[color][a][part]
                total[key] = value if key not in total else total[key] + value
            both.append(tuple(ahead[color][a][part] - behind[color][a][part] for part in range(2)))
        terms = block_terms(direction, both[0], both[1])
        outer = -1 if direction == 3 else 1
        for a in range(2):
            for part in range(2):
                key = (part, color, a + 2)
                sign, value = terms[a][part]
                total[key] = signed_add(total.get(key), outer * sign, value)


def hop(field, link, ahead_z, behind_z):
    total = {}
    for direction in (0, 1, 3):
        ahead = map_half(
            lambda v, d=direction: shift(v, d, True), half_of(field, direction, -1)
        )
        behind = color_apply(link, direction, half_of(field, direction, 1), True)
        behind = map_half(lambda v, d=direction: shift(v, d, False), behind)
        accumulate(total, direction, color_apply(link, direction, ahead, False), behind)
    accumulate(total, 2, color_apply(link, 2, ahead_z, False), behind_z)
    return total


def comp(part, color, spin):
    return color * 8 + part * 4 + spin


def slot(direction, row, col, part):
    return direction * 18 + row * 6 + col * 2 + part


def field_at(ref, layer):
    return lambda part, color, spin: ref[layer, comp(part, color, spin)]


def link_at(ref, layer):
    return lambda direction, row, col, part: ref[layer, slot(direction, row, col, part)]


def half_slot(part, color, spin):
    return color * 4 + spin * 2 + part


def put_half(ref, half):
    for color in range(3):
        for a in range(2):
            for part in range(2):
                ref[half_slot(part, color, a)] = half[color][a][part].astype(ref.dtype)


def get_half(ref, layer):
    return [
        [tuple(ref[layer, half_slot(part, color, a)] for part in range(2)) for a in range(2)]
        for color in range(3)
    ]


def assemble(wide, start, src, links, layer):
    slices = lax.broadcasted_iota(jnp.int32, (4, SITES), 0)
    turn = jnp.where(slices == 3, -1.0, 1.0)
    for color in range(3):
        for part in range(2):
            for spin in range(4):
                for which in range(2):
                    row = start + part * 24 + color * 8 + which * 4 + spin
                    src[layer, comp(part, color, spin), pl.ds(which, 4, stride=2)] = wide[
                        pl.ds(row, 4, stride=ROWS)
                    ]
    for entry in range(LINK):
        value = wide[pl.ds(start + FIELD + entry, 4, stride=ROWS)]
        if entry >= 54:
            value = value * turn
        for which in range(2):
            links[layer, entry, pl.ds(which, 4, stride=2)] = value


def sent_down(field):
    return half_of(field, 2, -1)


def sent_up(field, link):
    return color_apply(link, 2, half_of(field, 2, 1), True)


def own_kernel(side_ref, own_ref, base_ref, link_ref, near_ref, far_ref, wide):
    wide[...] = own_ref[...].reshape(16 * ROWS, SITES).astype(F32)
    side = side_ref[0]

    def one(layer, carry):
        assemble(wide, layer * 4 * ROWS, base_ref, link_ref, layer)
        return carry

    lax.fori_loop(0, 4, one, 0)
    near_ref[: 8 * ROWS] = own_ref[pl.ds(side * 8, 8)].reshape(8 * ROWS, SITES)

    def put(ref, start, below, above):
        for color in range(3):
            for a in range(2):
                at = start + 8 * half_slot(0, color, a)
                low = jnp.concatenate(below[color][a], 0)
                high = jnp.concatenate(above[color][a], 0)
                ref[at : at + 16] = jnp.where(side == 0, low, high).astype(BF16)

    def half_down(layer):
        return sent_down(field_at(base_ref, layer))

    def half_up(layer):
        return sent_up(field_at(base_ref, layer), link_at(link_ref, layer))

    put(near_ref, 8 * ROWS, half_down(2), half_up(1))
    put(far_ref, 0, half_down(0), half_up(3))


def keep_kernel(far_ref, matrix_ref, vector_ref, kept_matrix, kept_vector, tie_ref):
    kept_matrix[...] = matrix_ref[...]
    kept_vector[...] = vector_ref[...]
    tie_ref[...] = far_ref[:16]


def sweep_kernel(
    side_ref, near_ref, far_ref, base_ref, link_ref, tie_ref, out_ref,
    wide, src, one, two, links, ahead, behind, done,
):
    side = side_ref[0]
    wide[...] = near_ref[: 8 * ROWS].astype(F32)

    def gather(layer, carry):
        assemble(wide, layer * 4 * ROWS, src, links, layer + 4 * side)
        return carry

    lax.fori_loop(0, 2, gather, 0)
    src[pl.ds(2 - 2 * side, 4)] = base_ref[...]
    links[pl.ds(2 - 2 * side, 4)] = link_ref[...]
    near = near_ref[8 * ROWS :].astype(F32).reshape(12, 8, SITES)
    far = far_ref[...].astype(F32).reshape(12, 8, SITES)
    ahead[6] = jnp.where(side == 0, far, near)
    behind[0] = jnp.where(side == 0, near, far)

    def sweep(from_ref, halves, layers, put):
        def prepare(layer, carry):
            put_half(ahead.at[layer], sent_down(field_at(from_ref, layer)))
            put_half(behind.at[layer + 1], sent_up(field_at(from_ref, layer), link_at(links, layer)))
            return carry

        def step(layer, carry):
            total = hop(
                field_at(from_ref, layer),
                link_at(links, layer),
                get_half(ahead, layer + 1),
                get_half(behind, layer),
            )
            for key, value in total.items():
                put(layer, comp(*key), src[layer, comp(*key)] + HOPPING * value)
            return carry

        lax.fori_loop(*halves, prepare, 0)
        lax.fori_loop(*layers, step, 0)

    def put_one(layer, at, value):
        one[layer, at] = value

    def put_two(layer, at, value):
        two[layer, at] = value

    def put_done(layer, at, value):
        done[pl.ds(pl.multiple_of(((layer - 2) * 24 + at) * 8, 8), 8)] = value

    sweep(src, (0, 6), (0, 6), put_one)
    sweep(one, (0, 6), (1, 5), put_two)
    sweep(two, (1, 5), (2, 4), put_done)
    for layer in range(2):
        for time in range(4):
            for color in range(3):
                start = (layer * 24 + color * 8) * 8 + 2 * time
                pair = [done[pl.ds(start + which, 8, stride=8)] for which in range(2)]
                out_ref[layer * 4 + time, color * 16 : color * 16 + 16] = jnp.concatenate(
                    pair, 0
                ).astype(BF16)


def project_kernel(phi_ref, vector_ref, out_ref):
    totals = [None, None]
    for color in range(3):
        rows = phi_ref[:, color * 16 : color * 16 + 16].reshape(8 * 16, SITES)
        for part in range(2):
            value = lax.dot_general(
                rows,
                vector_ref[color, part],
                (((1,), (1,)), ((), ())),
                preferred_element_type=F32,
            )
            totals[part] = value if totals[part] is None else totals[part] + value
    crossed = pltpu.roll(totals[1].reshape(16, 8, 128), 4, 1)
    upper = lax.broadcasted_iota(jnp.int32, crossed.shape, 1) < 4
    mixed = totals[0].reshape(16, 8, 128) + jnp.where(upper, crossed, -crossed)
    out_ref[...] = mixed.reshape(8, 16, 128).astype(BF16)


def spread_kernel(value_ref, out_ref):
    total = value_ref[0].astype(F32)
    for member in range(1, value_ref.shape[0]):
        total = total + value_ref[member].astype(F32)
    total = total.astype(BF16)
    for member in range(out_ref.shape[0]):
        out_ref[member] = total


def summed(value, copies):
    shape = jax.ShapeDtypeStruct((copies, *value.shape[1:]), BF16)
    return local_call(spread_kernel, shape, [], 1 << 16)(value)


def all_reduce(partial_value):
    plane = lax.axis_size(PLANE)
    depth = lax.axis_size(DEPTH)
    copies = summed(exchange(partial_value, PLANE), depth)
    copies = summed(exchange(copies, DEPTH), plane)
    return exchange(copies, PLANE)


def spinors(sources, gauge_links, kept):
    moved = sources[0, :, :, :, :, 0].transpose(0, 2, 3, 1, 4)
    entries = gauge_links[:, 0, :, :, :, 0].transpose(0, 2, 3, 1, 4).reshape(36, 2, SITES)
    smem = [pl.BlockSpec(memory_space=pltpu.SMEM)]
    scalar = jax.ShapeDtypeStruct((1,), jnp.int32)
    place = jnp.stack([lax.axis_index("z_lo"), lax.axis_index(SPACE)]).astype(jnp.int32)
    packed, side, mine = local_call(
        pack_kernel,
        (jax.ShapeDtypeStruct((16, ROWS, SITES), BF16), scalar, scalar),
        [
            pltpu.VMEM((8, ROWS, SITES), F32),
            pltpu.VMEM((LINK, SITES), F32),
        ],
        1 << 17,
        in_specs=smem + [pl.BlockSpec()] * 2,
        out_specs=(pl.BlockSpec(), *smem, *smem),
    )(place, moved, entries)
    own = exchange(packed, GROUP)
    vectors = (8, SITES)
    base, links, near, far = local_call(
        own_kernel,
        (
            jax.ShapeDtypeStruct((4, 24, *vectors), F32),
            jax.ShapeDtypeStruct((4, LINK, *vectors), F32),
            jax.ShapeDtypeStruct((8 * ROWS + 96, SITES), BF16),
            jax.ShapeDtypeStruct((96, SITES), BF16),
        ),
        [pltpu.VMEM((16 * ROWS, SITES), F32)],
        1 << 20,
        in_specs=smem + [pl.BlockSpec()],
    )(side, own)
    matrix, spectrum = kept
    *kept, tie = local_call(
        keep_kernel,
        (
            jax.ShapeDtypeStruct(matrix.shape, F32),
            jax.ShapeDtypeStruct(spectrum.shape, BF16),
            jax.ShapeDtypeStruct((16, SITES), BF16),
        ),
        [],
        1 << 18,
    )(far, matrix, spectrum)
    near = send(near, POSITION, (1, 1))
    far = send(far, POSITION, (2, 2))
    done = local_call(
        sweep_kernel,
        jax.ShapeDtypeStruct((8, FIELD, SITES), BF16),
        [
            pltpu.VMEM((8 * ROWS, SITES), F32),
            pltpu.VMEM((6, 24, *vectors), F32),
            pltpu.VMEM((6, 24, *vectors), F32),
            pltpu.VMEM((6, 24, *vectors), F32),
            pltpu.VMEM((6, LINK, *vectors), F32),
            pltpu.VMEM((7, 12, *vectors), F32),
            pltpu.VMEM((7, 12, *vectors), F32),
            pltpu.VMEM((2 * 24 * 8, SITES), F32),
        ],
        1 << 24,
        in_specs=smem + [pl.BlockSpec()] * 5,
    )(side, near, far, base, links, tie)
    return exchange(done, BLOCK), mine, kept


def finish_kernel(mine_ref, total_ref, matrix_ref, projected_ref, contracted_ref):
    lane = lax.broadcasted_iota(jnp.int32, (8, 128), 1)
    row_re = jnp.broadcast_to(matrix_ref[0:1], (8, 128))
    row_im = jnp.broadcast_to(matrix_ref[1:2], (8, 128))
    pick = lane == mine_ref[0]
    own, by_re, by_im = (jnp.zeros((8, 128), F32) for _ in range(3))
    for pair in range(6):
        both = total_ref[pair].astype(F32)
        for which in range(2):
            value = both[8 * which : 8 * which + 8]
            here = lane == 2 * pair + which
            own = jnp.where(here, jnp.sum(jnp.where(pick, value, 0.0), 1, keepdims=True), own)
            by_re = jnp.where(here, jnp.sum(value * row_re, 1, keepdims=True), by_re)
            by_im = jnp.where(here, jnp.sum(value * row_im, 1, keepdims=True), by_im)
    crossed = pltpu.roll(by_im, 4, 0)
    upper = lax.broadcasted_iota(jnp.int32, (8, 128), 0) < 4
    contracted = by_re + jnp.where(upper, -crossed, crossed)
    for row in range(8):
        projected_ref[row] = own[row : row + 1, :12]
        contracted_ref[row] = contracted[row : row + 1, :12]


def placed_out(values):
    return values.reshape(1, 2, 4, 1, 12).transpose(0, 1, 2, 4, 3)


def local(sources, gauge_links, eigenvectors, elementals):
    vectors = eigenvectors[0, :, :, :, 0].transpose(2, 1, 0, 3)
    kept = (elementals[0, :, 0], vectors)
    finals, mine, (matrix, vectors) = spinors(sources, gauge_links, kept)
    partial_value = local_call(
        project_kernel, jax.ShapeDtypeStruct((8, 16, 128), BF16), [], 1 << 25
    )(finals, vectors)
    totals = all_reduce(partial_value)
    shape = jax.ShapeDtypeStruct((8, 1, 12), F32)
    projected, contracted = local_call(
        finish_kernel,
        (shape, shape),
        [],
        1 << 17,
        in_specs=[pl.BlockSpec(memory_space=pltpu.SMEM)] + [pl.BlockSpec()] * 2,
    )(mine, totals, matrix)
    return placed_out(projected), placed_out(contracted)


def solution(mesh):
    fine = Mesh(mesh.devices.reshape(2, 2, 4, 8, 2, 2), (*TM, *SPACE))
    placed = (
        P(TM, None, None, None, None, SPACE, None),
        P(None, TM, None, None, None, SPACE, None),
        P(TM, None, None, None, SPACE, None),
        P(TM, None, SPACE, None),
    )
    result = P(TM, None, None, None, SPACE)
    return jax.shard_map(
        local, mesh=fine, in_specs=placed, out_specs=(result, result), check_vma=False
    )
```

```python
import jax
import jax.numpy as jnp
from jax import lax
from jax.experimental import pallas as pl
from jax.experimental.pallas import tpu as pltpu
from jax.sharding import Mesh
from jax.sharding import PartitionSpec as P

HOPPING = 0.125
TM = ("y_hi", "core")
SPACE = ("x", "z_hi", "z_lo", "y_lo")
PLANE = ("x", "y_lo")
DEPTH = ("z_hi", "z_lo")
POSITION = ("x", *DEPTH)
BLOCK = ("y_lo", *TM)
GROUP = ("z_lo", *BLOCK)
LX = 8
FIELD = 48
LINK = 72
ROWS = FIELD + LINK
SITES = 128
F32 = jnp.float32
BF16 = jnp.bfloat16


def exchange(value, axes):
    return lax.all_to_all(value, axes, 0, 0, tiled=True)


def send(value, axes, steps):
    count = lax.axis_size(axes)
    pairs = [(i, (i + steps[1] if i % 2 else i - steps[0]) % count) for i in range(count)]
    return lax.ppermute(value, axes, pairs)


def local_call(kernel, outs, scratch, flops, **options):
    return pl.pallas_call(
        kernel,
        **options,
        out_shape=outs,
        scratch_shapes=scratch,
        compiler_params=pltpu.CompilerParams(vmem_limit_bytes=16 << 20),
        cost_estimate=pl.CostEstimate(flops=flops, bytes_accessed=1 << 20, transcendentals=0),
    )


def pack_kernel(source_ref, link_ref, out_ref, rows, links):
    for entry in range(36):
        links[2 * entry : 2 * entry + 2] = link_ref[entry].astype(F32)
    shared = links[...]
    for target in range(8):
        rows[target, FIELD:] = shared
    for target in range(8):
        for part in range(2):
            for color in range(3):
                for which in range(2):
                    at = part * 24 + color * 8 + which * 4
                    if target < 6:
                        piece = source_ref[part, color, 2 * target + which].astype(F32)
                    else:
                        piece = jnp.zeros((4, SITES), F32)
                    rows[target, at : at + 4] = piece
    packed = rows[...].astype(BF16)
    out_ref[:8] = packed
    out_ref[8:] = packed


def signed_add(base, sign, value):
    if base is None:
        return value if sign > 0 else -value
    return base + value if sign > 0 else base - value


def block_terms(direction, first, second):
    if direction == 0:
        return (((1, second[1]), (-1, second[0])), ((1, first[1]), (-1, first[0])))
    if direction == 1:
        return (((-1, second[0]), (-1, second[1])), ((1, first[0]), (1, first[1])))
    if direction == 2:
        return (((1, first[1]), (-1, first[0])), ((-1, second[1]), (1, second[0])))
    return (((1, first[0]), (1, first[1])), ((1, second[0]), (1, second[1])))


def half_of(field, direction, sign):
    half = []
    for color in range(3):
        up = [(field(0, color, a), field(1, color, a)) for a in range(4)]
        terms = block_terms(direction, up[2], up[3])
        half.append(
            [
                tuple(
                    signed_add(up[a][part], sign * terms[a][part][0], terms[a][part][1])
                    for part in range(2)
                )
                for a in range(2)
            ]
        )
    return half


def color_apply(link, direction, half, dagger):
    out = []
    for row in range(3):
        acc = [[None, None], [None, None]]
        for col in range(3):
            i, j = (col, row) if dagger else (row, col)
            re, im = link(direction, i, j, 0), link(direction, i, j, 1)
            flip = -1 if dagger else 1
            for a in range(2):
                vec_re, vec_im = half[col][a]
                acc[a][0] = signed_add(acc[a][0], 1, re * vec_re)
                acc[a][0] = signed_add(acc[a][0], -flip, im * vec_im)
                acc[a][1] = signed_add(acc[a][1], 1, re * vec_im)
                acc[a][1] = signed_add(acc[a][1], flip, im * vec_re)
        out.append([tuple(acc[a]) for a in range(2)])
    return out


def shift(value, direction, ahead):
    if direction == 3:
        return pltpu.roll(value, 6 if ahead else 2, 0)
    if direction == 1:
        return pltpu.roll(value, SITES - LX if ahead else LX, 1)
    column = lax.broadcasted_iota(jnp.int32, value.shape, 1) % LX
    if ahead:
        return jnp.where(
            column == LX - 1, pltpu.roll(value, LX - 1, 1), pltpu.roll(value, SITES - 1, 1)
        )
    return jnp.where(column == 0, pltpu.roll(value, SITES - (LX - 1), 1), pltpu.roll(value, 1, 1))


def map_half(function, half):
    return [[tuple(function(v) for v in pair) for pair in spins] for spins in half]


def accumulate(total, direction, ahead, behind):
    for color in range(3):
        both = []
        for a in range(2):
            for part in range(2):
                key = (part, color, a)
                value = ahead[color][a][part] + behind[color][a][part]
                total[key] = value if key not in total else total[key] + value
            both.append(tuple(ahead[color][a][part] - behind[color][a][part] for part in range(2)))
        terms = block_terms(direction, both[0], both[1])
        outer = -1 if direction == 3 else 1
        for a in range(2):
            for part in range(2):
                key = (part, color, a + 2)
                sign, value = terms[a][part]
                total[key] = signed_add(total.get(key), outer * sign, value)


def hop(field, link, ahead_z, behind_z):
    total = {}
    for direction in (0, 1, 3):
        ahead = map_half(
            lambda v, d=direction: shift(v, d, True), half_of(field, direction, -1)
        )
        behind = color_apply(link, direction, half_of(field, direction, 1), True)
        behind = map_half(lambda v, d=direction: shift(v, d, False), behind)
        accumulate(total, direction, color_apply(link, direction, ahead, False), behind)
    accumulate(total, 2, color_apply(link, 2, ahead_z, False), behind_z)
    return total


def comp(part, color, spin):
    return color * 8 + part * 4 + spin


def slot(direction, row, col, part):
    return direction * 18 + row * 6 + col * 2 + part


def field_at(ref, layer):
    return lambda part, color, spin: ref[layer, comp(part, color, spin)]


def link_at(ref, layer):
    return lambda direction, row, col, part: ref[layer, slot(direction, row, col, part)]


def half_slot(part, color, spin):
    return color * 4 + spin * 2 + part


def put_half(ref, half):
    for color in range(3):
        for a in range(2):
            for part in range(2):
                ref[half_slot(part, color, a)] = half[color][a][part].astype(ref.dtype)


def get_half(ref, layer):
    return [
        [tuple(ref[layer, half_slot(part, color, a)] for part in range(2)) for a in range(2)]
        for color in range(3)
    ]


def assemble(wide, start, src, links, layer):
    slices = lax.broadcasted_iota(jnp.int32, (4, SITES), 0)
    turn = jnp.where(slices == 3, -1.0, 1.0)
    for color in range(3):
        for part in range(2):
            for spin in range(4):
                for which in range(2):
                    row = start + part * 24 + color * 8 + which * 4 + spin
                    src[layer, comp(part, color, spin), pl.ds(which, 4, stride=2)] = wide[
                        pl.ds(row, 4, stride=ROWS)
                    ]
    for entry in range(LINK):
        value = wide[pl.ds(start + FIELD + entry, 4, stride=ROWS)]
        if entry >= 54:
            value = value * turn
        for which in range(2):
            links[layer, entry, pl.ds(which, 4, stride=2)] = value


def sent_down(field):
    return half_of(field, 2, -1)


def sent_up(field, link):
    return color_apply(link, 2, half_of(field, 2, 1), True)


def own_kernel(own_ref, base_ref, link_ref, near_ref, far_ref, wide):
    wide[...] = own_ref[...].reshape(16 * ROWS, SITES).astype(F32)
    side = lax.axis_index("z_lo")

    def one(layer, carry):
        assemble(wide, layer * 4 * ROWS, base_ref, link_ref, layer)
        return carry

    lax.fori_loop(0, 4, one, 0)
    near_ref[: 8 * ROWS] = own_ref[pl.ds(side * 8, 8)].reshape(8 * ROWS, SITES)

    def put(ref, start, below, above):
        for color in range(3):
            for a in range(2):
                at = start + 8 * half_slot(0, color, a)
                low = jnp.concatenate(below[color][a], 0)
                high = jnp.concatenate(above[color][a], 0)
                ref[at : at + 16] = jnp.where(side == 0, low, high).astype(BF16)

    def half_down(layer):
        return sent_down(field_at(base_ref, layer))

    def half_up(layer):
        return sent_up(field_at(base_ref, layer), link_at(link_ref, layer))

    put(near_ref, 8 * ROWS, half_down(2), half_up(1))
    put(far_ref, 0, half_down(0), half_up(3))


def sweep_layer(from_ref, src_ref, link_ref, layer, ahead, behind, put):
    total = hop(field_at(from_ref, layer), link_at(link_ref, layer), ahead, behind)
    for key, value in total.items():
        put(comp(*key), src_ref[layer, comp(*key)] + HOPPING * value)


def prepare_layer(from_ref, link_ref, layer, ahead_ref, ahead_at, behind_ref, behind_at):
    put_half(ahead_ref.at[ahead_at], sent_down(field_at(from_ref, layer)))
    put_half(
        behind_ref.at[behind_at], sent_up(field_at(from_ref, layer), link_at(link_ref, layer))
    )


def inner_kernel(
    matrix_ref, vector_ref, base_ref, link_ref,
    kept_matrix, kept_vector, inner_ref, ahead_ref, behind_ref,
):
    kept_matrix[...] = matrix_ref[...]
    kept_vector[...] = vector_ref[...]

    def prepare(layer, carry):
        prepare_layer(base_ref, link_ref, layer, ahead_ref, layer, behind_ref, layer)
        return carry

    def step(layer, carry):
        def put(at, value):
            inner_ref[layer - 1, at] = value

        ahead, behind = get_half(ahead_ref, layer + 1), get_half(behind_ref, layer - 1)
        sweep_layer(base_ref, base_ref, link_ref, layer, ahead, behind, put)
        return carry

    lax.fori_loop(0, 4, prepare, 0)
    lax.fori_loop(1, 3, step, 0)


def sweep_kernel(
    near_ref, far_ref, base_ref, link_ref, inner_ref, ahead_ref, behind_ref, out_ref,
    wide, src, one, two, links, ahead, behind, done,
):
    side = lax.axis_index("z_lo")
    block, halo = 2 - 2 * side, 4 * side
    wide[...] = near_ref[: 8 * ROWS].astype(F32)
    src[pl.ds(block, 4)] = base_ref[...]
    links[pl.ds(block, 4)] = link_ref[...]
    one[pl.ds(block + 1, 2)] = inner_ref[...]
    ahead[pl.ds(block, 4)] = ahead_ref[...]
    behind[pl.ds(block + 1, 4)] = behind_ref[...]
    near = near_ref[8 * ROWS :].astype(F32).reshape(12, 8, SITES)
    far = far_ref[...].astype(F32).reshape(12, 8, SITES)
    ahead[6] = jnp.where(side == 0, far, near)
    behind[0] = jnp.where(side == 0, near, far)

    def gather(at, carry):
        layer = halo + at
        assemble(wide, at * 4 * ROWS, src, links, layer)
        prepare_layer(src, links, layer, ahead, layer, behind, layer + 1)
        return carry

    def first(at, carry):
        layer = at + jnp.where(at >= 3 - 2 * side, 2, 0)

        def put(slot_at, value):
            one[layer, slot_at] = value

        halves = get_half(ahead, layer + 1), get_half(behind, layer)
        sweep_layer(src, src, links, layer, *halves, put)
        return carry

    lax.fori_loop(0, 2, gather, 0)
    lax.fori_loop(0, 4, first, 0)

    def prepare_one(layer, carry):
        prepare_layer(one, links, layer, ahead, layer, behind, layer + 1)
        return carry

    def second(layer, carry):
        def put(at, value):
            two[layer, at] = value

        sweep_layer(one, src, links, layer, get_half(ahead, layer + 1), get_half(behind, layer), put)
        return carry

    lax.fori_loop(0, 6, prepare_one, 0)
    lax.fori_loop(1, 5, second, 0)

    def prepare_two(layer, carry):
        prepare_layer(two, links, layer, ahead, layer, behind, layer + 1)
        return carry

    def third(layer, carry):
        def put(at, value):
            done[pl.ds(pl.multiple_of(((layer - 2) * 24 + at) * 8, 8), 8)] = value

        sweep_layer(two, src, links, layer, get_half(ahead, layer + 1), get_half(behind, layer), put)
        return carry

    lax.fori_loop(1, 5, prepare_two, 0)
    lax.fori_loop(2, 4, third, 0)
    for layer in range(2):
        for time in range(4):
            for color in range(3):
                start = (layer * 24 + color * 8) * 8 + 2 * time
                pair = [done[pl.ds(start + which, 8, stride=8)] for which in range(2)]
                out_ref[layer * 4 + time, color * 16 : color * 16 + 16] = jnp.concatenate(
                    pair, 0
                ).astype(BF16)


def project_kernel(phi_ref, vector_ref, out_ref):
    totals = [None, None]
    for color in range(3):
        rows = phi_ref[:, color * 16 : color * 16 + 16].reshape(8 * 16, SITES)
        for part in range(2):
            value = lax.dot_general(
                rows,
                vector_ref[color, part],
                (((1,), (1,)), ((), ())),
                preferred_element_type=F32,
            )
            totals[part] = value if totals[part] is None else totals[part] + value
    crossed = pltpu.roll(totals[1].reshape(16, 8, 128), 4, 1)
    upper = lax.broadcasted_iota(jnp.int32, crossed.shape, 1) < 4
    mixed = totals[0].reshape(16, 8, 128) + jnp.where(upper, crossed, -crossed)
    out_ref[...] = mixed.reshape(8, 16, 128).astype(BF16)


def spread_kernel(value_ref, out_ref):
    total = value_ref[0].astype(F32)
    for member in range(1, value_ref.shape[0]):
        total = total + value_ref[member].astype(F32)
    total = total.astype(BF16)
    for member in range(out_ref.shape[0]):
        out_ref[member] = total


def summed(value, copies):
    shape = jax.ShapeDtypeStruct((copies, *value.shape[1:]), BF16)
    return local_call(spread_kernel, shape, [], 1 << 16)(value)


def all_reduce(partial_value):
    plane = lax.axis_size(PLANE)
    depth = lax.axis_size(DEPTH)
    copies = summed(exchange(partial_value, PLANE), depth)
    copies = summed(exchange(copies, DEPTH), plane)
    return exchange(copies, PLANE)


def spinors(sources, gauge_links, kept):
    moved = sources[0, :, :, :, :, 0].transpose(0, 2, 3, 1, 4)
    entries = gauge_links[:, 0, :, :, :, 0].transpose(0, 2, 3, 1, 4).reshape(36, 2, SITES)
    packed = local_call(
        pack_kernel,
        jax.ShapeDtypeStruct((16, ROWS, SITES), BF16),
        [
            pltpu.VMEM((8, ROWS, SITES), F32),
            pltpu.VMEM((LINK, SITES), F32),
        ],
        1 << 17,
    )(moved, entries)
    own = exchange(packed, GROUP)
    vectors = (8, SITES)
    base, links, near, far = local_call(
        own_kernel,
        (
            jax.ShapeDtypeStruct((4, 24, *vectors), F32),
            jax.ShapeDtypeStruct((4, LINK, *vectors), F32),
            jax.ShapeDtypeStruct((8 * ROWS + 96, SITES), BF16),
            jax.ShapeDtypeStruct((96, SITES), BF16),
        ),
        [pltpu.VMEM((16 * ROWS, SITES), F32)],
        1 << 20,
    )(own)
    matrix, spectrum = kept
    matrix, spectrum, inner, ahead, behind = local_call(
        inner_kernel,
        (
            jax.ShapeDtypeStruct(matrix.shape, F32),
            jax.ShapeDtypeStruct(spectrum.shape, BF16),
            jax.ShapeDtypeStruct((2, 24, *vectors), F32),
            jax.ShapeDtypeStruct((4, 12, *vectors), F32),
            jax.ShapeDtypeStruct((4, 12, *vectors), F32),
        ),
        [],
        1 << 22,
    )(matrix, spectrum, base, links)
    near = send(near, POSITION, (1, 1))
    far = send(far, POSITION, (2, 2))
    done = local_call(
        sweep_kernel,
        jax.ShapeDtypeStruct((8, FIELD, SITES), BF16),
        [
            pltpu.VMEM((8 * ROWS, SITES), F32),
            pltpu.VMEM((6, 24, *vectors), F32),
            pltpu.VMEM((6, 24, *vectors), F32),
            pltpu.VMEM((6, 24, *vectors), F32),
            pltpu.VMEM((6, LINK, *vectors), F32),
            pltpu.VMEM((7, 12, *vectors), F32),
            pltpu.VMEM((7, 12, *vectors), F32),
            pltpu.VMEM((2 * 24 * 8, SITES), F32),
        ],
        1 << 24,
    )(near, far, base, links, inner, ahead, behind)
    return exchange(done, BLOCK), matrix, spectrum


def finish_kernel(total_ref, matrix_ref, projected_ref, contracted_ref):
    lane = lax.broadcasted_iota(jnp.int32, (8, 128), 1)
    row_re = jnp.broadcast_to(matrix_ref[0:1], (8, 128))
    row_im = jnp.broadcast_to(matrix_ref[1:2], (8, 128))
    pick = lane == lax.axis_index(SPACE)
    own, by_re, by_im = (jnp.zeros((8, 128), F32) for _ in range(3))
    for pair in range(6):
        both = total_ref[pair].astype(F32)
        for which in range(2):
            value = both[8 * which : 8 * which + 8]
            here = lane == 2 * pair + which
            own = jnp.where(here, jnp.sum(jnp.where(pick, value, 0.0), 1, keepdims=True), own)
            by_re = jnp.where(here, jnp.sum(value * row_re, 1, keepdims=True), by_re)
            by_im = jnp.where(here, jnp.sum(value * row_im, 1, keepdims=True), by_im)
    crossed = pltpu.roll(by_im, 4, 0)
    upper = lax.broadcasted_iota(jnp.int32, (8, 128), 0) < 4
    contracted = by_re + jnp.where(upper, -crossed, crossed)
    for row in range(8):
        projected_ref[row] = own[row : row + 1, :12]
        contracted_ref[row] = contracted[row : row + 1, :12]


def placed_out(values):
    return values.reshape(1, 2, 4, 1, 12).transpose(0, 1, 2, 4, 3)


def local(sources, gauge_links, eigenvectors, elementals):
    vectors = eigenvectors[0, :, :, :, 0].transpose(2, 1, 0, 3)
    kept = (elementals[0, :, 0], vectors)
    finals, matrix, vectors = spinors(sources, gauge_links, kept)
    partial_value = local_call(
        project_kernel, jax.ShapeDtypeStruct((8, 16, 128), BF16), [], 1 << 25
    )(finals, vectors)
    totals = all_reduce(partial_value)
    shape = jax.ShapeDtypeStruct((8, 1, 12), F32)
    projected, contracted = local_call(
        finish_kernel,
        (shape, shape),
        [],
        1 << 17,
    )(totals, matrix)
    return placed_out(projected), placed_out(contracted)


def solution(mesh):
    fine = Mesh(mesh.devices.reshape(2, 2, 4, 8, 2, 2), (*TM, *SPACE))
    placed = (
        P(TM, None, None, None, None, SPACE, None),
        P(None, TM, None, None, None, SPACE, None),
        P(TM, None, None, None, SPACE, None),
        P(TM, None, SPACE, None),
    )
    result = P(TM, None, None, None, SPACE)
    return jax.shard_map(
        local, mesh=fine, in_specs=placed, out_specs=(result, result), check_vma=False
    )
```

```python
import jax
import jax.numpy as jnp
from jax import lax
from jax.experimental import pallas as pl
from jax.experimental.pallas import tpu as pltpu
from jax.sharding import Mesh
from jax.sharding import PartitionSpec as P

HOPPING = 0.125
TM = ("y_hi", "core")
SPACE = ("x", "z_hi", "z_lo", "y_lo")
PLANE = ("x", "y_lo")
DEPTH = ("z_hi", "z_lo")
POSITION = ("x", *DEPTH)
BLOCK = ("y_lo", *TM)
GROUP = ("z_lo", *BLOCK)
LX = 8
FIELD = 48
LINK = 72
ROWS = FIELD + LINK
SITES = 128
F32 = jnp.float32
BF16 = jnp.bfloat16


def exchange(value, axes):
    return lax.all_to_all(value, axes, 0, 0, tiled=True)


def send(value, axes, steps):
    count = lax.axis_size(axes)
    pairs = [(i, (i + steps[1] if i % 2 else i - steps[0]) % count) for i in range(count)]
    return lax.ppermute(value, axes, pairs)


def local_call(kernel, outs, scratch, flops, **options):
    return pl.pallas_call(
        kernel,
        **options,
        out_shape=outs,
        scratch_shapes=scratch,
        compiler_params=pltpu.CompilerParams(vmem_limit_bytes=16 << 20),
        cost_estimate=pl.CostEstimate(flops=flops, bytes_accessed=1 << 20, transcendentals=0),
    )


def pack_kernel(source_ref, link_ref, out_ref, rows, links):
    for entry in range(36):
        links[2 * entry : 2 * entry + 2] = link_ref[entry].astype(F32)
    shared = links[...]
    for target in range(8):
        rows[target, FIELD:] = shared
    for target in range(8):
        for part in range(2):
            for color in range(3):
                for which in range(2):
                    at = part * 24 + color * 8 + which * 4
                    if target < 6:
                        piece = source_ref[part, color, 2 * target + which].astype(F32)
                    else:
                        piece = jnp.zeros((4, SITES), F32)
                    rows[target, at : at + 4] = piece
    packed = rows[...].astype(BF16)
    out_ref[:8] = packed
    out_ref[8:] = packed


def signed_add(base, sign, value):
    if base is None:
        return value if sign > 0 else -value
    return base + value if sign > 0 else base - value


def block_terms(direction, first, second):
    if direction == 0:
        return (((1, second[1]), (-1, second[0])), ((1, first[1]), (-1, first[0])))
    if direction == 1:
        return (((-1, second[0]), (-1, second[1])), ((1, first[0]), (1, first[1])))
    if direction == 2:
        return (((1, first[1]), (-1, first[0])), ((-1, second[1]), (1, second[0])))
    return (((1, first[0]), (1, first[1])), ((1, second[0]), (1, second[1])))


def half_of(field, direction, sign):
    half = []
    for color in range(3):
        up = [(field(0, color, a), field(1, color, a)) for a in range(4)]
        terms = block_terms(direction, up[2], up[3])
        half.append(
            [
                tuple(
                    signed_add(up[a][part], sign * terms[a][part][0], terms[a][part][1])
                    for part in range(2)
                )
                for a in range(2)
            ]
        )
    return half


def color_apply(link, direction, half, dagger):
    out = []
    for row in range(3):
        acc = [[None, None], [None, None]]
        for col in range(3):
            i, j = (col, row) if dagger else (row, col)
            re, im = link(direction, i, j, 0), link(direction, i, j, 1)
            flip = -1 if dagger else 1
            for a in range(2):
                vec_re, vec_im = half[col][a]
                acc[a][0] = signed_add(acc[a][0], 1, re * vec_re)
                acc[a][0] = signed_add(acc[a][0], -flip, im * vec_im)
                acc[a][1] = signed_add(acc[a][1], 1, re * vec_im)
                acc[a][1] = signed_add(acc[a][1], flip, im * vec_re)
        out.append([tuple(acc[a]) for a in range(2)])
    return out


def shift(value, direction, ahead):
    if direction == 3:
        return pltpu.roll(value, 6 if ahead else 2, 0)
    if direction == 1:
        return pltpu.roll(value, SITES - LX if ahead else LX, 1)
    column = lax.broadcasted_iota(jnp.int32, value.shape, 1) % LX
    if ahead:
        return jnp.where(
            column == LX - 1, pltpu.roll(value, LX - 1, 1), pltpu.roll(value, SITES - 1, 1)
        )
    return jnp.where(column == 0, pltpu.roll(value, SITES - (LX - 1), 1), pltpu.roll(value, 1, 1))


def map_half(function, half):
    return [[tuple(function(v) for v in pair) for pair in spins] for spins in half]


def accumulate(total, direction, ahead, behind):
    for color in range(3):
        both = []
        for a in range(2):
            for part in range(2):
                key = (part, color, a)
                value = ahead[color][a][part] + behind[color][a][part]
                total[key] = value if key not in total else total[key] + value
            both.append(tuple(ahead[color][a][part] - behind[color][a][part] for part in range(2)))
        terms = block_terms(direction, both[0], both[1])
        outer = -1 if direction == 3 else 1
        for a in range(2):
            for part in range(2):
                key = (part, color, a + 2)
                sign, value = terms[a][part]
                total[key] = signed_add(total.get(key), outer * sign, value)


def hop(field, link, ahead_z, behind_z):
    total = {}
    for direction in (0, 1, 3):
        ahead = map_half(
            lambda v, d=direction: shift(v, d, True), half_of(field, direction, -1)
        )
        behind = color_apply(link, direction, half_of(field, direction, 1), True)
        behind = map_half(lambda v, d=direction: shift(v, d, False), behind)
        accumulate(total, direction, color_apply(link, direction, ahead, False), behind)
    accumulate(total, 2, color_apply(link, 2, ahead_z, False), behind_z)
    return total


def comp(part, color, spin):
    return color * 8 + part * 4 + spin


def slot(direction, row, col, part):
    return direction * 18 + row * 6 + col * 2 + part


def field_at(ref, layer):
    return lambda part, color, spin: ref[layer, comp(part, color, spin)]


def link_at(ref, layer):
    return lambda direction, row, col, part: ref[layer, slot(direction, row, col, part)]


def half_slot(part, color, spin):
    return color * 4 + spin * 2 + part


def put_half(ref, half):
    for color in range(3):
        for a in range(2):
            for part in range(2):
                ref[half_slot(part, color, a)] = half[color][a][part].astype(ref.dtype)


def get_half(ref, layer):
    return [
        [tuple(ref[layer, half_slot(part, color, a)] for part in range(2)) for a in range(2)]
        for color in range(3)
    ]


def assemble(wide, start, src, links, layer):
    slices = lax.broadcasted_iota(jnp.int32, (4, SITES), 0)
    turn = jnp.where(slices == 3, -1.0, 1.0)
    for color in range(3):
        for part in range(2):
            for spin in range(4):
                for which in range(2):
                    row = start + part * 24 + color * 8 + which * 4 + spin
                    src[layer, comp(part, color, spin), pl.ds(which, 4, stride=2)] = wide[
                        pl.ds(row, 4, stride=ROWS)
                    ]
    for entry in range(LINK):
        value = wide[pl.ds(start + FIELD + entry, 4, stride=ROWS)]
        if entry >= 54:
            value = value * turn
        for which in range(2):
            links[layer, entry, pl.ds(which, 4, stride=2)] = value


def sent_down(field):
    return half_of(field, 2, -1)


def sent_up(field, link):
    return color_apply(link, 2, half_of(field, 2, 1), True)


def own_kernel(own_ref, base_ref, link_ref, near_ref, far_ref, wide, next_ref):
    wide[...] = own_ref[...].reshape(16 * ROWS, SITES).astype(F32)
    side = lax.axis_index("z_lo")

    def one(layer, carry):
        assemble(wide, layer * 4 * ROWS, base_ref, link_ref, layer)
        return carry

    lax.fori_loop(0, 4, one, 0)
    near_ref[: 4 * ROWS] = own_ref[pl.ds(side * 12, 4)].reshape(4 * ROWS, SITES)

    def put(ref, start, below, above):
        for color in range(3):
            for a in range(2):
                at = start + 8 * half_slot(0, color, a)
                low = jnp.concatenate(below[color][a], 0)
                high = jnp.concatenate(above[color][a], 0)
                ref[at : at + 16] = jnp.where(side == 0, low, high).astype(BF16)

    def half_down(layer):
        return sent_down(field_at(base_ref, layer))

    def half_up(layer):
        return sent_up(field_at(base_ref, layer), link_at(link_ref, layer))

    put(far_ref, 0, half_down(0), half_up(3))
    put(near_ref, 4 * ROWS, half_down(1), half_up(2))
    second = 1 + side

    def keep(at, value):
        next_ref[at] = value

    sweep_layer(base_ref, base_ref, link_ref, second, half_down(second + 1), half_up(second - 1), keep)

    def field(part, color, spin):
        return next_ref[comp(part, color, spin)]

    put(near_ref, 4 * ROWS + 96, sent_down(field), sent_up(field, link_at(link_ref, second)))


def sweep_layer(from_ref, src_ref, link_ref, layer, ahead, behind, put):
    total = hop(field_at(from_ref, layer), link_at(link_ref, layer), ahead, behind)
    for key, value in total.items():
        put(comp(*key), src_ref[layer, comp(*key)] + HOPPING * value)


def prepare_layer(from_ref, link_ref, layer, ahead_ref, ahead_at, behind_ref, behind_at):
    put_half(ahead_ref.at[ahead_at], sent_down(field_at(from_ref, layer)))
    put_half(
        behind_ref.at[behind_at], sent_up(field_at(from_ref, layer), link_at(link_ref, layer))
    )


def inner_kernel(
    matrix_ref, vector_ref, base_ref, link_ref,
    kept_matrix, kept_vector, inner_ref, ahead_ref, behind_ref,
):
    kept_matrix[...] = matrix_ref[...]
    kept_vector[...] = vector_ref[...]

    def prepare(layer, carry):
        prepare_layer(base_ref, link_ref, layer, ahead_ref, layer, behind_ref, layer)
        return carry

    def step(layer, carry):
        def put(at, value):
            inner_ref[layer - 1, at] = value

        ahead, behind = get_half(ahead_ref, layer + 1), get_half(behind_ref, layer - 1)
        sweep_layer(base_ref, base_ref, link_ref, layer, ahead, behind, put)
        return carry

    lax.fori_loop(0, 4, prepare, 0)
    lax.fori_loop(1, 3, step, 0)


def sweep_kernel(
    near_ref, far_ref, base_ref, link_ref, inner_ref, ahead_ref, behind_ref, out_ref,
    wide, src, one, two, links, ahead, behind, done,
):
    side = lax.axis_index("z_lo")
    block, halo = 2 - 2 * side, 1 + 3 * side
    wide[...] = near_ref[: 4 * ROWS].astype(F32)
    src[pl.ds(block, 4)] = base_ref[...]
    links[pl.ds(block, 4)] = link_ref[...]
    one[pl.ds(block + 1, 2)] = inner_ref[...]
    ahead[pl.ds(block, 4)] = ahead_ref[...]
    behind[pl.ds(block + 1, 4)] = behind_ref[...]
    near = near_ref[4 * ROWS : 4 * ROWS + 96].astype(F32).reshape(12, 8, SITES)
    far = far_ref[...].astype(F32).reshape(12, 8, SITES)
    ahead[6 - side] = jnp.where(side == 0, far, near)
    behind[1 - side] = jnp.where(side == 0, near, far)
    assemble(wide, 0, src, links, halo)
    prepare_layer(src, links, halo, ahead, halo, behind, halo + 1)

    def first(at, carry):
        layer = at + 1 - side + jnp.where(at >= 2 - side, 2, 0)

        def put(slot_at, value):
            one[layer, slot_at] = value

        halves = get_half(ahead, layer + 1), get_half(behind, layer)
        sweep_layer(src, src, links, layer, *halves, put)
        return carry

    lax.fori_loop(0, 3, first, 0)

    def prepare(from_ref, layer):
        put_half(ahead.at[layer + 2], sent_down(field_at(from_ref, layer + 2)))
        put_half(behind.at[layer + 1], sent_up(field_at(from_ref, layer), link_at(links, layer)))

    def prepare_one(layer, carry):
        prepare(one, layer)
        return carry

    def second(layer, carry):
        def put(at, value):
            two[layer, at] = value

        sweep_layer(one, src, links, layer, get_half(ahead, layer + 1), get_half(behind, layer), put)
        return carry

    lax.fori_loop(0, 4, prepare_one, 0)
    near = near_ref[4 * ROWS + 96 :].astype(F32).reshape(12, 8, SITES)

    @pl.when(side == 0)
    def _():
        behind[1] = near

    @pl.when(side == 1)
    def _():
        ahead[5] = near

    lax.fori_loop(1, 5, second, 0)

    def prepare_two(layer, carry):
        prepare(two, layer)
        return carry

    def third(layer, carry):
        def put(at, value):
            done[pl.ds(pl.multiple_of(((layer - 2) * 24 + at) * 8, 8), 8)] = value

        sweep_layer(two, src, links, layer, get_half(ahead, layer + 1), get_half(behind, layer), put)
        return carry

    lax.fori_loop(1, 3, prepare_two, 0)
    lax.fori_loop(2, 4, third, 0)
    for layer in range(2):
        for time in range(4):
            for color in range(3):
                start = (layer * 24 + color * 8) * 8 + 2 * time
                pair = [done[pl.ds(start + which, 8, stride=8)] for which in range(2)]
                out_ref[layer * 4 + time, color * 16 : color * 16 + 16] = jnp.concatenate(
                    pair, 0
                ).astype(BF16)


def project_kernel(phi_ref, vector_ref, out_ref):
    totals = [None, None]
    for color in range(3):
        rows = phi_ref[:, color * 16 : color * 16 + 16].reshape(8 * 16, SITES)
        for part in range(2):
            value = lax.dot_general(
                rows,
                vector_ref[color, part],
                (((1,), (1,)), ((), ())),
                preferred_element_type=F32,
            )
            totals[part] = value if totals[part] is None else totals[part] + value
    crossed = pltpu.roll(totals[1].reshape(16, 8, 128), 4, 1)
    upper = lax.broadcasted_iota(jnp.int32, crossed.shape, 1) < 4
    mixed = totals[0].reshape(16, 8, 128) + jnp.where(upper, crossed, -crossed)
    out_ref[...] = mixed.reshape(8, 16, 128).astype(BF16)


def spread_kernel(value_ref, out_ref):
    total = value_ref[0].astype(F32)
    for member in range(1, value_ref.shape[0]):
        total = total + value_ref[member].astype(F32)
    total = total.astype(BF16)
    for member in range(out_ref.shape[0]):
        out_ref[member] = total


def summed(value, copies):
    shape = jax.ShapeDtypeStruct((copies, *value.shape[1:]), BF16)
    return local_call(spread_kernel, shape, [], 1 << 16)(value)


def all_reduce(partial_value):
    plane = lax.axis_size(PLANE)
    depth = lax.axis_size(DEPTH)
    copies = summed(exchange(partial_value, PLANE), depth)
    copies = summed(exchange(copies, DEPTH), plane)
    return exchange(copies, PLANE)


def spinors(sources, gauge_links, kept):
    moved = sources[0, :, :, :, :, 0].transpose(0, 2, 3, 1, 4)
    entries = gauge_links[:, 0, :, :, :, 0].transpose(0, 2, 3, 1, 4).reshape(36, 2, SITES)
    packed = local_call(
        pack_kernel,
        jax.ShapeDtypeStruct((16, ROWS, SITES), BF16),
        [
            pltpu.VMEM((8, ROWS, SITES), F32),
            pltpu.VMEM((LINK, SITES), F32),
        ],
        1 << 17,
    )(moved, entries)
    own = exchange(packed, GROUP)
    vectors = (8, SITES)
    base, links, near, far = local_call(
        own_kernel,
        (
            jax.ShapeDtypeStruct((4, 24, *vectors), F32),
            jax.ShapeDtypeStruct((4, LINK, *vectors), F32),
            jax.ShapeDtypeStruct((4 * ROWS + 192, SITES), BF16),
            jax.ShapeDtypeStruct((96, SITES), BF16),
        ),
        [pltpu.VMEM((16 * ROWS, SITES), F32), pltpu.VMEM((24, *vectors), F32)],
        1 << 20,
    )(own)
    matrix, spectrum = kept
    matrix, spectrum, inner, ahead, behind = local_call(
        inner_kernel,
        (
            jax.ShapeDtypeStruct(matrix.shape, F32),
            jax.ShapeDtypeStruct(spectrum.shape, BF16),
            jax.ShapeDtypeStruct((2, 24, *vectors), F32),
            jax.ShapeDtypeStruct((4, 12, *vectors), F32),
            jax.ShapeDtypeStruct((4, 12, *vectors), F32),
        ),
        [],
        1 << 22,
    )(matrix, spectrum, base, links)
    near = send(near, POSITION, (1, 1))
    far = send(far, POSITION, (2, 2))
    done = local_call(
        sweep_kernel,
        jax.ShapeDtypeStruct((8, FIELD, SITES), BF16),
        [
            pltpu.VMEM((4 * ROWS, SITES), F32),
            pltpu.VMEM((6, 24, *vectors), F32),
            pltpu.VMEM((6, 24, *vectors), F32),
            pltpu.VMEM((6, 24, *vectors), F32),
            pltpu.VMEM((6, LINK, *vectors), F32),
            pltpu.VMEM((7, 12, *vectors), F32),
            pltpu.VMEM((7, 12, *vectors), F32),
            pltpu.VMEM((2 * 24 * 8, SITES), F32),
        ],
        1 << 24,
    )(near, far, base, links, inner, ahead, behind)
    return exchange(done, BLOCK), matrix, spectrum


def finish_kernel(total_ref, matrix_ref, projected_ref, contracted_ref):
    lane = lax.broadcasted_iota(jnp.int32, (8, 128), 1)
    row_re = jnp.broadcast_to(matrix_ref[0:1], (8, 128))
    row_im = jnp.broadcast_to(matrix_ref[1:2], (8, 128))
    pick = lane == lax.axis_index(SPACE)
    own, by_re, by_im = (jnp.zeros((8, 128), F32) for _ in range(3))
    for pair in range(6):
        both = total_ref[pair].astype(F32)
        for which in range(2):
            value = both[8 * which : 8 * which + 8]
            here = lane == 2 * pair + which
            own = jnp.where(here, jnp.sum(jnp.where(pick, value, 0.0), 1, keepdims=True), own)
            by_re = jnp.where(here, jnp.sum(value * row_re, 1, keepdims=True), by_re)
            by_im = jnp.where(here, jnp.sum(value * row_im, 1, keepdims=True), by_im)
    crossed = pltpu.roll(by_im, 4, 0)
    upper = lax.broadcasted_iota(jnp.int32, (8, 128), 0) < 4
    contracted = by_re + jnp.where(upper, -crossed, crossed)
    for row in range(8):
        projected_ref[row] = own[row : row + 1, :12]
        contracted_ref[row] = contracted[row : row + 1, :12]


def placed_out(values):
    return values.reshape(1, 2, 4, 1, 12).transpose(0, 1, 2, 4, 3)


def local(sources, gauge_links, eigenvectors, elementals):
    vectors = eigenvectors[0, :, :, :, 0].transpose(2, 1, 0, 3)
    kept = (elementals[0, :, 0], vectors)
    finals, matrix, vectors = spinors(sources, gauge_links, kept)
    partial_value = local_call(
        project_kernel, jax.ShapeDtypeStruct((8, 16, 128), BF16), [], 1 << 25
    )(finals, vectors)
    totals = all_reduce(partial_value)
    shape = jax.ShapeDtypeStruct((8, 1, 12), F32)
    projected, contracted = local_call(
        finish_kernel,
        (shape, shape),
        [],
        1 << 17,
    )(totals, matrix)
    return placed_out(projected), placed_out(contracted)


def solution(mesh):
    fine = Mesh(mesh.devices.reshape(2, 2, 4, 8, 2, 2), (*TM, *SPACE))
    placed = (
        P(TM, None, None, None, None, SPACE, None),
        P(None, TM, None, None, None, SPACE, None),
        P(TM, None, None, None, SPACE, None),
        P(TM, None, SPACE, None),
    )
    result = P(TM, None, None, None, SPACE)
    return jax.shard_map(
        local, mesh=fine, in_specs=placed, out_specs=(result, result), check_vma=False
    )
```

```python
import jax
import jax.numpy as jnp
from jax import lax
from jax.experimental import pallas as pl
from jax.experimental.pallas import tpu as pltpu
from jax.sharding import Mesh
from jax.sharding import PartitionSpec as P

HOPPING = 0.125
TM = ("y_hi", "core")
SPACE = ("x", "z_hi", "z_lo", "y_lo")
PLANE = ("x", "y_lo")
DEPTH = ("z_hi", "z_lo")
POSITION = ("x", *DEPTH)
BLOCK = ("y_lo", *TM)
GROUP = ("z_lo", *BLOCK)
LX = 8
FIELD = 48
LINK = 72
ROWS = FIELD + LINK
SITES = 128
F32 = jnp.float32
BF16 = jnp.bfloat16


def exchange(value, axes):
    return lax.all_to_all(value, axes, 0, 0, tiled=True)


def send(value, axes, steps):
    count = lax.axis_size(axes)
    pairs = [(i, (i + steps[1] if i % 2 else i - steps[0]) % count) for i in range(count)]
    return lax.ppermute(value, axes, pairs)


def local_call(kernel, outs, scratch, flops, **options):
    return pl.pallas_call(
        kernel,
        **options,
        out_shape=outs,
        scratch_shapes=scratch,
        compiler_params=pltpu.CompilerParams(vmem_limit_bytes=16 << 20),
        cost_estimate=pl.CostEstimate(flops=flops, bytes_accessed=1 << 20, transcendentals=0),
    )


def clear_kernel(out_ref):
    out_ref[...] = jnp.zeros(out_ref.shape, F32)


def pack_kernel(clear_ref, source_ref, link_ref, out_ref, rows, links):
    for entry in range(36):
        links[2 * entry : 2 * entry + 2] = link_ref[entry].astype(F32)
    shared = links[...]
    for target in range(8):
        rows[target, FIELD:] = shared
    for target in range(8):
        for part in range(2):
            for color in range(3):
                for which in range(2):
                    at = part * 24 + color * 8 + which * 4
                    if target < 6:
                        piece = source_ref[part, color, 2 * target + which].astype(F32)
                    else:
                        piece = clear_ref[:4]
                    rows[target, at : at + 4] = piece
    packed = rows[...].astype(BF16)
    out_ref[:8] = packed
    out_ref[8:] = packed


def signed_add(base, sign, value):
    if base is None:
        return value if sign > 0 else -value
    return base + value if sign > 0 else base - value


def block_terms(direction, first, second):
    if direction == 0:
        return (((1, second[1]), (-1, second[0])), ((1, first[1]), (-1, first[0])))
    if direction == 1:
        return (((-1, second[0]), (-1, second[1])), ((1, first[0]), (1, first[1])))
    if direction == 2:
        return (((1, first[1]), (-1, first[0])), ((-1, second[1]), (1, second[0])))
    return (((1, first[0]), (1, first[1])), ((1, second[0]), (1, second[1])))


def half_of(field, direction, sign):
    half = []
    for color in range(3):
        up = [(field(0, color, a), field(1, color, a)) for a in range(4)]
        terms = block_terms(direction, up[2], up[3])
        half.append(
            [
                tuple(
                    signed_add(up[a][part], sign * terms[a][part][0], terms[a][part][1])
                    for part in range(2)
                )
                for a in range(2)
            ]
        )
    return half


def color_apply(link, direction, half, dagger):
    out = []
    for row in range(3):
        acc = [[None, None], [None, None]]
        for col in range(3):
            i, j = (col, row) if dagger else (row, col)
            re, im = link(direction, i, j, 0), link(direction, i, j, 1)
            flip = -1 if dagger else 1
            for a in range(2):
                vec_re, vec_im = half[col][a]
                acc[a][0] = signed_add(acc[a][0], 1, re * vec_re)
                acc[a][0] = signed_add(acc[a][0], -flip, im * vec_im)
                acc[a][1] = signed_add(acc[a][1], 1, re * vec_im)
                acc[a][1] = signed_add(acc[a][1], flip, im * vec_re)
        out.append([tuple(acc[a]) for a in range(2)])
    return out


def shift(value, direction, ahead):
    if direction == 3:
        return pltpu.roll(value, 6 if ahead else 2, 0)
    if direction == 1:
        return pltpu.roll(value, SITES - LX if ahead else LX, 1)
    column = lax.broadcasted_iota(jnp.int32, value.shape, 1) % LX
    if ahead:
        return jnp.where(
            column == LX - 1, pltpu.roll(value, LX - 1, 1), pltpu.roll(value, SITES - 1, 1)
        )
    return jnp.where(column == 0, pltpu.roll(value, SITES - (LX - 1), 1), pltpu.roll(value, 1, 1))


def map_half(function, half):
    return [[tuple(function(v) for v in pair) for pair in spins] for spins in half]


def accumulate(total, direction, ahead, behind):
    for color in range(3):
        both = []
        for a in range(2):
            for part in range(2):
                key = (part, color, a)
                value = ahead[color][a][part] + behind[color][a][part]
                total[key] = value if key not in total else total[key] + value
            both.append(tuple(ahead[color][a][part] - behind[color][a][part] for part in range(2)))
        terms = block_terms(direction, both[0], both[1])
        outer = -1 if direction == 3 else 1
        for a in range(2):
            for part in range(2):
                key = (part, color, a + 2)
                sign, value = terms[a][part]
                total[key] = signed_add(total.get(key), outer * sign, value)


def hop(field, link, ahead_z, behind_z):
    total = {}
    for direction in (0, 1, 3):
        ahead = map_half(
            lambda v, d=direction: shift(v, d, True), half_of(field, direction, -1)
        )
        behind = color_apply(link, direction, half_of(field, direction, 1), True)
        behind = map_half(lambda v, d=direction: shift(v, d, False), behind)
        accumulate(total, direction, color_apply(link, direction, ahead, False), behind)
    accumulate(total, 2, color_apply(link, 2, ahead_z, False), behind_z)
    return total


def comp(part, color, spin):
    return color * 8 + part * 4 + spin


def slot(direction, row, col, part):
    return direction * 18 + row * 6 + col * 2 + part


def field_at(ref, layer):
    return lambda part, color, spin: ref[layer, comp(part, color, spin)]


def link_at(ref, layer):
    return lambda direction, row, col, part: ref[layer, slot(direction, row, col, part)]


def half_slot(part, color, spin):
    return color * 4 + spin * 2 + part


def put_half(ref, half):
    for color in range(3):
        for a in range(2):
            for part in range(2):
                ref[half_slot(part, color, a)] = half[color][a][part].astype(ref.dtype)


def get_half(ref, layer):
    return [
        [tuple(ref[layer, half_slot(part, color, a)] for part in range(2)) for a in range(2)]
        for color in range(3)
    ]


def assemble(wide, start, src, links, layer):
    slices = lax.broadcasted_iota(jnp.int32, (4, SITES), 0)
    turn = jnp.where(slices == 3, -1.0, 1.0)
    for color in range(3):
        for part in range(2):
            for spin in range(4):
                for which in range(2):
                    row = start + part * 24 + color * 8 + which * 4 + spin
                    src[layer, comp(part, color, spin), pl.ds(which, 4, stride=2)] = wide[
                        pl.ds(row, 4, stride=ROWS)
                    ]
    for entry in range(LINK):
        value = wide[pl.ds(start + FIELD + entry, 4, stride=ROWS)]
        if entry >= 54:
            value = value * turn
        for which in range(2):
            links[layer, entry, pl.ds(which, 4, stride=2)] = value


def sent_down(field):
    return half_of(field, 2, -1)


def sent_up(field, link):
    return color_apply(link, 2, half_of(field, 2, 1), True)


def own_kernel(own_ref, base_ref, link_ref, near_ref, far_ref, wide, next_ref):
    wide[...] = own_ref[...].reshape(16 * ROWS, SITES).astype(F32)
    side = lax.axis_index("z_lo")

    def one(layer, carry):
        assemble(wide, layer * 4 * ROWS, base_ref, link_ref, layer)
        return carry

    lax.fori_loop(0, 4, one, 0)
    near_ref[: 4 * ROWS] = own_ref[pl.ds(side * 12, 4)].reshape(4 * ROWS, SITES)

    def put(ref, start, below, above):
        for color in range(3):
            for a in range(2):
                at = start + 8 * half_slot(0, color, a)
                low = jnp.concatenate(below[color][a], 0)
                high = jnp.concatenate(above[color][a], 0)
                ref[at : at + 16] = jnp.where(side == 0, low, high).astype(BF16)

    def half_down(layer):
        return sent_down(field_at(base_ref, layer))

    def half_up(layer):
        return sent_up(field_at(base_ref, layer), link_at(link_ref, layer))

    put(far_ref, 0, half_down(0), half_up(3))
    put(near_ref, 4 * ROWS, half_down(1), half_up(2))
    second = 1 + side

    def keep(at, value):
        next_ref[at] = value

    sweep_layer(base_ref, base_ref, link_ref, second, half_down(second + 1), half_up(second - 1), keep)

    def field(part, color, spin):
        return next_ref[comp(part, color, spin)]

    put(near_ref, 4 * ROWS + 96, sent_down(field), sent_up(field, link_at(link_ref, second)))


def sweep_layer(from_ref, src_ref, link_ref, layer, ahead, behind, put):
    total = hop(field_at(from_ref, layer), link_at(link_ref, layer), ahead, behind)
    for key, value in total.items():
        put(comp(*key), src_ref[layer, comp(*key)] + HOPPING * value)


def prepare_layer(from_ref, link_ref, layer, ahead_ref, ahead_at, behind_ref, behind_at):
    put_half(ahead_ref.at[ahead_at], sent_down(field_at(from_ref, layer)))
    put_half(
        behind_ref.at[behind_at], sent_up(field_at(from_ref, layer), link_at(link_ref, layer))
    )


def inner_kernel(
    matrix_ref, vector_ref, base_ref, link_ref,
    kept_matrix, kept_vector, inner_ref, ahead_ref, behind_ref,
):
    kept_matrix[...] = matrix_ref[...]
    kept_vector[...] = vector_ref[...]

    def prepare(layer, carry):
        prepare_layer(base_ref, link_ref, layer, ahead_ref, layer, behind_ref, layer)
        return carry

    def step(layer, carry):
        def put(at, value):
            inner_ref[layer - 1, at] = value

        ahead, behind = get_half(ahead_ref, layer + 1), get_half(behind_ref, layer - 1)
        sweep_layer(base_ref, base_ref, link_ref, layer, ahead, behind, put)
        return carry

    lax.fori_loop(0, 4, prepare, 0)
    lax.fori_loop(1, 3, step, 0)


def sweep_kernel(
    near_ref, far_ref, base_ref, link_ref, inner_ref, ahead_ref, behind_ref, out_ref,
    wide, src, one, two, links, ahead, behind, done,
):
    side = lax.axis_index("z_lo")
    block, halo = 2 - 2 * side, 1 + 3 * side
    wide[...] = near_ref[: 4 * ROWS].astype(F32)
    src[pl.ds(block, 4)] = base_ref[...]
    links[pl.ds(block, 4)] = link_ref[...]
    one[pl.ds(block + 1, 2)] = inner_ref[...]
    ahead[pl.ds(block, 4)] = ahead_ref[...]
    behind[pl.ds(block + 1, 4)] = behind_ref[...]
    near = near_ref[4 * ROWS : 4 * ROWS + 96].astype(F32).reshape(12, 8, SITES)
    far = far_ref[...].astype(F32).reshape(12, 8, SITES)
    ahead[6 - side] = jnp.where(side == 0, far, near)
    behind[1 - side] = jnp.where(side == 0, near, far)
    assemble(wide, 0, src, links, halo)
    prepare_layer(src, links, halo, ahead, halo, behind, halo + 1)

    def first(at, carry):
        layer = at + 1 - side + jnp.where(at >= 2 - side, 2, 0)

        def put(slot_at, value):
            one[layer, slot_at] = value

        halves = get_half(ahead, layer + 1), get_half(behind, layer)
        sweep_layer(src, src, links, layer, *halves, put)
        return carry

    lax.fori_loop(0, 3, first, 0)

    def prepare(from_ref, layer):
        put_half(ahead.at[layer + 2], sent_down(field_at(from_ref, layer + 2)))
        put_half(behind.at[layer + 1], sent_up(field_at(from_ref, layer), link_at(links, layer)))

    def prepare_one(layer, carry):
        prepare(one, layer)
        return carry

    def second(layer, carry):
        def put(at, value):
            two[layer, at] = value

        sweep_layer(one, src, links, layer, get_half(ahead, layer + 1), get_half(behind, layer), put)
        return carry

    lax.fori_loop(0, 4, prepare_one, 0)
    near = near_ref[4 * ROWS + 96 :].astype(F32).reshape(12, 8, SITES)

    @pl.when(side == 0)
    def _():
        behind[1] = near

    @pl.when(side == 1)
    def _():
        ahead[5] = near

    lax.fori_loop(1, 5, second, 0)

    def prepare_two(layer, carry):
        prepare(two, layer)
        return carry

    def third(layer, carry):
        def put(at, value):
            done[pl.ds(pl.multiple_of(((layer - 2) * 24 + at) * 8, 8), 8)] = value

        sweep_layer(two, src, links, layer, get_half(ahead, layer + 1), get_half(behind, layer), put)
        return carry

    lax.fori_loop(1, 3, prepare_two, 0)
    lax.fori_loop(2, 4, third, 0)
    for layer in range(2):
        for time in range(4):
            for color in range(3):
                start = (layer * 24 + color * 8) * 8 + 2 * time
                pair = [done[pl.ds(start + which, 8, stride=8)] for which in range(2)]
                out_ref[layer * 4 + time, color * 16 : color * 16 + 16] = jnp.concatenate(
                    pair, 0
                ).astype(BF16)


def project_kernel(phi_ref, vector_ref, out_ref):
    totals = [None, None]
    for color in range(3):
        rows = phi_ref[:, color * 16 : color * 16 + 16].reshape(8 * 16, SITES)
        for part in range(2):
            value = lax.dot_general(
                rows,
                vector_ref[color, part],
                (((1,), (1,)), ((), ())),
                preferred_element_type=F32,
            )
            totals[part] = value if totals[part] is None else totals[part] + value
    crossed = pltpu.roll(totals[1].reshape(16, 8, 128), 4, 1)
    upper = lax.broadcasted_iota(jnp.int32, crossed.shape, 1) < 4
    mixed = totals[0].reshape(16, 8, 128) + jnp.where(upper, crossed, -crossed)
    for source in range(12):
        for part in range(2):
            member, at = divmod(2 * source + part, 3)
            out_ref[member, at] = mixed[source, 4 * part : 4 * part + 4].astype(BF16)


def spread_kernel(value_ref, out_ref):
    total = value_ref[0].astype(F32)
    for member in range(1, value_ref.shape[0]):
        total = total + value_ref[member].astype(F32)
    total = total.astype(BF16)
    for member in range(out_ref.shape[0]):
        out_ref[member] = total


def summed(value, copies):
    shape = jax.ShapeDtypeStruct((copies, *value.shape[1:]), BF16)
    return local_call(spread_kernel, shape, [], 1 << 16)(value)


def all_reduce(partial_value):
    plane = lax.axis_size(PLANE)
    depth = lax.axis_size(DEPTH)
    copies = summed(exchange(partial_value, PLANE), depth)
    copies = summed(exchange(copies, DEPTH), plane)
    return exchange(copies, PLANE)


def spinors(sources, gauge_links, kept):
    moved = sources[0, :, :, :, :, 0].transpose(0, 2, 3, 1, 4)
    entries = gauge_links[:, 0, :, :, :, 0].transpose(0, 2, 3, 1, 4).reshape(36, 2, SITES)
    clear = local_call(clear_kernel, jax.ShapeDtypeStruct((8, SITES), F32), [], 1 << 32)()
    packed = local_call(
        pack_kernel,
        jax.ShapeDtypeStruct((16, ROWS, SITES), BF16),
        [
            pltpu.VMEM((8, ROWS, SITES), F32),
            pltpu.VMEM((LINK, SITES), F32),
        ],
        1 << 17,
    )(clear, moved, entries)
    own = exchange(packed, GROUP)
    vectors = (8, SITES)
    base, links, near, far = local_call(
        own_kernel,
        (
            jax.ShapeDtypeStruct((4, 24, *vectors), F32),
            jax.ShapeDtypeStruct((4, LINK, *vectors), F32),
            jax.ShapeDtypeStruct((4 * ROWS + 192, SITES), BF16),
            jax.ShapeDtypeStruct((96, SITES), BF16),
        ),
        [pltpu.VMEM((16 * ROWS, SITES), F32), pltpu.VMEM((24, *vectors), F32)],
        1 << 20,
    )(own)
    matrix, spectrum = kept
    matrix, spectrum, inner, ahead, behind = local_call(
        inner_kernel,
        (
            jax.ShapeDtypeStruct(matrix.shape, F32),
            jax.ShapeDtypeStruct(spectrum.shape, BF16),
            jax.ShapeDtypeStruct((2, 24, *vectors), F32),
            jax.ShapeDtypeStruct((4, 12, *vectors), F32),
            jax.ShapeDtypeStruct((4, 12, *vectors), F32),
        ),
        [],
        1 << 22,
    )(matrix, spectrum, base, links)
    near = send(near, POSITION, (1, 1))
    far = send(far, POSITION, (2, 2))
    done = local_call(
        sweep_kernel,
        jax.ShapeDtypeStruct((8, FIELD, SITES), BF16),
        [
            pltpu.VMEM((4 * ROWS, SITES), F32),
            pltpu.VMEM((6, 24, *vectors), F32),
            pltpu.VMEM((6, 24, *vectors), F32),
            pltpu.VMEM((6, 24, *vectors), F32),
            pltpu.VMEM((6, LINK, *vectors), F32),
            pltpu.VMEM((7, 12, *vectors), F32),
            pltpu.VMEM((7, 12, *vectors), F32),
            pltpu.VMEM((2 * 24 * 8, SITES), F32),
        ],
        1 << 24,
    )(near, far, base, links, inner, ahead, behind)
    return exchange(done, BLOCK), matrix, spectrum


def finish_kernel(total_ref, matrix_ref, projected_ref, contracted_ref, rows):
    for piece in range(24):
        rows[4 * piece : 4 * piece + 4] = total_ref[piece // 3, piece % 3].astype(F32)
    lane = lax.broadcasted_iota(jnp.int32, (8, 128), 1)
    row_re = jnp.broadcast_to(matrix_ref[0:1], (8, 128))
    row_im = jnp.broadcast_to(matrix_ref[1:2], (8, 128))
    pick = lane == lax.axis_index(SPACE)
    own, by_re, by_im = (jnp.zeros((8, 128), F32) for _ in range(3))
    for source in range(12):
        value = rows[8 * source : 8 * source + 8]
        here = lane == source
        own = jnp.where(here, jnp.sum(jnp.where(pick, value, 0.0), 1, keepdims=True), own)
        by_re = jnp.where(here, jnp.sum(value * row_re, 1, keepdims=True), by_re)
        by_im = jnp.where(here, jnp.sum(value * row_im, 1, keepdims=True), by_im)
    crossed = pltpu.roll(by_im, 4, 0)
    upper = lax.broadcasted_iota(jnp.int32, (8, 128), 0) < 4
    contracted = by_re + jnp.where(upper, -crossed, crossed)
    for row in range(8):
        projected_ref[row] = own[row : row + 1, :12]
        contracted_ref[row] = contracted[row : row + 1, :12]


def placed_out(values):
    return values.reshape(1, 2, 4, 1, 12).transpose(0, 1, 2, 4, 3)


def local(sources, gauge_links, eigenvectors, elementals):
    vectors = eigenvectors[0, :, :, :, 0].transpose(2, 1, 0, 3)
    kept = (elementals[0, :, 0], vectors)
    finals, matrix, vectors = spinors(sources, gauge_links, kept)
    partial_value = local_call(
        project_kernel, jax.ShapeDtypeStruct((8, 3, 4, 128), BF16), [], 1 << 25
    )(finals, vectors)
    totals = all_reduce(partial_value)
    shape = jax.ShapeDtypeStruct((8, 1, 12), F32)
    projected, contracted = local_call(
        finish_kernel,
        (shape, shape),
        [pltpu.VMEM((96, 128), F32)],
        1 << 17,
    )(totals, matrix)
    return placed_out(projected), placed_out(contracted)


def solution(mesh):
    fine = Mesh(mesh.devices.reshape(2, 2, 4, 8, 2, 2), (*TM, *SPACE))
    placed = (
        P(TM, None, None, None, None, SPACE, None),
        P(None, TM, None, None, None, SPACE, None),
        P(TM, None, None, None, SPACE, None),
        P(TM, None, SPACE, None),
    )
    result = P(TM, None, None, None, SPACE)
    return jax.shard_map(
        local, mesh=fine, in_specs=placed, out_specs=(result, result), check_vma=False
    )
```

```python
import jax
import jax.numpy as jnp
from jax import lax
from jax.experimental import pallas as pl
from jax.experimental.pallas import tpu as pltpu
from jax.sharding import Mesh
from jax.sharding import PartitionSpec as P

HOPPING = 0.125
TM = ("y_hi", "core")
SPACE = ("x", "z_hi", "z_lo", "y_lo")
PLANE = ("x", "y_lo")
DEPTH = ("z_hi", "z_lo")
POSITION = ("x", *DEPTH)
BLOCK = ("y_lo", *TM)
GROUP = ("z_lo", *BLOCK)
LX = 8
FIELD = 48
LINK = 72
ROWS = FIELD + LINK
SITES = 128
F32 = jnp.float32
BF16 = jnp.bfloat16


def exchange(value, axes):
    return lax.all_to_all(value, axes, 0, 0, tiled=True)


def send(value, axes):
    count = lax.axis_size(axes)
    pairs = [(i, (i + 1 if i % 2 else i - 1) % count) for i in range(count)]
    return lax.ppermute(value, axes, pairs)


def local_call(kernel, outs, scratch, flops, **options):
    return pl.pallas_call(
        kernel,
        **options,
        out_shape=outs,
        scratch_shapes=scratch,
        compiler_params=pltpu.CompilerParams(vmem_limit_bytes=16 << 20),
        cost_estimate=pl.CostEstimate(flops=flops, bytes_accessed=1 << 20, transcendentals=0),
    )


def clear_kernel(out_ref):
    out_ref[...] = jnp.zeros(out_ref.shape, F32)


def pack_kernel(clear_ref, source_ref, link_ref, out_ref, rows, links):
    for entry in range(36):
        links[2 * entry : 2 * entry + 2] = link_ref[entry].astype(F32)
    shared = links[...]
    for target in range(8):
        rows[target, FIELD:] = shared
    for target in range(8):
        for part in range(2):
            for color in range(3):
                for which in range(2):
                    at = part * 24 + color * 8 + which * 4
                    if target < 6:
                        piece = source_ref[part, color, 2 * target + which].astype(F32)
                    else:
                        piece = clear_ref[:4]
                    rows[target, at : at + 4] = piece
    packed = rows[...].astype(BF16)
    out_ref[:8] = packed
    out_ref[8:] = packed


def signed_add(base, sign, value):
    if base is None:
        return value if sign > 0 else -value
    return base + value if sign > 0 else base - value


def block_terms(direction, first, second):
    if direction == 0:
        return (((1, second[1]), (-1, second[0])), ((1, first[1]), (-1, first[0])))
    if direction == 1:
        return (((-1, second[0]), (-1, second[1])), ((1, first[0]), (1, first[1])))
    if direction == 2:
        return (((1, first[1]), (-1, first[0])), ((-1, second[1]), (1, second[0])))
    return (((1, first[0]), (1, first[1])), ((1, second[0]), (1, second[1])))


def half_of(field, direction, sign):
    half = []
    for color in range(3):
        up = [(field(0, color, a), field(1, color, a)) for a in range(4)]
        terms = block_terms(direction, up[2], up[3])
        half.append(
            [
                tuple(
                    signed_add(up[a][part], sign * terms[a][part][0], terms[a][part][1])
                    for part in range(2)
                )
                for a in range(2)
            ]
        )
    return half


def color_apply(link, direction, half, dagger):
    out = []
    for row in range(3):
        acc = [[None, None], [None, None]]
        for col in range(3):
            i, j = (col, row) if dagger else (row, col)
            re, im = link(direction, i, j, 0), link(direction, i, j, 1)
            flip = -1 if dagger else 1
            for a in range(2):
                vec_re, vec_im = half[col][a]
                acc[a][0] = signed_add(acc[a][0], 1, re * vec_re)
                acc[a][0] = signed_add(acc[a][0], -flip, im * vec_im)
                acc[a][1] = signed_add(acc[a][1], 1, re * vec_im)
                acc[a][1] = signed_add(acc[a][1], flip, im * vec_re)
        out.append([tuple(acc[a]) for a in range(2)])
    return out


def shift(value, direction, ahead):
    if direction == 3:
        return pltpu.roll(value, 6 if ahead else 2, 0)
    if direction == 1:
        return pltpu.roll(value, SITES - LX if ahead else LX, 1)
    column = lax.broadcasted_iota(jnp.int32, value.shape, 1) % LX
    if ahead:
        return jnp.where(
            column == LX - 1, pltpu.roll(value, LX - 1, 1), pltpu.roll(value, SITES - 1, 1)
        )
    return jnp.where(column == 0, pltpu.roll(value, SITES - (LX - 1), 1), pltpu.roll(value, 1, 1))


def map_half(function, half):
    return [[tuple(function(v) for v in pair) for pair in spins] for spins in half]


def accumulate(total, direction, ahead, behind):
    for color in range(3):
        both = []
        for a in range(2):
            for part in range(2):
                key = (part, color, a)
                value = ahead[color][a][part] + behind[color][a][part]
                total[key] = value if key not in total else total[key] + value
            both.append(tuple(ahead[color][a][part] - behind[color][a][part] for part in range(2)))
        terms = block_terms(direction, both[0], both[1])
        outer = -1 if direction == 3 else 1
        for a in range(2):
            for part in range(2):
                key = (part, color, a + 2)
                sign, value = terms[a][part]
                total[key] = signed_add(total.get(key), outer * sign, value)


def hop(field, link, ahead_z, behind_z):
    total = {}
    for direction in (0, 1, 3):
        ahead = map_half(
            lambda v, d=direction: shift(v, d, True), half_of(field, direction, -1)
        )
        behind = color_apply(link, direction, half_of(field, direction, 1), True)
        behind = map_half(lambda v, d=direction: shift(v, d, False), behind)
        accumulate(total, direction, color_apply(link, direction, ahead, False), behind)
    accumulate(total, 2, color_apply(link, 2, ahead_z, False), behind_z)
    return total


def comp(part, color, spin):
    return color * 8 + part * 4 + spin


def slot(direction, row, col, part):
    return direction * 18 + row * 6 + col * 2 + part


def field_at(ref, layer):
    return lambda part, color, spin: ref[layer, comp(part, color, spin)]


def link_at(ref, layer):
    return lambda direction, row, col, part: ref[layer, slot(direction, row, col, part)]


def half_slot(part, color, spin):
    return color * 4 + spin * 2 + part


def put_half(ref, half):
    for color in range(3):
        for a in range(2):
            for part in range(2):
                ref[half_slot(part, color, a)] = half[color][a][part].astype(ref.dtype)


def get_half(ref, layer):
    return [
        [tuple(ref[layer, half_slot(part, color, a)] for part in range(2)) for a in range(2)]
        for color in range(3)
    ]


def assemble(wide, start, src, links, layer):
    slices = lax.broadcasted_iota(jnp.int32, (4, SITES), 0)
    turn = jnp.where(slices == 3, -1.0, 1.0)
    for color in range(3):
        for part in range(2):
            for spin in range(4):
                for which in range(2):
                    row = start + part * 24 + color * 8 + which * 4 + spin
                    src[layer, comp(part, color, spin), pl.ds(which, 4, stride=2)] = wide[
                        pl.ds(row, 4, stride=ROWS)
                    ]
    for entry in range(LINK):
        value = wide[pl.ds(start + FIELD + entry, 4, stride=ROWS)]
        if entry >= 54:
            value = value * turn
        for which in range(2):
            links[layer, entry, pl.ds(which, 4, stride=2)] = value


def sent_down(field):
    return half_of(field, 2, -1)


def sent_up(field, link):
    return color_apply(link, 2, half_of(field, 2, 1), True)


def own_kernel(own_ref, base_ref, link_ref, near_ref, wide, next_ref):
    wide[...] = own_ref[...].reshape(16 * ROWS, SITES).astype(F32)
    side = lax.axis_index("z_lo")

    def one(layer, carry):
        assemble(wide, layer * 4 * ROWS, base_ref, link_ref, layer)
        return carry

    lax.fori_loop(0, 4, one, 0)
    near_ref[: 4 * ROWS] = own_ref[pl.ds(side * 12, 4)].reshape(4 * ROWS, SITES)

    def put(ref, start, below, above):
        for color in range(3):
            for a in range(2):
                at = start + 8 * half_slot(0, color, a)
                low = jnp.concatenate(below[color][a], 0)
                high = jnp.concatenate(above[color][a], 0)
                ref[at : at + 16] = jnp.where(side == 0, low, high).astype(BF16)

    def half_down(layer):
        return sent_down(field_at(base_ref, layer))

    def half_up(layer):
        return sent_up(field_at(base_ref, layer), link_at(link_ref, layer))

    put(near_ref, 4 * ROWS, half_down(1), half_up(2))
    second = 1 + side

    def keep(at, value):
        next_ref[at] = value

    sweep_layer(base_ref, base_ref, link_ref, second, half_down(second + 1), half_up(second - 1), keep)

    def field(part, color, spin):
        return next_ref[comp(part, color, spin)]

    put(near_ref, 4 * ROWS + 96, sent_down(field), sent_up(field, link_at(link_ref, second)))


def sweep_layer(from_ref, src_ref, link_ref, layer, ahead, behind, put):
    total = hop(field_at(from_ref, layer), link_at(link_ref, layer), ahead, behind)
    for key, value in total.items():
        put(comp(*key), src_ref[layer, comp(*key)] + HOPPING * value)


def prepare_layer(from_ref, link_ref, layer, ahead_ref, ahead_at, behind_ref, behind_at):
    put_half(ahead_ref.at[ahead_at], sent_down(field_at(from_ref, layer)))
    put_half(
        behind_ref.at[behind_at], sent_up(field_at(from_ref, layer), link_at(link_ref, layer))
    )


def inner_kernel(
    matrix_ref, vector_ref, base_ref, link_ref,
    kept_matrix, kept_vector, inner_ref, ahead_ref, behind_ref,
):
    kept_matrix[...] = matrix_ref[...]
    kept_vector[...] = vector_ref[...]

    def prepare(layer, carry):
        prepare_layer(base_ref, link_ref, layer, ahead_ref, layer, behind_ref, layer)
        return carry

    def step(layer, carry):
        def put(at, value):
            inner_ref[layer - 1, at] = value

        ahead, behind = get_half(ahead_ref, layer + 1), get_half(behind_ref, layer - 1)
        sweep_layer(base_ref, base_ref, link_ref, layer, ahead, behind, put)
        return carry

    lax.fori_loop(0, 4, prepare, 0)
    lax.fori_loop(1, 3, step, 0)


def sweep_kernel(
    near_ref, base_ref, link_ref, inner_ref, ahead_ref, behind_ref, out_ref,
    wide, src, one, two, links, ahead, behind, done,
):
    side = lax.axis_index("z_lo")
    block, halo = 2 - 2 * side, 1 + 3 * side
    wide[...] = near_ref[: 4 * ROWS].astype(F32)
    src[pl.ds(block, 4)] = base_ref[...]
    links[pl.ds(block, 4)] = link_ref[...]
    one[pl.ds(block + 1, 2)] = inner_ref[...]
    ahead[pl.ds(block, 4)] = ahead_ref[...]
    behind[pl.ds(block + 1, 4)] = behind_ref[...]
    near = near_ref[4 * ROWS : 4 * ROWS + 96].astype(F32).reshape(12, 8, SITES)

    def place_near(value):
        @pl.when(side == 0)
        def _():
            behind[1] = value

        @pl.when(side == 1)
        def _():
            ahead[5] = value

    place_near(near)
    assemble(wide, 0, src, links, halo)
    prepare_layer(src, links, halo, ahead, halo, behind, halo + 1)

    def first(at, carry):
        layer = at + 1 + 2 * side

        def put(slot_at, value):
            one[layer, slot_at] = value

        halves = get_half(ahead, layer + 1), get_half(behind, layer)
        sweep_layer(src, src, links, layer, *halves, put)
        return carry

    lax.fori_loop(0, 2, first, 0)

    def prepare_one(layer, carry):
        put_half(ahead.at[layer + 1], sent_down(field_at(one, layer + 1)))
        put_half(behind.at[layer + 1], sent_up(field_at(one, layer), link_at(links, layer)))
        return carry

    def second(at, carry):
        layer = at + 1 + side

        def put(slot_at, value):
            two[layer, slot_at] = value

        sweep_layer(one, src, links, layer, get_half(ahead, layer + 1), get_half(behind, layer), put)
        return carry

    lax.fori_loop(1, 4, prepare_one, 0)
    place_near(near_ref[4 * ROWS + 96 :].astype(F32).reshape(12, 8, SITES))
    lax.fori_loop(0, 3, second, 0)
    put_half(ahead.at[3], sent_down(field_at(two, 3)))
    put_half(behind.at[3], sent_up(field_at(two, 2), link_at(links, 2)))
    nothing = jnp.zeros((12, 8, SITES), F32)

    def put_done(at, slot_at, value):
        done[pl.ds(pl.multiple_of((at * 24 + slot_at) * 8, 8), 8)] = value

    def put_cross(down, up):
        total = {}
        accumulate(total, 2, down, up)
        for key, value in total.items():
            put_done(2 - side, comp(*key), HOPPING * value)

    none = [[(nothing[0], nothing[0])] * 2] * 3

    @pl.when(side == 0)
    def _():
        put_half(behind.at[2], sent_up(field_at(two, 1), link_at(links, 1)))
        ahead[4] = nothing
        put_cross(none, sent_up(field_at(two, 3), link_at(links, 3)))

    @pl.when(side == 1)
    def _():
        put_half(ahead.at[4], sent_down(field_at(two, 4)))
        behind[2] = nothing
        put_cross(color_apply(link_at(links, 1), 2, sent_down(field_at(two, 2)), False), none)

    def third(layer, carry):
        def put(at, value):
            put_done(layer - 2 + 2 * side, at, value)

        sweep_layer(two, src, links, layer, get_half(ahead, layer + 1), get_half(behind, layer), put)
        return carry

    lax.fori_loop(2, 4, third, 0)
    for at in range(24):
        put_done(3 - 3 * side, at, nothing[0])
    for layer in range(4):
        for time in range(4):
            for color in range(3):
                start = (layer * 24 + color * 8) * 8 + 2 * time
                pair = [done[pl.ds(start + which, 8, stride=8)] for which in range(2)]
                out_ref[layer * 4 + time, color * 16 : color * 16 + 16] = jnp.concatenate(
                    pair, 0
                ).astype(BF16)


def project_kernel(phi_ref, vector_ref, out_ref):
    totals = [None, None]
    for color in range(3):
        parts = phi_ref[:, color * 16 : color * 16 + 16].reshape(2, 8 * 16, SITES)
        rows = (parts[0].astype(F32) + parts[1].astype(F32)).astype(BF16)
        for part in range(2):
            value = lax.dot_general(
                rows,
                vector_ref[color, part],
                (((1,), (1,)), ((), ())),
                preferred_element_type=F32,
            )
            totals[part] = value if totals[part] is None else totals[part] + value
    crossed = pltpu.roll(totals[1].reshape(16, 8, 128), 4, 1)
    upper = lax.broadcasted_iota(jnp.int32, crossed.shape, 1) < 4
    mixed = totals[0].reshape(16, 8, 128) + jnp.where(upper, crossed, -crossed)
    for source in range(12):
        for part in range(2):
            member, at = divmod(2 * source + part, 3)
            out_ref[member, at] = mixed[source, 4 * part : 4 * part + 4].astype(BF16)


def spread_kernel(value_ref, out_ref):
    total = value_ref[0].astype(F32)
    for member in range(1, value_ref.shape[0]):
        total = total + value_ref[member].astype(F32)
    total = total.astype(BF16)
    for member in range(out_ref.shape[0]):
        out_ref[member] = total


def summed(value, copies):
    shape = jax.ShapeDtypeStruct((copies, *value.shape[1:]), BF16)
    return local_call(spread_kernel, shape, [], 1 << 16)(value)


def all_reduce(partial_value):
    plane = lax.axis_size(PLANE)
    depth = lax.axis_size(DEPTH)
    copies = summed(exchange(partial_value, PLANE), depth)
    copies = summed(exchange(copies, DEPTH), plane)
    return exchange(copies, PLANE)


def spinors(sources, gauge_links, kept):
    moved = sources[0, :, :, :, :, 0].transpose(0, 2, 3, 1, 4)
    entries = gauge_links[:, 0, :, :, :, 0].transpose(0, 2, 3, 1, 4).reshape(36, 2, SITES)
    clear = local_call(clear_kernel, jax.ShapeDtypeStruct((8, SITES), F32), [], 1 << 32)()
    packed = local_call(
        pack_kernel,
        jax.ShapeDtypeStruct((16, ROWS, SITES), BF16),
        [
            pltpu.VMEM((8, ROWS, SITES), F32),
            pltpu.VMEM((LINK, SITES), F32),
        ],
        1 << 17,
    )(clear, moved, entries)
    own = exchange(packed, GROUP)
    vectors = (8, SITES)
    base, links, near = local_call(
        own_kernel,
        (
            jax.ShapeDtypeStruct((4, 24, *vectors), F32),
            jax.ShapeDtypeStruct((4, LINK, *vectors), F32),
            jax.ShapeDtypeStruct((4 * ROWS + 192, SITES), BF16),
        ),
        [pltpu.VMEM((16 * ROWS, SITES), F32), pltpu.VMEM((24, *vectors), F32)],
        1 << 20,
    )(own)
    matrix, spectrum = kept
    matrix, spectrum, inner, ahead, behind = local_call(
        inner_kernel,
        (
            jax.ShapeDtypeStruct(matrix.shape, F32),
            jax.ShapeDtypeStruct(spectrum.shape, BF16),
            jax.ShapeDtypeStruct((2, 24, *vectors), F32),
            jax.ShapeDtypeStruct((4, 12, *vectors), F32),
            jax.ShapeDtypeStruct((4, 12, *vectors), F32),
        ),
        [],
        1 << 22,
    )(matrix, spectrum, base, links)
    near = send(near, POSITION)
    done = local_call(
        sweep_kernel,
        jax.ShapeDtypeStruct((16, FIELD, SITES), BF16),
        [
            pltpu.VMEM((4 * ROWS, SITES), F32),
            pltpu.VMEM((6, 24, *vectors), F32),
            pltpu.VMEM((6, 24, *vectors), F32),
            pltpu.VMEM((6, 24, *vectors), F32),
            pltpu.VMEM((6, LINK, *vectors), F32),
            pltpu.VMEM((7, 12, *vectors), F32),
            pltpu.VMEM((7, 12, *vectors), F32),
            pltpu.VMEM((4 * 24 * 8, SITES), F32),
        ],
        1 << 24,
    )(near, base, links, inner, ahead, behind)
    return exchange(done, GROUP), matrix, spectrum


def finish_kernel(total_ref, matrix_ref, projected_ref, contracted_ref, rows):
    for piece in range(24):
        rows[4 * piece : 4 * piece + 4] = total_ref[piece // 3, piece % 3].astype(F32)
    lane = lax.broadcasted_iota(jnp.int32, (8, 128), 1)
    row_re = jnp.broadcast_to(matrix_ref[0:1], (8, 128))
    row_im = jnp.broadcast_to(matrix_ref[1:2], (8, 128))
    pick = lane == lax.axis_index(SPACE)
    own, by_re, by_im = (jnp.zeros((8, 128), F32) for _ in range(3))
    for source in range(12):
        value = rows[8 * source : 8 * source + 8]
        here = lane == source
        own = jnp.where(here, jnp.sum(jnp.where(pick, value, 0.0), 1, keepdims=True), own)
        by_re = jnp.where(here, jnp.sum(value * row_re, 1, keepdims=True), by_re)
        by_im = jnp.where(here, jnp.sum(value * row_im, 1, keepdims=True), by_im)
    crossed = pltpu.roll(by_im, 4, 0)
    upper = lax.broadcasted_iota(jnp.int32, (8, 128), 0) < 4
    contracted = by_re + jnp.where(upper, -crossed, crossed)
    for row in range(8):
        projected_ref[row] = own[row : row + 1, :12]
        contracted_ref[row] = contracted[row : row + 1, :12]


def placed_out(values):
    return values.reshape(1, 2, 4, 1, 12).transpose(0, 1, 2, 4, 3)


def local(sources, gauge_links, eigenvectors, elementals):
    vectors = eigenvectors[0, :, :, :, 0].transpose(2, 1, 0, 3)
    kept = (elementals[0, :, 0], vectors)
    finals, matrix, vectors = spinors(sources, gauge_links, kept)
    partial_value = local_call(
        project_kernel, jax.ShapeDtypeStruct((8, 3, 4, 128), BF16), [], 1 << 25
    )(finals, vectors)
    totals = all_reduce(partial_value)
    shape = jax.ShapeDtypeStruct((8, 1, 12), F32)
    projected, contracted = local_call(
        finish_kernel,
        (shape, shape),
        [pltpu.VMEM((96, 128), F32)],
        1 << 17,
    )(totals, matrix)
    return placed_out(projected), placed_out(contracted)


def solution(mesh):
    fine = Mesh(mesh.devices.reshape(2, 2, 4, 8, 2, 2), (*TM, *SPACE))
    placed = (
        P(TM, None, None, None, None, SPACE, None),
        P(None, TM, None, None, None, SPACE, None),
        P(TM, None, None, None, SPACE, None),
        P(TM, None, SPACE, None),
    )
    result = P(TM, None, None, None, SPACE)
    return jax.shard_map(
        local, mesh=fine, in_specs=placed, out_specs=(result, result), check_vma=False
    )
```

```python
import jax
import jax.numpy as jnp
from jax import lax
from jax.experimental import pallas as pl
from jax.experimental.pallas import tpu as pltpu
from jax.sharding import Mesh
from jax.sharding import PartitionSpec as P

HOPPING = 0.125
TM = ("y_hi", "core")
SPACE = ("x", "z_hi", "z_lo", "y_lo")
PLANE = ("x", "y_lo")
DEPTH = ("z_hi", "z_lo")
POSITION = ("x", *DEPTH)
BLOCK = ("y_hi", "core", "y_lo")
GROUP = ("y_hi", "y_lo", "core", "z_lo")
LX = 8
FIELD = 48
LINK = 72
ROWS = FIELD + LINK
SITES = 128
F32 = jnp.float32
BF16 = jnp.bfloat16


def exchange(value, axes):
    return lax.all_to_all(value, axes, 0, 0, tiled=True)


def send(value, axes, steps):
    count = lax.axis_size(axes)
    pairs = [(i, (i + steps[1] if i % 2 else i - steps[0]) % count) for i in range(count)]
    return lax.ppermute(value, axes, pairs)


def local_call(kernel, outs, scratch, flops, **options):
    return pl.pallas_call(
        kernel,
        **options,
        out_shape=outs,
        scratch_shapes=scratch,
        compiler_params=pltpu.CompilerParams(vmem_limit_bytes=16 << 20),
        cost_estimate=pl.CostEstimate(flops=flops, bytes_accessed=1 << 20, transcendentals=0),
    )


def member(high, low, core, position):
    return high * 8 + low * 4 + core * 2 + position


def clear_kernel(out_ref):
    out_ref[...] = jnp.zeros(out_ref.shape, F32)


def pack_kernel(clear_ref, source_ref, link_ref, out_ref, rows, links):
    for entry in range(36):
        links[2 * entry : 2 * entry + 2] = link_ref[entry].astype(F32)
    shared = links[...]
    for target in range(8):
        rows[target, FIELD:] = shared
    for target in range(8):
        for part in range(2):
            for color in range(3):
                for which in range(2):
                    at = part * 24 + color * 8 + which * 4
                    if target < 6:
                        piece = source_ref[part, color, 2 * target + which].astype(F32)
                    else:
                        piece = clear_ref[:4]
                    rows[target, at : at + 4] = piece
    for target in range(8):
        packed = rows[target].astype(BF16)
        high, core, low = target // 4, target // 2 % 2, target % 2
        for position in range(2):
            out_ref[member(high, low, core, position)] = packed


def signed_add(base, sign, value):
    if base is None:
        return value if sign > 0 else -value
    return base + value if sign > 0 else base - value


def block_terms(direction, first, second):
    if direction == 0:
        return (((1, second[1]), (-1, second[0])), ((1, first[1]), (-1, first[0])))
    if direction == 1:
        return (((-1, second[0]), (-1, second[1])), ((1, first[0]), (1, first[1])))
    if direction == 2:
        return (((1, first[1]), (-1, first[0])), ((-1, second[1]), (1, second[0])))
    return (((1, first[0]), (1, first[1])), ((1, second[0]), (1, second[1])))


def half_of(field, direction, sign):
    half = []
    for color in range(3):
        up = [(field(0, color, a), field(1, color, a)) for a in range(4)]
        terms = block_terms(direction, up[2], up[3])
        half.append(
            [
                tuple(
                    signed_add(up[a][part], sign * terms[a][part][0], terms[a][part][1])
                    for part in range(2)
                )
                for a in range(2)
            ]
        )
    return half


def color_apply(link, direction, half, dagger):
    out = []
    for row in range(3):
        acc = [[None, None], [None, None]]
        for col in range(3):
            i, j = (col, row) if dagger else (row, col)
            re, im = link(direction, i, j, 0), link(direction, i, j, 1)
            flip = -1 if dagger else 1
            for a in range(2):
                vec_re, vec_im = half[col][a]
                acc[a][0] = signed_add(acc[a][0], 1, re * vec_re)
                acc[a][0] = signed_add(acc[a][0], -flip, im * vec_im)
                acc[a][1] = signed_add(acc[a][1], 1, re * vec_im)
                acc[a][1] = signed_add(acc[a][1], flip, im * vec_re)
        out.append([tuple(acc[a]) for a in range(2)])
    return out


def shift(value, direction, ahead):
    if direction == 3:
        return pltpu.roll(value, 6 if ahead else 2, 0)
    if direction == 1:
        return pltpu.roll(value, SITES - LX if ahead else LX, 1)
    column = lax.broadcasted_iota(jnp.int32, value.shape, 1) % LX
    if ahead:
        return jnp.where(
            column == LX - 1, pltpu.roll(value, LX - 1, 1), pltpu.roll(value, SITES - 1, 1)
        )
    return jnp.where(column == 0, pltpu.roll(value, SITES - (LX - 1), 1), pltpu.roll(value, 1, 1))


def map_half(function, half):
    return [[tuple(function(v) for v in pair) for pair in spins] for spins in half]


def accumulate(total, direction, ahead, behind):
    for color in range(3):
        both = []
        for a in range(2):
            for part in range(2):
                key = (part, color, a)
                value = ahead[color][a][part] + behind[color][a][part]
                total[key] = value if key not in total else total[key] + value
            both.append(tuple(ahead[color][a][part] - behind[color][a][part] for part in range(2)))
        terms = block_terms(direction, both[0], both[1])
        outer = -1 if direction == 3 else 1
        for a in range(2):
            for part in range(2):
                key = (part, color, a + 2)
                sign, value = terms[a][part]
                total[key] = signed_add(total.get(key), outer * sign, value)


def hop(field, link, ahead_z, behind_z):
    total = {}
    for direction in (0, 1, 3):
        ahead = map_half(
            lambda v, d=direction: shift(v, d, True), half_of(field, direction, -1)
        )
        behind = color_apply(link, direction, half_of(field, direction, 1), True)
        behind = map_half(lambda v, d=direction: shift(v, d, False), behind)
        accumulate(total, direction, color_apply(link, direction, ahead, False), behind)
    accumulate(total, 2, color_apply(link, 2, ahead_z, False), behind_z)
    return total


def comp(part, color, spin):
    return color * 8 + part * 4 + spin


def slot(direction, row, col, part):
    return direction * 18 + row * 6 + col * 2 + part


def field_at(ref, layer):
    return lambda part, color, spin: ref[layer, comp(part, color, spin)]


def link_at(ref, layer):
    return lambda direction, row, col, part: ref[layer, slot(direction, row, col, part)]


def half_slot(part, color, spin):
    return color * 4 + spin * 2 + part


def put_half(ref, half):
    for color in range(3):
        for a in range(2):
            for part in range(2):
                ref[half_slot(part, color, a)] = half[color][a][part].astype(ref.dtype)


def get_half(ref, layer):
    return [
        [tuple(ref[layer, half_slot(part, color, a)] for part in range(2)) for a in range(2)]
        for color in range(3)
    ]


def assemble(wide, start, src, links, layer):
    slices = lax.broadcasted_iota(jnp.int32, (4, SITES), 0)
    turn = jnp.where(slices == 3, -1.0, 1.0)
    for color in range(3):
        for part in range(2):
            for spin in range(4):
                for which in range(2):
                    row = start + part * 24 + color * 8 + which * 4 + spin
                    src[layer, comp(part, color, spin), pl.ds(which, 4, stride=2)] = wide[
                        pl.ds(row, 4, stride=ROWS)
                    ]
    for entry in range(LINK):
        value = wide[pl.ds(start + FIELD + entry, 4, stride=ROWS)]
        if entry >= 54:
            value = value * turn
        for which in range(2):
            links[layer, entry, pl.ds(which, 4, stride=2)] = value


def sent_down(field):
    return half_of(field, 2, -1)


def sent_up(field, link):
    return color_apply(link, 2, half_of(field, 2, 1), True)


def own_kernel(own_ref, base_ref, link_ref, near_ref, far_ref, wide, next_ref):
    for layer in range(4):
        for time in range(4):
            start = (layer * 4 + time) * ROWS
            wide[start : start + ROWS] = own_ref[
                member(time // 2, layer % 2, time % 2, layer // 2)
            ].astype(F32)
    side = lax.axis_index("z_lo")

    def one(layer, carry):
        assemble(wide, layer * 4 * ROWS, base_ref, link_ref, layer)
        return carry

    lax.fori_loop(0, 4, one, 0)
    edge = pl.ds(pl.multiple_of(side * 12 * ROWS, 8), 4 * ROWS)
    near_ref[: 4 * ROWS] = wide[edge].astype(BF16)

    def put(ref, start, below, above):
        for color in range(3):
            for a in range(2):
                at = start + 8 * half_slot(0, color, a)
                low = jnp.concatenate(below[color][a], 0)
                high = jnp.concatenate(above[color][a], 0)
                ref[at : at + 16] = jnp.where(side == 0, low, high).astype(BF16)

    def half_down(layer):
        return sent_down(field_at(base_ref, layer))

    def half_up(layer):
        return sent_up(field_at(base_ref, layer), link_at(link_ref, layer))

    put(far_ref, 0, half_down(0), half_up(3))
    put(near_ref, 4 * ROWS, half_down(1), half_up(2))
    second = 1 + side

    def keep(at, value):
        next_ref[at] = value

    sweep_layer(base_ref, base_ref, link_ref, second, half_down(second + 1), half_up(second - 1), keep)

    def field(part, color, spin):
        return next_ref[comp(part, color, spin)]

    put(near_ref, 4 * ROWS + 96, sent_down(field), sent_up(field, link_at(link_ref, second)))


def sweep_layer(from_ref, src_ref, link_ref, layer, ahead, behind, put):
    total = hop(field_at(from_ref, layer), link_at(link_ref, layer), ahead, behind)
    for key, value in total.items():
        put(comp(*key), src_ref[layer, comp(*key)] + HOPPING * value)


def prepare_layer(from_ref, link_ref, layer, ahead_ref, ahead_at, behind_ref, behind_at):
    put_half(ahead_ref.at[ahead_at], sent_down(field_at(from_ref, layer)))
    put_half(
        behind_ref.at[behind_at], sent_up(field_at(from_ref, layer), link_at(link_ref, layer))
    )


def inner_kernel(
    matrix_ref, vector_ref, base_ref, link_ref,
    kept_matrix, kept_vector, inner_ref, ahead_ref, behind_ref,
):
    kept_matrix[...] = matrix_ref[...]
    kept_vector[...] = vector_ref[...]

    def prepare(layer, carry):
        prepare_layer(base_ref, link_ref, layer, ahead_ref, layer, behind_ref, layer)
        return carry

    def step(layer, carry):
        def put(at, value):
            inner_ref[layer - 1, at] = value

        ahead, behind = get_half(ahead_ref, layer + 1), get_half(behind_ref, layer - 1)
        sweep_layer(base_ref, base_ref, link_ref, layer, ahead, behind, put)
        return carry

    lax.fori_loop(0, 4, prepare, 0)
    lax.fori_loop(1, 3, step, 0)


def sweep_kernel(
    near_ref, far_ref, base_ref, link_ref, inner_ref, ahead_ref, behind_ref, out_ref,
    wide, src, one, two, links, ahead, behind, done,
):
    side = lax.axis_index("z_lo")
    block, halo = 2 - 2 * side, 1 + 3 * side
    wide[...] = near_ref[: 4 * ROWS].astype(F32)
    src[pl.ds(block, 4)] = base_ref[...]
    links[pl.ds(block, 4)] = link_ref[...]
    one[pl.ds(block + 1, 2)] = inner_ref[...]
    ahead[pl.ds(block, 4)] = ahead_ref[...]
    behind[pl.ds(block + 1, 4)] = behind_ref[...]
    near = near_ref[4 * ROWS : 4 * ROWS + 96].astype(F32).reshape(12, 8, SITES)
    far = far_ref[...].astype(F32).reshape(12, 8, SITES)
    ahead[6 - side] = jnp.where(side == 0, far, near)
    behind[1 - side] = jnp.where(side == 0, near, far)
    assemble(wide, 0, src, links, halo)
    prepare_layer(src, links, halo, ahead, halo, behind, halo + 1)

    def first(at, carry):
        layer = at + 1 - side + jnp.where(at >= 2 - side, 2, 0)

        def put(slot_at, value):
            one[layer, slot_at] = value

        halves = get_half(ahead, layer + 1), get_half(behind, layer)
        sweep_layer(src, src, links, layer, *halves, put)
        return carry

    lax.fori_loop(0, 3, first, 0)

    def prepare(from_ref, layer):
        put_half(ahead.at[layer + 2], sent_down(field_at(from_ref, layer + 2)))
        put_half(behind.at[layer + 1], sent_up(field_at(from_ref, layer), link_at(links, layer)))

    def prepare_one(layer, carry):
        prepare(one, layer)
        return carry

    def second(layer, carry):
        def put(at, value):
            two[layer, at] = value

        sweep_layer(one, src, links, layer, get_half(ahead, layer + 1), get_half(behind, layer), put)
        return carry

    lax.fori_loop(0, 4, prepare_one, 0)
    near = near_ref[4 * ROWS + 96 :].astype(F32).reshape(12, 8, SITES)

    @pl.when(side == 0)
    def _():
        behind[1] = near

    @pl.when(side == 1)
    def _():
        ahead[5] = near

    lax.fori_loop(1, 5, second, 0)

    def prepare_two(layer, carry):
        prepare(two, layer)
        return carry

    def third(layer, carry):
        def put(at, value):
            done[pl.ds(pl.multiple_of(((layer - 2) * 24 + at) * 8, 8), 8)] = value

        sweep_layer(two, src, links, layer, get_half(ahead, layer + 1), get_half(behind, layer), put)
        return carry

    lax.fori_loop(1, 3, prepare_two, 0)
    lax.fori_loop(2, 4, third, 0)
    for layer in range(2):
        for time in range(4):
            for color in range(3):
                start = (layer * 24 + color * 8) * 8 + 2 * time
                pair = [done[pl.ds(start + which, 8, stride=8)] for which in range(2)]
                out_ref[time * 2 + layer, color * 16 : color * 16 + 16] = jnp.concatenate(
                    pair, 0
                ).astype(BF16)


def project_kernel(phi_ref, vector_ref, out_ref):
    totals = [None, None]
    for color in range(3):
        rows = phi_ref[:, color * 16 : color * 16 + 16].reshape(8 * 16, SITES)
        for part in range(2):
            value = lax.dot_general(
                rows,
                vector_ref[color, part],
                (((1,), (1,)), ((), ())),
                preferred_element_type=F32,
            )
            totals[part] = value if totals[part] is None else totals[part] + value
    crossed = pltpu.roll(totals[1].reshape(16, 8, 128), 4, 1)
    upper = lax.broadcasted_iota(jnp.int32, crossed.shape, 1) < 4
    mixed = totals[0].reshape(16, 8, 128) + jnp.where(upper, crossed, -crossed)
    for source in range(12):
        for part in range(2):
            member, at = divmod(2 * source + part, 3)
            out_ref[member, at] = mixed[source, 4 * part : 4 * part + 4].astype(BF16)


def spread_kernel(value_ref, out_ref):
    total = value_ref[0].astype(F32)
    for member in range(1, value_ref.shape[0]):
        total = total + value_ref[member].astype(F32)
    total = total.astype(BF16)
    for member in range(out_ref.shape[0]):
        out_ref[member] = total


def summed(value, copies):
    shape = jax.ShapeDtypeStruct((copies, *value.shape[1:]), BF16)
    return local_call(spread_kernel, shape, [], 1 << 16)(value)


def all_reduce(partial_value):
    plane = lax.axis_size(PLANE)
    depth = lax.axis_size(DEPTH)
    copies = summed(exchange(partial_value, PLANE), depth)
    copies = summed(exchange(copies, DEPTH), plane)
    return exchange(copies, PLANE)


def spinors(sources, gauge_links, kept):
    moved = sources[0, :, :, :, :, 0].transpose(0, 2, 3, 1, 4)
    entries = gauge_links[:, 0, :, :, :, 0].transpose(0, 2, 3, 1, 4).reshape(36, 2, SITES)
    clear = local_call(clear_kernel, jax.ShapeDtypeStruct((8, SITES), F32), [], 1 << 32)()
    packed = local_call(
        pack_kernel,
        jax.ShapeDtypeStruct((16, ROWS, SITES), BF16),
        [
            pltpu.VMEM((8, ROWS, SITES), F32),
            pltpu.VMEM((LINK, SITES), F32),
        ],
        1 << 17,
    )(clear, moved, entries)
    own = exchange(packed, GROUP)
    vectors = (8, SITES)
    base, links, near, far = local_call(
        own_kernel,
        (
            jax.ShapeDtypeStruct((4, 24, *vectors), F32),
            jax.ShapeDtypeStruct((4, LINK, *vectors), F32),
            jax.ShapeDtypeStruct((4 * ROWS + 192, SITES), BF16),
            jax.ShapeDtypeStruct((96, SITES), BF16),
        ),
        [pltpu.VMEM((16 * ROWS, SITES), F32), pltpu.VMEM((24, *vectors), F32)],
        1 << 20,
    )(own)
    matrix, spectrum = kept
    matrix, spectrum, inner, ahead, behind = local_call(
        inner_kernel,
        (
            jax.ShapeDtypeStruct(matrix.shape, F32),
            jax.ShapeDtypeStruct(spectrum.shape, BF16),
            jax.ShapeDtypeStruct((2, 24, *vectors), F32),
            jax.ShapeDtypeStruct((4, 12, *vectors), F32),
            jax.ShapeDtypeStruct((4, 12, *vectors), F32),
        ),
        [],
        1 << 22,
    )(matrix, spectrum, base, links)
    near = send(near, POSITION, (1, 1))
    far = send(far, POSITION, (2, 2))
    done = local_call(
        sweep_kernel,
        jax.ShapeDtypeStruct((8, FIELD, SITES), BF16),
        [
            pltpu.VMEM((4 * ROWS, SITES), F32),
            pltpu.VMEM((6, 24, *vectors), F32),
            pltpu.VMEM((6, 24, *vectors), F32),
            pltpu.VMEM((6, 24, *vectors), F32),
            pltpu.VMEM((6, LINK, *vectors), F32),
            pltpu.VMEM((7, 12, *vectors), F32),
            pltpu.VMEM((7, 12, *vectors), F32),
            pltpu.VMEM((2 * 24 * 8, SITES), F32),
        ],
        1 << 24,
    )(near, far, base, links, inner, ahead, behind)
    return exchange(done, BLOCK), matrix, spectrum


def finish_kernel(total_ref, matrix_ref, projected_ref, contracted_ref, rows):
    for piece in range(24):
        rows[4 * piece : 4 * piece + 4] = total_ref[piece // 3, piece % 3].astype(F32)
    lane = lax.broadcasted_iota(jnp.int32, (8, 128), 1)
    row_re = jnp.broadcast_to(matrix_ref[0:1], (8, 128))
    row_im = jnp.broadcast_to(matrix_ref[1:2], (8, 128))
    pick = lane == lax.axis_index(SPACE)
    own, by_re, by_im = (jnp.zeros((8, 128), F32) for _ in range(3))
    for source in range(12):
        value = rows[8 * source : 8 * source + 8]
        here = lane == source
        own = jnp.where(here, jnp.sum(jnp.where(pick, value, 0.0), 1, keepdims=True), own)
        by_re = jnp.where(here, jnp.sum(value * row_re, 1, keepdims=True), by_re)
        by_im = jnp.where(here, jnp.sum(value * row_im, 1, keepdims=True), by_im)
    crossed = pltpu.roll(by_im, 4, 0)
    upper = lax.broadcasted_iota(jnp.int32, (8, 128), 0) < 4
    contracted = by_re + jnp.where(upper, -crossed, crossed)
    for row in range(8):
        projected_ref[row] = own[row : row + 1, :12]
        contracted_ref[row] = contracted[row : row + 1, :12]


def placed_out(values):
    return values.reshape(1, 2, 4, 1, 12).transpose(0, 1, 2, 4, 3)


def local(sources, gauge_links, eigenvectors, elementals):
    vectors = eigenvectors[0, :, :, :, 0].transpose(2, 1, 0, 3)
    kept = (elementals[0, :, 0], vectors)
    finals, matrix, vectors = spinors(sources, gauge_links, kept)
    partial_value = local_call(
        project_kernel, jax.ShapeDtypeStruct((8, 3, 4, 128), BF16), [], 1 << 25
    )(finals, vectors)
    totals = all_reduce(partial_value)
    shape = jax.ShapeDtypeStruct((8, 1, 12), F32)
    projected, contracted = local_call(
        finish_kernel,
        (shape, shape),
        [pltpu.VMEM((96, 128), F32)],
        1 << 17,
    )(totals, matrix)
    return placed_out(projected), placed_out(contracted)


def solution(mesh):
    fine = Mesh(mesh.devices.reshape(2, 2, 4, 8, 2, 2), (*TM, *SPACE))
    placed = (
        P(TM, None, None, None, None, SPACE, None),
        P(None, TM, None, None, None, SPACE, None),
        P(TM, None, None, None, SPACE, None),
        P(TM, None, SPACE, None),
    )
    result = P(TM, None, None, None, SPACE)
    return jax.shard_map(
        local, mesh=fine, in_specs=placed, out_specs=(result, result), check_vma=False
    )
```

```python
import jax
import jax.numpy as jnp
from jax import lax
from jax.experimental import pallas as pl
from jax.experimental.pallas import tpu as pltpu
from jax.sharding import Mesh
from jax.sharding import PartitionSpec as P

HOPPING = 0.125
TM = ("y_hi", "core")
SPACE = ("x", "z_hi", "z_lo", "y_lo")
PLANE = ("x", "y_lo")
DEPTH = ("z_lo", "z_hi")
POSITION = ("x", "z_hi", "z_lo")
BLOCK = ("y_hi", "core", "y_lo")
GROUP = ("y_hi", "y_lo", "core", "z_lo")
LX = 8
FIELD = 48
LINK = 72
ROWS = FIELD + LINK
SITES = 128
F32 = jnp.float32
BF16 = jnp.bfloat16


def exchange(value, axes):
    return lax.all_to_all(value, axes, 0, 0, tiled=True)


def send(value, axes, steps):
    count = lax.axis_size(axes)
    pairs = [(i, (i + steps[1] if i % 2 else i - steps[0]) % count) for i in range(count)]
    return lax.ppermute(value, axes, pairs)


def local_call(kernel, outs, scratch, flops, **options):
    return pl.pallas_call(
        kernel,
        **options,
        out_shape=outs,
        scratch_shapes=scratch,
        compiler_params=pltpu.CompilerParams(vmem_limit_bytes=16 << 20),
        cost_estimate=pl.CostEstimate(flops=flops, bytes_accessed=1 << 20, transcendentals=0),
    )


def member(high, low, core, position):
    return high * 8 + low * 4 + core * 2 + position


def clear_kernel(out_ref):
    out_ref[...] = jnp.zeros(out_ref.shape, F32)


def pack_kernel(clear_ref, source_ref, link_ref, out_ref, rows, links):
    for entry in range(36):
        links[2 * entry : 2 * entry + 2] = link_ref[entry].astype(F32)
    shared = links[...]
    for target in range(8):
        rows[target, FIELD:] = shared
    for target in range(8):
        for part in range(2):
            for color in range(3):
                for which in range(2):
                    at = part * 24 + color * 8 + which * 4
                    if target < 6:
                        piece = source_ref[part, color, 2 * target + which].astype(F32)
                    else:
                        piece = clear_ref[:4]
                    rows[target, at : at + 4] = piece
    for target in range(8):
        packed = rows[target].astype(BF16)
        high, core, low = target // 4, target // 2 % 2, target % 2
        for position in range(2):
            out_ref[member(high, low, core, position)] = packed


def signed_add(base, sign, value):
    if base is None:
        return value if sign > 0 else -value
    return base + value if sign > 0 else base - value


def block_terms(direction, first, second):
    if direction == 0:
        return (((1, second[1]), (-1, second[0])), ((1, first[1]), (-1, first[0])))
    if direction == 1:
        return (((-1, second[0]), (-1, second[1])), ((1, first[0]), (1, first[1])))
    if direction == 2:
        return (((1, first[1]), (-1, first[0])), ((-1, second[1]), (1, second[0])))
    return (((1, first[0]), (1, first[1])), ((1, second[0]), (1, second[1])))


def half_of(field, direction, sign):
    half = []
    for color in range(3):
        up = [(field(0, color, a), field(1, color, a)) for a in range(4)]
        terms = block_terms(direction, up[2], up[3])
        half.append(
            [
                tuple(
                    signed_add(up[a][part], sign * terms[a][part][0], terms[a][part][1])
                    for part in range(2)
                )
                for a in range(2)
            ]
        )
    return half


def color_apply(link, direction, half, dagger):
    out = []
    for row in range(3):
        acc = [[None, None], [None, None]]
        for col in range(3):
            i, j = (col, row) if dagger else (row, col)
            re, im = link(direction, i, j, 0), link(direction, i, j, 1)
            flip = -1 if dagger else 1
            for a in range(2):
                vec_re, vec_im = half[col][a]
                acc[a][0] = signed_add(acc[a][0], 1, re * vec_re)
                acc[a][0] = signed_add(acc[a][0], -flip, im * vec_im)
                acc[a][1] = signed_add(acc[a][1], 1, re * vec_im)
                acc[a][1] = signed_add(acc[a][1], flip, im * vec_re)
        out.append([tuple(acc[a]) for a in range(2)])
    return out


def shift(value, direction, ahead):
    if direction == 3:
        return pltpu.roll(value, 6 if ahead else 2, 0)
    if direction == 1:
        return pltpu.roll(value, SITES - LX if ahead else LX, 1)
    column = lax.broadcasted_iota(jnp.int32, value.shape, 1) % LX
    if ahead:
        return jnp.where(
            column == LX - 1, pltpu.roll(value, LX - 1, 1), pltpu.roll(value, SITES - 1, 1)
        )
    return jnp.where(column == 0, pltpu.roll(value, SITES - (LX - 1), 1), pltpu.roll(value, 1, 1))


def map_half(function, half):
    return [[tuple(function(v) for v in pair) for pair in spins] for spins in half]


def accumulate(total, direction, ahead, behind):
    for color in range(3):
        both = []
        for a in range(2):
            for part in range(2):
                key = (part, color, a)
                value = ahead[color][a][part] + behind[color][a][part]
                total[key] = value if key not in total else total[key] + value
            both.append(tuple(ahead[color][a][part] - behind[color][a][part] for part in range(2)))
        terms = block_terms(direction, both[0], both[1])
        outer = -1 if direction == 3 else 1
        for a in range(2):
            for part in range(2):
                key = (part, color, a + 2)
                sign, value = terms[a][part]
                total[key] = signed_add(total.get(key), outer * sign, value)


def hop(field, link, ahead_z, behind_z):
    total = {}
    for direction in (0, 1, 3):
        ahead = map_half(
            lambda v, d=direction: shift(v, d, True), half_of(field, direction, -1)
        )
        behind = color_apply(link, direction, half_of(field, direction, 1), True)
        behind = map_half(lambda v, d=direction: shift(v, d, False), behind)
        accumulate(total, direction, color_apply(link, direction, ahead, False), behind)
    accumulate(total, 2, color_apply(link, 2, ahead_z, False), behind_z)
    return total


def comp(part, color, spin):
    return color * 8 + part * 4 + spin


def slot(direction, row, col, part):
    return direction * 18 + row * 6 + col * 2 + part


def field_at(ref, layer):
    return lambda part, color, spin: ref[layer, comp(part, color, spin)]


def link_at(ref, layer):
    return lambda direction, row, col, part: ref[layer, slot(direction, row, col, part)]


def half_slot(part, color, spin):
    return color * 4 + spin * 2 + part


def put_half(ref, half):
    for color in range(3):
        for a in range(2):
            for part in range(2):
                ref[half_slot(part, color, a)] = half[color][a][part].astype(ref.dtype)


def get_half(ref, layer):
    return [
        [tuple(ref[layer, half_slot(part, color, a)] for part in range(2)) for a in range(2)]
        for color in range(3)
    ]


def assemble(wide, start, src, links, layer):
    slices = lax.broadcasted_iota(jnp.int32, (4, SITES), 0)
    turn = jnp.where(slices == 3, -1.0, 1.0)
    for color in range(3):
        for part in range(2):
            for spin in range(4):
                for which in range(2):
                    row = start + part * 24 + color * 8 + which * 4 + spin
                    src[layer, comp(part, color, spin), pl.ds(which, 4, stride=2)] = wide[
                        pl.ds(row, 4, stride=ROWS)
                    ]
    for entry in range(LINK):
        value = wide[pl.ds(start + FIELD + entry, 4, stride=ROWS)]
        if entry >= 54:
            value = value * turn
        for which in range(2):
            links[layer, entry, pl.ds(which, 4, stride=2)] = value


def sent_down(field):
    return half_of(field, 2, -1)


def sent_up(field, link):
    return color_apply(link, 2, half_of(field, 2, 1), True)


def own_kernel(own_ref, base_ref, link_ref, near_ref, far_ref, wide, next_ref):
    for layer in range(4):
        for time in range(4):
            start = (layer * 4 + time) * ROWS
            wide[start : start + ROWS] = own_ref[
                member(time // 2, layer % 2, time % 2, layer // 2)
            ].astype(F32)
    side = lax.axis_index("z_lo")

    def one(layer, carry):
        assemble(wide, layer * 4 * ROWS, base_ref, link_ref, layer)
        return carry

    lax.fori_loop(0, 4, one, 0)
    edge = pl.ds(pl.multiple_of(side * 12 * ROWS, 8), 4 * ROWS)
    near_ref[: 4 * ROWS] = wide[edge].astype(BF16)

    def put(ref, start, below, above):
        for color in range(3):
            for a in range(2):
                at = start + 8 * half_slot(0, color, a)
                low = jnp.concatenate(below[color][a], 0)
                high = jnp.concatenate(above[color][a], 0)
                ref[at : at + 16] = jnp.where(side == 0, low, high).astype(BF16)

    def half_down(layer):
        return sent_down(field_at(base_ref, layer))

    def half_up(layer):
        return sent_up(field_at(base_ref, layer), link_at(link_ref, layer))

    put(far_ref, 0, half_down(0), half_up(3))
    put(near_ref, 4 * ROWS, half_down(1), half_up(2))
    second = 1 + side

    def keep(at, value):
        next_ref[at] = value

    sweep_layer(base_ref, base_ref, link_ref, second, half_down(second + 1), half_up(second - 1), keep)

    def field(part, color, spin):
        return next_ref[comp(part, color, spin)]

    put(near_ref, 4 * ROWS + 96, sent_down(field), sent_up(field, link_at(link_ref, second)))


def sweep_layer(from_ref, src_ref, link_ref, layer, ahead, behind, put):
    total = hop(field_at(from_ref, layer), link_at(link_ref, layer), ahead, behind)
    for key, value in total.items():
        put(comp(*key), src_ref[layer, comp(*key)] + HOPPING * value)


def prepare_layer(from_ref, link_ref, layer, ahead_ref, ahead_at, behind_ref, behind_at):
    put_half(ahead_ref.at[ahead_at], sent_down(field_at(from_ref, layer)))
    put_half(
        behind_ref.at[behind_at], sent_up(field_at(from_ref, layer), link_at(link_ref, layer))
    )


def inner_kernel(
    matrix_ref, vector_ref, base_ref, link_ref,
    kept_matrix, kept_vector, inner_ref, ahead_ref, behind_ref,
):
    kept_matrix[...] = matrix_ref[...]
    kept_vector[...] = vector_ref[...]

    def prepare(layer, carry):
        prepare_layer(base_ref, link_ref, layer, ahead_ref, layer, behind_ref, layer)
        return carry

    def step(layer, carry):
        def put(at, value):
            inner_ref[layer - 1, at] = value

        ahead, behind = get_half(ahead_ref, layer + 1), get_half(behind_ref, layer - 1)
        sweep_layer(base_ref, base_ref, link_ref, layer, ahead, behind, put)
        return carry

    lax.fori_loop(0, 4, prepare, 0)
    lax.fori_loop(1, 3, step, 0)


def sweep_kernel(
    near_ref, far_ref, base_ref, link_ref, inner_ref, ahead_ref, behind_ref, out_ref,
    wide, src, one, two, links, ahead, behind, done,
):
    side = lax.axis_index("z_lo")
    block, halo = 2 - 2 * side, 1 + 3 * side
    wide[...] = near_ref[: 4 * ROWS].astype(F32)
    src[pl.ds(block, 4)] = base_ref[...]
    links[pl.ds(block, 4)] = link_ref[...]
    one[pl.ds(block + 1, 2)] = inner_ref[...]
    ahead[pl.ds(block, 4)] = ahead_ref[...]
    behind[pl.ds(block + 1, 4)] = behind_ref[...]
    near = near_ref[4 * ROWS : 4 * ROWS + 96].astype(F32).reshape(12, 8, SITES)
    far = far_ref[...].astype(F32).reshape(12, 8, SITES)
    ahead[6 - side] = jnp.where(side == 0, far, near)
    behind[1 - side] = jnp.where(side == 0, near, far)
    assemble(wide, 0, src, links, halo)
    prepare_layer(src, links, halo, ahead, halo, behind, halo + 1)

    def first(at, carry):
        layer = at + 1 - side + jnp.where(at >= 2 - side, 2, 0)

        def put(slot_at, value):
            one[layer, slot_at] = value

        halves = get_half(ahead, layer + 1), get_half(behind, layer)
        sweep_layer(src, src, links, layer, *halves, put)
        return carry

    lax.fori_loop(0, 3, first, 0)

    def prepare(from_ref, layer):
        put_half(ahead.at[layer + 2], sent_down(field_at(from_ref, layer + 2)))
        put_half(behind.at[layer + 1], sent_up(field_at(from_ref, layer), link_at(links, layer)))

    def prepare_one(layer, carry):
        prepare(one, layer)
        return carry

    def second(layer, carry):
        def put(at, value):
            two[layer, at] = value

        sweep_layer(one, src, links, layer, get_half(ahead, layer + 1), get_half(behind, layer), put)
        return carry

    lax.fori_loop(0, 4, prepare_one, 0)
    near = near_ref[4 * ROWS + 96 :].astype(F32).reshape(12, 8, SITES)

    @pl.when(side == 0)
    def _():
        behind[1] = near

    @pl.when(side == 1)
    def _():
        ahead[5] = near

    lax.fori_loop(1, 5, second, 0)

    def prepare_two(layer, carry):
        prepare(two, layer)
        return carry

    def third(layer, carry):
        def put(at, value):
            done[pl.ds(pl.multiple_of(((layer - 2) * 24 + at) * 8, 8), 8)] = value

        sweep_layer(two, src, links, layer, get_half(ahead, layer + 1), get_half(behind, layer), put)
        return carry

    lax.fori_loop(1, 3, prepare_two, 0)
    lax.fori_loop(2, 4, third, 0)
    for layer in range(2):
        for time in range(4):
            for color in range(3):
                start = (layer * 24 + color * 8) * 8 + 2 * time
                pair = [done[pl.ds(start + which, 8, stride=8)] for which in range(2)]
                out_ref[time * 2 + layer, color * 16 : color * 16 + 16] = jnp.concatenate(
                    pair, 0
                ).astype(BF16)


def project_kernel(phi_ref, vector_ref, out_ref):
    totals = [None, None]
    for color in range(3):
        rows = phi_ref[:, color * 16 : color * 16 + 16].reshape(8 * 16, SITES)
        for part in range(2):
            value = lax.dot_general(
                rows,
                vector_ref[color, part],
                (((1,), (1,)), ((), ())),
                preferred_element_type=F32,
            )
            totals[part] = value if totals[part] is None else totals[part] + value
    crossed = pltpu.roll(totals[1].reshape(16, 8, 128), 4, 1)
    upper = lax.broadcasted_iota(jnp.int32, crossed.shape, 1) < 4
    mixed = totals[0].reshape(16, 8, 128) + jnp.where(upper, crossed, -crossed)
    for source in range(12):
        for part in range(2):
            member, at = divmod(2 * source + part, 3)
            out_ref[member, at] = mixed[source, 4 * part : 4 * part + 4].astype(BF16)


def spread_kernel(value_ref, out_ref):
    total = value_ref[0].astype(F32)
    for member in range(1, value_ref.shape[0]):
        total = total + value_ref[member].astype(F32)
    total = total.astype(BF16)
    for member in range(out_ref.shape[0]):
        out_ref[member] = total


def summed(value, copies):
    shape = jax.ShapeDtypeStruct((copies, *value.shape[1:]), BF16)
    return local_call(spread_kernel, shape, [], 1 << 16)(value)


def all_reduce(partial_value):
    plane = lax.axis_size(PLANE)
    depth = lax.axis_size(DEPTH)
    copies = summed(exchange(partial_value, PLANE), depth)
    copies = summed(exchange(copies, DEPTH), plane)
    return exchange(copies, PLANE)


def spinors(sources, gauge_links, kept):
    moved = sources[0, :, :, :, :, 0].transpose(0, 2, 3, 1, 4)
    entries = gauge_links[:, 0, :, :, :, 0].transpose(0, 2, 3, 1, 4).reshape(36, 2, SITES)
    clear = local_call(clear_kernel, jax.ShapeDtypeStruct((8, SITES), F32), [], 1 << 32)()
    packed = local_call(
        pack_kernel,
        jax.ShapeDtypeStruct((16, ROWS, SITES), BF16),
        [
            pltpu.VMEM((8, ROWS, SITES), F32),
            pltpu.VMEM((LINK, SITES), F32),
        ],
        1 << 17,
    )(clear, moved, entries)
    own = exchange(packed, GROUP)
    vectors = (8, SITES)
    base, links, near, far = local_call(
        own_kernel,
        (
            jax.ShapeDtypeStruct((4, 24, *vectors), F32),
            jax.ShapeDtypeStruct((4, LINK, *vectors), F32),
            jax.ShapeDtypeStruct((4 * ROWS + 192, SITES), BF16),
            jax.ShapeDtypeStruct((96, SITES), BF16),
        ),
        [pltpu.VMEM((16 * ROWS, SITES), F32), pltpu.VMEM((24, *vectors), F32)],
        1 << 20,
    )(own)
    matrix, spectrum = kept
    matrix, spectrum, inner, ahead, behind = local_call(
        inner_kernel,
        (
            jax.ShapeDtypeStruct(matrix.shape, F32),
            jax.ShapeDtypeStruct(spectrum.shape, BF16),
            jax.ShapeDtypeStruct((2, 24, *vectors), F32),
            jax.ShapeDtypeStruct((4, 12, *vectors), F32),
            jax.ShapeDtypeStruct((4, 12, *vectors), F32),
        ),
        [],
        1 << 22,
    )(matrix, spectrum, base, links)
    near = send(near, POSITION, (1, 1))
    far = send(far, POSITION, (2, 2))
    done = local_call(
        sweep_kernel,
        jax.ShapeDtypeStruct((8, FIELD, SITES), BF16),
        [
            pltpu.VMEM((4 * ROWS, SITES), F32),
            pltpu.VMEM((6, 24, *vectors), F32),
            pltpu.VMEM((6, 24, *vectors), F32),
            pltpu.VMEM((6, 24, *vectors), F32),
            pltpu.VMEM((6, LINK, *vectors), F32),
            pltpu.VMEM((7, 12, *vectors), F32),
            pltpu.VMEM((7, 12, *vectors), F32),
            pltpu.VMEM((2 * 24 * 8, SITES), F32),
        ],
        1 << 24,
    )(near, far, base, links, inner, ahead, behind)
    return exchange(done, BLOCK), matrix, spectrum


def finish_kernel(total_ref, matrix_ref, projected_ref, contracted_ref, rows):
    for piece in range(24):
        rows[4 * piece : 4 * piece + 4] = total_ref[piece // 3, piece % 3].astype(F32)
    lane = lax.broadcasted_iota(jnp.int32, (8, 128), 1)
    row_re = jnp.broadcast_to(matrix_ref[0:1], (8, 128))
    row_im = jnp.broadcast_to(matrix_ref[1:2], (8, 128))
    pick = lane == lax.axis_index(SPACE)
    own, by_re, by_im = (jnp.zeros((8, 128), F32) for _ in range(3))
    for source in range(12):
        value = rows[8 * source : 8 * source + 8]
        here = lane == source
        own = jnp.where(here, jnp.sum(jnp.where(pick, value, 0.0), 1, keepdims=True), own)
        by_re = jnp.where(here, jnp.sum(value * row_re, 1, keepdims=True), by_re)
        by_im = jnp.where(here, jnp.sum(value * row_im, 1, keepdims=True), by_im)
    crossed = pltpu.roll(by_im, 4, 0)
    upper = lax.broadcasted_iota(jnp.int32, (8, 128), 0) < 4
    contracted = by_re + jnp.where(upper, -crossed, crossed)
    for row in range(8):
        projected_ref[row] = own[row : row + 1, :12]
        contracted_ref[row] = contracted[row : row + 1, :12]


def placed_out(values):
    return values.reshape(1, 2, 4, 1, 12).transpose(0, 1, 2, 4, 3)


def local(sources, gauge_links, eigenvectors, elementals):
    vectors = eigenvectors[0, :, :, :, 0].transpose(2, 1, 0, 3)
    kept = (elementals[0, :, 0], vectors)
    finals, matrix, vectors = spinors(sources, gauge_links, kept)
    partial_value = local_call(
        project_kernel, jax.ShapeDtypeStruct((8, 3, 4, 128), BF16), [], 1 << 25
    )(finals, vectors)
    totals = all_reduce(partial_value)
    shape = jax.ShapeDtypeStruct((8, 1, 12), F32)
    projected, contracted = local_call(
        finish_kernel,
        (shape, shape),
        [pltpu.VMEM((96, 128), F32)],
        1 << 17,
    )(totals, matrix)
    return placed_out(projected), placed_out(contracted)


def solution(mesh):
    fine = Mesh(mesh.devices.reshape(2, 2, 4, 8, 2, 2), (*TM, *SPACE))
    placed = (
        P(TM, None, None, None, None, SPACE, None),
        P(None, TM, None, None, None, SPACE, None),
        P(TM, None, None, None, SPACE, None),
        P(TM, None, SPACE, None),
    )
    result = P(TM, None, None, None, SPACE)
    return jax.shard_map(
        local, mesh=fine, in_specs=placed, out_specs=(result, result), check_vma=False
    )
```

```python
import jax
import jax.numpy as jnp
from jax import lax
from jax.experimental import pallas as pl
from jax.experimental.pallas import tpu as pltpu
from jax.sharding import Mesh
from jax.sharding import PartitionSpec as P

HOPPING = 0.125
TM = ("y_hi", "core")
SPACE = ("x", "z_hi", "z_lo", "y_lo")
PLANE = ("y_lo", "x")
DEPTH = ("z_hi", "z_lo")
POSITION = ("x", *DEPTH)
BLOCK = ("y_hi", "core", "y_lo")
GROUP = ("y_hi", "y_lo", "core", "z_lo")
LX = 8
FIELD = 48
LINK = 72
ROWS = FIELD + LINK
SITES = 128
F32 = jnp.float32
BF16 = jnp.bfloat16


def exchange(value, axes):
    return lax.all_to_all(value, axes, 0, 0, tiled=True)


def send(value, axes, steps):
    count = lax.axis_size(axes)
    pairs = [(i, (i + steps[1] if i % 2 else i - steps[0]) % count) for i in range(count)]
    return lax.ppermute(value, axes, pairs)


def local_call(kernel, outs, scratch, flops, **options):
    return pl.pallas_call(
        kernel,
        **options,
        out_shape=outs,
        scratch_shapes=scratch,
        compiler_params=pltpu.CompilerParams(vmem_limit_bytes=16 << 20),
        cost_estimate=pl.CostEstimate(flops=flops, bytes_accessed=1 << 20, transcendentals=0),
    )


def member(high, low, core, position):
    return high * 8 + low * 4 + core * 2 + position


def clear_kernel(out_ref):
    out_ref[...] = jnp.zeros(out_ref.shape, F32)


def pack_kernel(clear_ref, source_ref, link_ref, out_ref, rows, links):
    for entry in range(36):
        links[2 * entry : 2 * entry + 2] = link_ref[entry].astype(F32)
    shared = links[...]
    for target in range(8):
        rows[target, FIELD:] = shared
    for target in range(8):
        for part in range(2):
            for color in range(3):
                for which in range(2):
                    at = part * 24 + color * 8 + which * 4
                    if target < 6:
                        piece = source_ref[part, color, 2 * target + which].astype(F32)
                    else:
                        piece = clear_ref[:4]
                    rows[target, at : at + 4] = piece
    for target in range(8):
        packed = rows[target].astype(BF16)
        high, core, low = target // 4, target // 2 % 2, target % 2
        for position in range(2):
            out_ref[member(high, low, core, position)] = packed


def signed_add(base, sign, value):
    if base is None:
        return value if sign > 0 else -value
    return base + value if sign > 0 else base - value


def block_terms(direction, first, second):
    if direction == 0:
        return (((1, second[1]), (-1, second[0])), ((1, first[1]), (-1, first[0])))
    if direction == 1:
        return (((-1, second[0]), (-1, second[1])), ((1, first[0]), (1, first[1])))
    if direction == 2:
        return (((1, first[1]), (-1, first[0])), ((-1, second[1]), (1, second[0])))
    return (((1, first[0]), (1, first[1])), ((1, second[0]), (1, second[1])))


def half_of(field, direction, sign):
    half = []
    for color in range(3):
        up = [(field(0, color, a), field(1, color, a)) for a in range(4)]
        terms = block_terms(direction, up[2], up[3])
        half.append(
            [
                tuple(
                    signed_add(up[a][part], sign * terms[a][part][0], terms[a][part][1])
                    for part in range(2)
                )
                for a in range(2)
            ]
        )
    return half


def color_apply(link, direction, half, dagger):
    out = []
    for row in range(3):
        acc = [[None, None], [None, None]]
        for col in range(3):
            i, j = (col, row) if dagger else (row, col)
            re, im = link(direction, i, j, 0), link(direction, i, j, 1)
            flip = -1 if dagger else 1
            for a in range(2):
                vec_re, vec_im = half[col][a]
                acc[a][0] = signed_add(acc[a][0], 1, re * vec_re)
                acc[a][0] = signed_add(acc[a][0], -flip, im * vec_im)
                acc[a][1] = signed_add(acc[a][1], 1, re * vec_im)
                acc[a][1] = signed_add(acc[a][1], flip, im * vec_re)
        out.append([tuple(acc[a]) for a in range(2)])
    return out


def shift(value, direction, ahead):
    if direction == 3:
        return pltpu.roll(value, 6 if ahead else 2, 0)
    if direction == 1:
        return pltpu.roll(value, SITES - LX if ahead else LX, 1)
    column = lax.broadcasted_iota(jnp.int32, value.shape, 1) % LX
    if ahead:
        return jnp.where(
            column == LX - 1, pltpu.roll(value, LX - 1, 1), pltpu.roll(value, SITES - 1, 1)
        )
    return jnp.where(column == 0, pltpu.roll(value, SITES - (LX - 1), 1), pltpu.roll(value, 1, 1))


def map_half(function, half):
    return [[tuple(function(v) for v in pair) for pair in spins] for spins in half]


def accumulate(total, direction, ahead, behind):
    for color in range(3):
        both = []
        for a in range(2):
            for part in range(2):
                key = (part, color, a)
                value = ahead[color][a][part] + behind[color][a][part]
                total[key] = value if key not in total else total[key] + value
            both.append(tuple(ahead[color][a][part] - behind[color][a][part] for part in range(2)))
        terms = block_terms(direction, both[0], both[1])
        outer = -1 if direction == 3 else 1
        for a in range(2):
            for part in range(2):
                key = (part, color, a + 2)
                sign, value = terms[a][part]
                total[key] = signed_add(total.get(key), outer * sign, value)


def hop(field, link, ahead_z, behind_z):
    total = {}
    for direction in (0, 1, 3):
        ahead = map_half(
            lambda v, d=direction: shift(v, d, True), half_of(field, direction, -1)
        )
        behind = color_apply(link, direction, half_of(field, direction, 1), True)
        behind = map_half(lambda v, d=direction: shift(v, d, False), behind)
        accumulate(total, direction, color_apply(link, direction, ahead, False), behind)
    accumulate(total, 2, color_apply(link, 2, ahead_z, False), behind_z)
    return total


def comp(part, color, spin):
    return color * 8 + part * 4 + spin


def slot(direction, row, col, part):
    return direction * 18 + row * 6 + col * 2 + part


def field_at(ref, layer):
    return lambda part, color, spin: ref[layer, comp(part, color, spin)]


def link_at(ref, layer):
    return lambda direction, row, col, part: ref[layer, slot(direction, row, col, part)]


def half_slot(part, color, spin):
    return color * 4 + spin * 2 + part


def put_half(ref, half):
    for color in range(3):
        for a in range(2):
            for part in range(2):
                ref[half_slot(part, color, a)] = half[color][a][part].astype(ref.dtype)


def get_half(ref, layer):
    return [
        [tuple(ref[layer, half_slot(part, color, a)] for part in range(2)) for a in range(2)]
        for color in range(3)
    ]


def assemble(wide, start, src, links, layer):
    slices = lax.broadcasted_iota(jnp.int32, (4, SITES), 0)
    turn = jnp.where(slices == 3, -1.0, 1.0)
    for color in range(3):
        for part in range(2):
            for spin in range(4):
                for which in range(2):
                    row = start + part * 24 + color * 8 + which * 4 + spin
                    src[layer, comp(part, color, spin), pl.ds(which, 4, stride=2)] = wide[
                        pl.ds(row, 4, stride=ROWS)
                    ]
    for entry in range(LINK):
        value = wide[pl.ds(start + FIELD + entry, 4, stride=ROWS)]
        if entry >= 54:
            value = value * turn
        for which in range(2):
            links[layer, entry, pl.ds(which, 4, stride=2)] = value


def sent_down(field):
    return half_of(field, 2, -1)


def sent_up(field, link):
    return color_apply(link, 2, half_of(field, 2, 1), True)


def own_kernel(own_ref, base_ref, link_ref, near_ref, far_ref, wide, next_ref):
    for layer in range(4):
        for time in range(4):
            start = (layer * 4 + time) * ROWS
            wide[start : start + ROWS] = own_ref[
                member(time // 2, layer % 2, time % 2, layer // 2)
            ].astype(F32)
    side = lax.axis_index("z_lo")

    def one(layer, carry):
        assemble(wide, layer * 4 * ROWS, base_ref, link_ref, layer)
        return carry

    lax.fori_loop(0, 4, one, 0)
    edge = pl.ds(pl.multiple_of(side * 12 * ROWS, 8), 4 * ROWS)
    near_ref[: 4 * ROWS] = wide[edge].astype(BF16)

    def put(ref, start, below, above):
        for color in range(3):
            for a in range(2):
                at = start + 8 * half_slot(0, color, a)
                low = jnp.concatenate(below[color][a], 0)
                high = jnp.concatenate(above[color][a], 0)
                ref[at : at + 16] = jnp.where(side == 0, low, high).astype(BF16)

    def half_down(layer):
        return sent_down(field_at(base_ref, layer))

    def half_up(layer):
        return sent_up(field_at(base_ref, layer), link_at(link_ref, layer))

    put(far_ref, 0, half_down(0), half_up(3))
    put(near_ref, 4 * ROWS, half_down(1), half_up(2))
    second = 1 + side

    def keep(at, value):
        next_ref[at] = value

    sweep_layer(base_ref, base_ref, link_ref, second, half_down(second + 1), half_up(second - 1), keep)

    def field(part, color, spin):
        return next_ref[comp(part, color, spin)]

    put(near_ref, 4 * ROWS + 96, sent_down(field), sent_up(field, link_at(link_ref, second)))


def sweep_layer(from_ref, src_ref, link_ref, layer, ahead, behind, put):
    total = hop(field_at(from_ref, layer), link_at(link_ref, layer), ahead, behind)
    for key, value in total.items():
        put(comp(*key), src_ref[layer, comp(*key)] + HOPPING * value)


def prepare_layer(from_ref, link_ref, layer, ahead_ref, ahead_at, behind_ref, behind_at):
    put_half(ahead_ref.at[ahead_at], sent_down(field_at(from_ref, layer)))
    put_half(
        behind_ref.at[behind_at], sent_up(field_at(from_ref, layer), link_at(link_ref, layer))
    )


def inner_kernel(
    matrix_ref, vector_ref, base_ref, link_ref,
    kept_matrix, kept_vector, inner_ref, ahead_ref, behind_ref,
):
    kept_matrix[...] = matrix_ref[...]
    kept_vector[...] = vector_ref[...]

    def prepare(layer, carry):
        prepare_layer(base_ref, link_ref, layer, ahead_ref, layer, behind_ref, layer)
        return carry

    def step(layer, carry):
        def put(at, value):
            inner_ref[layer - 1, at] = value

        ahead, behind = get_half(ahead_ref, layer + 1), get_half(behind_ref, layer - 1)
        sweep_layer(base_ref, base_ref, link_ref, layer, ahead, behind, put)
        return carry

    lax.fori_loop(0, 4, prepare, 0)
    lax.fori_loop(1, 3, step, 0)


def sweep_kernel(
    near_ref, far_ref, base_ref, link_ref, inner_ref, ahead_ref, behind_ref, out_ref,
    wide, src, one, two, links, ahead, behind, done,
):
    side = lax.axis_index("z_lo")
    block, halo = 2 - 2 * side, 1 + 3 * side
    wide[...] = near_ref[: 4 * ROWS].astype(F32)
    src[pl.ds(block, 4)] = base_ref[...]
    links[pl.ds(block, 4)] = link_ref[...]
    one[pl.ds(block + 1, 2)] = inner_ref[...]
    ahead[pl.ds(block, 4)] = ahead_ref[...]
    behind[pl.ds(block + 1, 4)] = behind_ref[...]
    near = near_ref[4 * ROWS : 4 * ROWS + 96].astype(F32).reshape(12, 8, SITES)
    far = far_ref[...].astype(F32).reshape(12, 8, SITES)
    ahead[6 - side] = jnp.where(side == 0, far, near)
    behind[1 - side] = jnp.where(side == 0, near, far)
    assemble(wide, 0, src, links, halo)
    prepare_layer(src, links, halo, ahead, halo, behind, halo + 1)

    def first(at, carry):
        layer = at + 1 - side + jnp.where(at >= 2 - side, 2, 0)

        def put(slot_at, value):
            one[layer, slot_at] = value

        halves = get_half(ahead, layer + 1), get_half(behind, layer)
        sweep_layer(src, src, links, layer, *halves, put)
        return carry

    lax.fori_loop(0, 3, first, 0)

    def prepare(from_ref, layer):
        put_half(ahead.at[layer + 2], sent_down(field_at(from_ref, layer + 2)))
        put_half(behind.at[layer + 1], sent_up(field_at(from_ref, layer), link_at(links, layer)))

    def prepare_one(layer, carry):
        prepare(one, layer)
        return carry

    def second(layer, carry):
        def put(at, value):
            two[layer, at] = value

        sweep_layer(one, src, links, layer, get_half(ahead, layer + 1), get_half(behind, layer), put)
        return carry

    lax.fori_loop(0, 4, prepare_one, 0)
    near = near_ref[4 * ROWS + 96 :].astype(F32).reshape(12, 8, SITES)

    @pl.when(side == 0)
    def _():
        behind[1] = near

    @pl.when(side == 1)
    def _():
        ahead[5] = near

    lax.fori_loop(1, 5, second, 0)

    def prepare_two(layer, carry):
        prepare(two, layer)
        return carry

    def third(layer, carry):
        def put(at, value):
            done[pl.ds(pl.multiple_of(((layer - 2) * 24 + at) * 8, 8), 8)] = value

        sweep_layer(two, src, links, layer, get_half(ahead, layer + 1), get_half(behind, layer), put)
        return carry

    lax.fori_loop(1, 3, prepare_two, 0)
    lax.fori_loop(2, 4, third, 0)
    for layer in range(2):
        for time in range(4):
            for color in range(3):
                start = (layer * 24 + color * 8) * 8 + 2 * time
                pair = [done[pl.ds(start + which, 8, stride=8)] for which in range(2)]
                out_ref[time * 2 + layer, color * 16 : color * 16 + 16] = jnp.concatenate(
                    pair, 0
                ).astype(BF16)


def project_kernel(phi_ref, vector_ref, out_ref):
    totals = [None, None]
    for color in range(3):
        rows = phi_ref[:, color * 16 : color * 16 + 16].reshape(8 * 16, SITES)
        for part in range(2):
            value = lax.dot_general(
                rows,
                vector_ref[color, part],
                (((1,), (1,)), ((), ())),
                preferred_element_type=F32,
            )
            totals[part] = value if totals[part] is None else totals[part] + value
    crossed = pltpu.roll(totals[1].reshape(16, 8, 128), 4, 1)
    upper = lax.broadcasted_iota(jnp.int32, crossed.shape, 1) < 4
    mixed = totals[0].reshape(16, 8, 128) + jnp.where(upper, crossed, -crossed)
    for source in range(12):
        for part in range(2):
            member, at = divmod(2 * source + part, 3)
            out_ref[member, at] = mixed[source, 4 * part : 4 * part + 4].astype(BF16)


def spread_kernel(value_ref, out_ref):
    total = value_ref[0].astype(F32)
    for member in range(1, value_ref.shape[0]):
        total = total + value_ref[member].astype(F32)
    total = total.astype(BF16)
    for member in range(out_ref.shape[0]):
        out_ref[member] = total


def summed(value, copies):
    shape = jax.ShapeDtypeStruct((copies, *value.shape[1:]), BF16)
    return local_call(spread_kernel, shape, [], 1 << 16)(value)


def all_reduce(partial_value):
    plane = lax.axis_size(PLANE)
    depth = lax.axis_size(DEPTH)
    copies = summed(exchange(partial_value, PLANE), depth)
    copies = summed(exchange(copies, DEPTH), plane)
    return exchange(copies, PLANE)


def spinors(sources, gauge_links, kept):
    moved = sources[0, :, :, :, :, 0].transpose(0, 2, 3, 1, 4)
    entries = gauge_links[:, 0, :, :, :, 0].transpose(0, 2, 3, 1, 4).reshape(36, 2, SITES)
    clear = local_call(clear_kernel, jax.ShapeDtypeStruct((8, SITES), F32), [], 1 << 32)()
    packed = local_call(
        pack_kernel,
        jax.ShapeDtypeStruct((16, ROWS, SITES), BF16),
        [
            pltpu.VMEM((8, ROWS, SITES), F32),
            pltpu.VMEM((LINK, SITES), F32),
        ],
        1 << 17,
    )(clear, moved, entries)
    own = exchange(packed, GROUP)
    vectors = (8, SITES)
    base, links, near, far = local_call(
        own_kernel,
        (
            jax.ShapeDtypeStruct((4, 24, *vectors), F32),
            jax.ShapeDtypeStruct((4, LINK, *vectors), F32),
            jax.ShapeDtypeStruct((4 * ROWS + 192, SITES), BF16),
            jax.ShapeDtypeStruct((96, SITES), BF16),
        ),
        [pltpu.VMEM((16 * ROWS, SITES), F32), pltpu.VMEM((24, *vectors), F32)],
        1 << 20,
    )(own)
    matrix, spectrum = kept
    matrix, spectrum, inner, ahead, behind = local_call(
        inner_kernel,
        (
            jax.ShapeDtypeStruct(matrix.shape, F32),
            jax.ShapeDtypeStruct(spectrum.shape, BF16),
            jax.ShapeDtypeStruct((2, 24, *vectors), F32),
            jax.ShapeDtypeStruct((4, 12, *vectors), F32),
            jax.ShapeDtypeStruct((4, 12, *vectors), F32),
        ),
        [],
        1 << 22,
    )(matrix, spectrum, base, links)
    near = send(near, POSITION, (1, 1))
    far = send(far, POSITION, (2, 2))
    done = local_call(
        sweep_kernel,
        jax.ShapeDtypeStruct((8, FIELD, SITES), BF16),
        [
            pltpu.VMEM((4 * ROWS, SITES), F32),
            pltpu.VMEM((6, 24, *vectors), F32),
            pltpu.VMEM((6, 24, *vectors), F32),
            pltpu.VMEM((6, 24, *vectors), F32),
            pltpu.VMEM((6, LINK, *vectors), F32),
            pltpu.VMEM((7, 12, *vectors), F32),
            pltpu.VMEM((7, 12, *vectors), F32),
            pltpu.VMEM((2 * 24 * 8, SITES), F32),
        ],
        1 << 24,
    )(near, far, base, links, inner, ahead, behind)
    return exchange(done, BLOCK), matrix, spectrum


def finish_kernel(total_ref, matrix_ref, projected_ref, contracted_ref, rows):
    for piece in range(24):
        rows[4 * piece : 4 * piece + 4] = total_ref[piece // 3, piece % 3].astype(F32)
    lane = lax.broadcasted_iota(jnp.int32, (8, 128), 1)
    row_re = jnp.broadcast_to(matrix_ref[0:1], (8, 128))
    row_im = jnp.broadcast_to(matrix_ref[1:2], (8, 128))
    pick = lane == lax.axis_index(SPACE)
    own, by_re, by_im = (jnp.zeros((8, 128), F32) for _ in range(3))
    for source in range(12):
        value = rows[8 * source : 8 * source + 8]
        here = lane == source
        own = jnp.where(here, jnp.sum(jnp.where(pick, value, 0.0), 1, keepdims=True), own)
        by_re = jnp.where(here, jnp.sum(value * row_re, 1, keepdims=True), by_re)
        by_im = jnp.where(here, jnp.sum(value * row_im, 1, keepdims=True), by_im)
    crossed = pltpu.roll(by_im, 4, 0)
    upper = lax.broadcasted_iota(jnp.int32, (8, 128), 0) < 4
    contracted = by_re + jnp.where(upper, -crossed, crossed)
    for row in range(8):
        projected_ref[row] = own[row : row + 1, :12]
        contracted_ref[row] = contracted[row : row + 1, :12]


def placed_out(values):
    return values.reshape(1, 2, 4, 1, 12).transpose(0, 1, 2, 4, 3)


def local(sources, gauge_links, eigenvectors, elementals):
    vectors = eigenvectors[0, :, :, :, 0].transpose(2, 1, 0, 3)
    kept = (elementals[0, :, 0], vectors)
    finals, matrix, vectors = spinors(sources, gauge_links, kept)
    partial_value = local_call(
        project_kernel, jax.ShapeDtypeStruct((8, 3, 4, 128), BF16), [], 1 << 25
    )(finals, vectors)
    totals = all_reduce(partial_value)
    shape = jax.ShapeDtypeStruct((8, 1, 12), F32)
    projected, contracted = local_call(
        finish_kernel,
        (shape, shape),
        [pltpu.VMEM((96, 128), F32)],
        1 << 17,
    )(totals, matrix)
    return placed_out(projected), placed_out(contracted)


def solution(mesh):
    fine = Mesh(mesh.devices.reshape(2, 2, 4, 8, 2, 2), (*TM, *SPACE))
    placed = (
        P(TM, None, None, None, None, SPACE, None),
        P(None, TM, None, None, None, SPACE, None),
        P(TM, None, None, None, SPACE, None),
        P(TM, None, SPACE, None),
    )
    result = P(TM, None, None, None, SPACE)
    return jax.shard_map(
        local, mesh=fine, in_specs=placed, out_specs=(result, result), check_vma=False
    )
```
